32 devices in a mesh: ens: 8 (over z, y), space: 4 (over x, core).
Axes of the slice: x: 2, y: 2, z: 4, core: 2. Of those that a mesh axis runs over, the one named last changes fastest.
Arguments:
- grid_hidden: bfloat16 [8, 512, 1024], P('ens', 'space'), may hold values from -600 to 600
- latent: bfloat16 [8, 512, 1024], P('ens', 'space'), may hold values from -6 to 6
- tile_neighbor_index: int32 [4, 128], P('space'), may hold values from 0 to 511, as said below
- target: float32 [100, 512], P(None, 'space'), may hold values from -6 to 6
- w_query: bfloat16 [1024, 1024], replicated, may hold values from -0.1875 to 0.1875
- w_key: bfloat16 [1024, 1024], replicated, may hold values from -0.1875 to 0.1875
- w_value: bfloat16 [1024, 1024], replicated, may hold values from -0.1875 to 0.1875
- w_mix: bfloat16 [1024, 1024], replicated, may hold values from -0.1875 to 0.1875
- readout_weight: bfloat16 [100, 1024], replicated, may hold values from -0.1875 to 0.1875
Outputs:
- fair_ranked_score_loss: float32 [], replicated
- grad_out: float32 [100, 1024], replicated
- grad_query: float32 [1024, 1024], P('ens', 'space')
- grad_key: float32 [1024, 1024], P('ens', 'space')
- grad_value: float32 [1024, 1024], P('ens', 'space')
- grad_mix: float32 [1024, 1024], P('ens', 'space')
The draws below stay inside these ranges and needn't reach their ends.
Inputs may be any that keep to these rules, and one draw needn't show every extreme that they name: `tile_neighbor_index`: row t holds 128 distinct latent node indices, all among the nodes of space shard s = t and of the two shards beside it, counted cyclically; shard s holds nodes s * 128 to (s + 1) * 128 - 1.
All inputs are finite; a program needn't handle non-finite values.
Results may differ from the reference program's by a relative error of at most 0.025.
Values may be sent and summed in bfloat16 or wider, within the bound.
No kernel may reach another device: no remote copies, remote signals or barrier semaphores. Data moves between devices by JAX's collectives and lax.ppermute only.
A program may use at most 128 MiB of HBM per device.

```python
import jax
import jax.numpy as jnp
from jax import lax

H = 1024
HEADS = 16
C = 100
G_DEV = 128
LAT_DEV = 128
MEMBERS = 8
GRID = 512
NLAT = 512
N_SPACE = 4


def draw_tile_neighbor_index(key, part):
    tile_count = GRID // 128
    tiles_each = G_DEV // 128
    candidates = 3 * LAT_DEV
    tile_keys = jax.random.split(key, tile_count)

    def one_tile(tile_key):
        ranking = jax.random.randint(tile_key, (candidates,), 0, 1 << 20) * (4 * LAT_DEV) + jnp.arange(candidates)
        return jnp.argsort(ranking)[:128]
    chosen = jax.vmap(one_tile)(tile_keys).astype(jnp.int32)
    owners = (jnp.arange(tile_count) // tiles_each).astype(jnp.int32)
    return jnp.mod((owners[:, None] - 1) * LAT_DEV + chosen, LAT_DEV * N_SPACE).astype(jnp.int32)


def draw_grid_hidden(key, part):
    base_key = jax.random.fold_in(key, 11)
    values_out = jnp.clip(jax.random.normal(base_key, (MEMBERS, GRID, H), jnp.float32), -6.0, 6.0)
    return values_out.astype(jnp.bfloat16)


def block_levels(key, shape, cuts, smallest, high):
    gain = 1.0
    for position, blocks in cuts:
        heights = jax.random.uniform(jax.random.fold_in(jax.random.fold_in(key, 6), position), (blocks,), jnp.float32, smallest / len(cuts), high / len(cuts))
        gain = gain * jnp.repeat(jnp.exp(heights), shape[position] // blocks).reshape((-1,) + (1,) * (len(shape) - 1 - position))
    return gain


def centred(rng, dims, scale, most, pieces=(), dtype=jnp.bfloat16):
    values = scale * jax.random.normal(rng, dims, jnp.float32)
    if pieces:
        values = values * block_levels(rng, dims, pieces, -0.22, 0.18)
    return jnp.clip(values, -most, most).astype(dtype)


def setup_inputs(seed: int = 0) -> dict:
    key_of = jax.random.split(jax.random.key(seed), 10)
    grid_hidden = draw_grid_hidden(jax.random.fold_in(key_of[9], 71), 0)
    latent = centred(key_of[1], (MEMBERS, NLAT, H), 1.0, 6.0, ((0, 8), (1, 4)))
    tile_neighbor_index = draw_tile_neighbor_index(jax.random.fold_in(key_of[9], 71), 0)
    target = centred(key_of[3], (C, GRID), 1.0, 6.0, ((1, 4),), jnp.float32)
    w_query = centred(key_of[4], (H, H), H ** -0.5, 0.1875)
    w_key = centred(key_of[5], (H, H), H ** -0.5, 0.1875)
    w_value = centred(key_of[6], (H, H), H ** -0.5, 0.1875)
    w_mix = centred(key_of[7], (H, H), H ** -0.5, 0.1875)
    readout_weight = centred(key_of[8], (C, H), H ** -0.5, 0.1875)
    return {"grid_hidden": grid_hidden, "latent": latent, "tile_neighbor_index": tile_neighbor_index, "target": target, "w_query": w_query, "w_key": w_key, "w_value": w_value, "w_mix": w_mix, "readout_weight": readout_weight}


EPS = 1e-06
SMOOTH = 0.01

def widened(values_in):
    return lax.optimization_barrier(values_in).astype(jnp.float32)

def by_heads(values_in):
    return widened(values_in).reshape(values_in.shape[0], values_in.shape[1], HEADS, values_in.shape[2] // HEADS)

def rows_times(blocks, matrix):
    flat_rows = blocks.reshape(-1, blocks.shape[-1])
    product = jnp.dot(flat_rows, matrix, preferred_element_type=jnp.float32)
    return product.reshape(blocks.shape[:-1] + (matrix.shape[1],))

def contract_rows(left_side, right_side):
    return lax.dot_general(left_side, right_side, (((0,), (0,)), ((), ())), preferred_element_type=jnp.float32)

def contracted_columns(left_side, right_side):
    return lax.dot_general(left_side, right_side, (((1,), (1,)), ((), ())), preferred_element_type=jnp.float32)

def decoder_forward(grid_point_rows, latent_node_rows, weight_params):
    w_query, w_key, w_value, w_mix, readout_weight = weight_params
    features = grid_point_rows.shape[-1]
    factor = (features // HEADS) ** (-0.5)
    queries = rows_times(grid_point_rows, w_query).astype(jnp.bfloat16)
    keyset = rows_times(latent_node_rows, w_key).astype(jnp.bfloat16)
    valueset = rows_times(latent_node_rows, w_value).astype(jnp.bfloat16)
    scores = jnp.einsum('tqhd,tkhd->thqk', by_heads(queries), by_heads(keyset)) * factor
    highest = lax.optimization_barrier(jnp.max(scores, axis=-1, keepdims=True))
    raised = jnp.exp(scores - highest)
    softmaxed = raised / lax.optimization_barrier(jnp.sum(raised, axis=-1, keepdims=True))
    softmaxed_b = softmaxed.astype(jnp.bfloat16)
    attended = jnp.einsum('thqk,tkhd->tqhd', widened(softmaxed_b), by_heads(valueset))
    attended = attended.reshape(grid_point_rows.shape).astype(jnp.bfloat16)
    hidden = grid_point_rows.astype(jnp.float32) + rows_times(attended, w_mix)
    inverse = lax.rsqrt(lax.optimization_barrier(jnp.mean(hidden * hidden, axis=-1, keepdims=True)) + EPS)
    normed = hidden * inverse
    normed_backward = normed.astype(jnp.bfloat16).reshape(-1, features)
    member_prediction = contracted_columns(readout_weight, normed_backward)
    saved_activations = (grid_point_rows, latent_node_rows, queries, keyset, valueset, softmaxed, softmaxed_b, attended, inverse, normed, normed_backward)
    return (member_prediction, saved_activations)

def backward(saved_activations, loss_slopes, weight_params):
    w_query, w_key, w_value, w_mix, readout_weight = weight_params
    grid_point_rows, latent_node_rows, queries, keyset, valueset, softmaxed, softmaxed_b, attended, inverse, normed, normed_backward = saved_activations
    features = grid_point_rows.shape[-1]
    factor = (features // HEADS) ** (-0.5)
    slopes_b = loss_slopes.astype(jnp.bfloat16)
    grad_out = jnp.dot(slopes_b, normed_backward, preferred_element_type=jnp.float32)
    d_normed = contract_rows(slopes_b, readout_weight)
    normed_rows = normed.reshape(-1, features)
    d_hidden = inverse.reshape(-1, 1) * (d_normed - normed_rows * lax.optimization_barrier(jnp.mean(d_normed * normed_rows, axis=-1, keepdims=True)))
    d_hidden_b = d_hidden.astype(jnp.bfloat16)
    grad_mix = contract_rows(attended.reshape(-1, features), d_hidden_b)
    d_attended = contracted_columns(d_hidden_b, w_mix).astype(jnp.bfloat16).reshape(grid_point_rows.shape)
    d_probs = jnp.einsum('tqhd,tkhd->thqk', by_heads(d_attended), by_heads(valueset))
    d_values = jnp.einsum('thqk,tqhd->tkhd', widened(softmaxed_b), by_heads(d_attended))
    d_values = d_values.reshape(latent_node_rows.shape).astype(jnp.bfloat16)
    d_scores = softmaxed * (d_probs - lax.optimization_barrier(jnp.sum(d_probs * softmaxed, axis=-1, keepdims=True))) * factor
    d_scores_b = d_scores.astype(jnp.bfloat16)
    d_queries = jnp.einsum('thqk,tkhd->tqhd', widened(d_scores_b), by_heads(keyset))
    d_queries = d_queries.reshape(grid_point_rows.shape).astype(jnp.bfloat16)
    d_keys = jnp.einsum('thqk,tqhd->tkhd', widened(d_scores_b), by_heads(queries))
    d_keys = d_keys.reshape(latent_node_rows.shape).astype(jnp.bfloat16)
    grid_flat = grid_point_rows.reshape(-1, features)
    node_flat = latent_node_rows.reshape(-1, features)
    grad_query = contract_rows(grid_flat, d_queries.reshape(-1, features))
    grad_key = contract_rows(node_flat, d_keys.reshape(-1, features))
    grad_value = contract_rows(node_flat, d_values.reshape(-1, features))
    return (grad_out, grad_query, grad_key, grad_value, grad_mix)

def member_ranked_score(member_own_field, members_all, truth_rows, loss_scale_weight):
    members_count = members_all.shape[0]
    to_truth = member_own_field - truth_rows[None]
    skill_term = jnp.sqrt(to_truth * to_truth + SMOOTH)

    def add_member(running, other_member):
        apart_by = member_own_field - other_member[None]
        spread = jnp.sqrt(apart_by * apart_by + SMOOTH)
        return ((running[0] + spread, running[1] + apart_by / spread), None)
    zero_field = jnp.zeros(member_own_field.shape, jnp.float32)
    (spread_sum, slope_sum), _ = lax.scan(add_member, (zero_field, zero_field), members_all)
    pair_weight = 1.0 / (members_count * (members_count - 1))
    loss_part = loss_scale_weight * (jnp.sum(skill_term) / members_count - 0.5 * pair_weight * jnp.sum(spread_sum - jnp.sqrt(jnp.float32(SMOOTH))))
    loss_slopes = loss_scale_weight * (to_truth / skill_term / members_count - pair_weight * slope_sum)
    return (loss_part, loss_slopes)

def reference(grid_hidden, latent, tile_neighbor_index, target, w_query, w_key, w_value, w_mix, readout_weight):
    members_count, points, features = grid_hidden.shape
    tile_layout = grid_hidden.reshape(members_count, points // 128, 128, features)
    weight_params = (w_query, w_key, w_value, w_mix, readout_weight)

    def predict_fields(member_data):
        return decoder_forward(member_data[0], member_data[1][tile_neighbor_index], weight_params)[0]
    ensemble_predictions = lax.map(predict_fields, (tile_layout, latent))
    loss_scale_weight = (target.shape[0] * target.shape[1]) ** (-0.5)
    fair_ranked_score_loss, loss_slopes = member_ranked_score(ensemble_predictions, ensemble_predictions, target, loss_scale_weight)

    def accumulate(totals, member_data):
        grid_partial, latent_partial, slope_m = member_data
        member_prediction, saved_activations = decoder_forward(grid_partial, latent_partial[tile_neighbor_index], weight_params)
        gradients = backward(saved_activations, slope_m, weight_params)
        return (tuple((first + second for first, second in zip(totals, gradients))), None)
    square = jnp.zeros((features, features), jnp.float32)
    start_sums = (jnp.zeros((target.shape[0], features), jnp.float32), square, square, square, square)
    totals, _ = lax.scan(accumulate, start_sums, (tile_layout, latent, loss_slopes))
    grad_out, grad_query, grad_key, grad_value, grad_mix = totals
    return (fair_ranked_score_loss, grad_out, grad_query, grad_key, grad_value, grad_mix)
```

```python
import jax
import jax.numpy as jnp
from jax import lax
from jax.sharding import PartitionSpec as P

HEADS = 16
EPS = 1e-06
SMOOTH = 0.01


def swap(value, axis, bit):
    size = lax.axis_size(axis)
    return lax.ppermute(value, axis, [(i, i ^ bit) for i in range(size)])


def gather_shards(value, axis):
    size = lax.axis_size(axis)
    parts, slots = value[None], [0]
    bit = size // 2
    while bit:
        parts = jnp.concatenate([parts, swap(parts, axis, bit)], axis=0)
        slots = slots + [s ^ bit for s in slots]
        bit //= 2
    return parts, slots


def in_shard_order(parts, slots, axis):
    place = [0] * len(slots)
    for position, slot in enumerate(slots):
        place[slot] = position
    order = jnp.asarray(place, jnp.int32)[lax.axis_index(axis) ^ jnp.arange(len(slots))]
    return jnp.take(parts, order, axis=0)


def by_heads(values_in):
    return values_in.reshape(values_in.shape[0], HEADS, values_in.shape[1] // HEADS)


def dot32(left, right, dims):
    return lax.dot_general(left, right, (dims, ((), ())), preferred_element_type=jnp.float32)


def rows_times(rows, matrix):
    return dot32(rows, matrix, ((1,), (0,)))


def split16(value):
    high = lax.reduce_precision(value, 8, 7)
    return high.astype(jnp.bfloat16), (value - high).astype(jnp.bfloat16)


def forward(grid_rows, node_rows, weights):
    w_query, w_key, w_value, w_mix, readout_weight = weights
    features = grid_rows.shape[-1]
    factor = (features // HEADS) ** (-0.5)
    queries = rows_times(grid_rows, w_query).astype(jnp.bfloat16)
    keyset = rows_times(node_rows, w_key).astype(jnp.bfloat16)
    valueset = rows_times(node_rows, w_value).astype(jnp.bfloat16)
    scores = factor * jnp.einsum(
        "qhd,khd->hqk", by_heads(queries), by_heads(keyset), preferred_element_type=jnp.float32
    )
    raised = jnp.exp(scores - jnp.max(scores, axis=-1, keepdims=True))
    softmaxed = raised / jnp.sum(raised, axis=-1, keepdims=True)
    attended = jnp.einsum(
        "hqk,khd->qhd",
        softmaxed.astype(jnp.bfloat16),
        by_heads(valueset),
        preferred_element_type=jnp.float32,
    )
    attended = attended.reshape(grid_rows.shape).astype(jnp.bfloat16)
    hidden = grid_rows.astype(jnp.float32) + rows_times(attended, w_mix)
    inverse = lax.rsqrt(jnp.mean(hidden * hidden, axis=-1, keepdims=True) + EPS)
    normed = hidden * inverse
    normed_b = normed.astype(jnp.bfloat16)
    forecast = dot32(readout_weight, normed_b, ((1,), (1,)))
    return forecast, (queries, keyset, valueset, softmaxed, attended, inverse, normed, normed_b)


def backward(saved, slopes_b, weights):
    w_query, w_key, w_value, w_mix, readout_weight = weights
    queries, keyset, valueset, softmaxed, attended, inverse, normed, normed_b = saved
    features = queries.shape[-1]
    factor = (features // HEADS) ** (-0.5)
    softmaxed_b = softmaxed.astype(jnp.bfloat16)
    d_normed = dot32(slopes_b, readout_weight, ((0,), (0,)))
    d_hidden = inverse * (d_normed - normed * jnp.mean(d_normed * normed, axis=-1, keepdims=True))
    d_hidden = d_hidden.astype(jnp.bfloat16)
    d_attended = dot32(d_hidden, w_mix, ((1,), (1,))).astype(jnp.bfloat16)
    d_heads = by_heads(d_attended)
    d_probs = jnp.einsum(
        "qhd,khd->hqk", d_heads, by_heads(valueset), preferred_element_type=jnp.float32
    )
    d_values = jnp.einsum(
        "hqk,qhd->khd", softmaxed_b, d_heads, preferred_element_type=jnp.float32
    )
    d_scores = softmaxed * (d_probs - jnp.sum(d_probs * softmaxed, axis=-1, keepdims=True)) * factor
    d_scores = d_scores.astype(jnp.bfloat16)
    d_queries = jnp.einsum(
        "hqk,khd->qhd", d_scores, by_heads(keyset), preferred_element_type=jnp.float32
    )
    d_keys = jnp.einsum(
        "hqk,qhd->khd", d_scores, by_heads(queries), preferred_element_type=jnp.float32
    )
    flat = lambda v: v.reshape(queries.shape).astype(jnp.bfloat16)
    return d_hidden, flat(d_queries), flat(d_keys), flat(d_values)


def ranked_score(fields, truth, weight):
    members = fields.shape[0]
    pair_weight = 1.0 / (members * (members - 1))
    to_truth = fields - truth[None]
    skill = jnp.sqrt(to_truth * to_truth + SMOOTH)
    apart = fields[:, None] - fields[None, :]
    spread = jnp.sqrt(apart * apart + SMOOTH)
    loss = weight * (
        jnp.sum(skill) / members
        - 0.5 * pair_weight * jnp.sum(jnp.sum(spread, axis=1) - jnp.sqrt(jnp.float32(SMOOTH)))
    )
    slopes = weight * (to_truth / skill / members - pair_weight * jnp.sum(apart / spread, axis=1))
    return loss, slopes


def rows_of(flat, width):
    short = -flat.shape[0] % (16 * width)
    return jnp.pad(flat, (0, short)).reshape(-1, width)


def body(
    grid_hidden, latent, tile_neighbor_index, target, w_query, w_key, w_value, w_mix, readout_weight
):
    nodes, features = latent.shape[1:]
    points = grid_hidden.shape[1]
    channels = target.shape[0]
    shards, members = lax.axis_size("space"), lax.axis_size("ens")
    shard, member = lax.axis_index("space"), lax.axis_index("ens")
    weights = (w_query, w_key, w_value, w_mix, readout_weight)
    weight = (channels * points * shards) ** (-0.5)
    width, depth = features // shards, features // members
    bf16 = jnp.bfloat16

    latents, latent_slots = gather_shards(latent[0], "space")
    latents = in_shard_order(latents, latent_slots, "space").reshape(-1, features)
    index = tile_neighbor_index.reshape(-1)
    node_rows = jnp.take(latents, index, axis=0)
    grid_rows = grid_hidden[0]
    forecast, saved = forward(grid_rows, node_rows, weights)
    attended, normed_b = saved[4], saved[7]

    tags = jnp.concatenate([index // 128, index % 128]).astype(bf16)
    extra = jnp.concatenate([grid_rows, attended, rows_of(tags, features)], axis=0)

    high, low = split16(forecast)
    slices = jnp.transpose(normed_b.reshape(points, members, depth), (1, 0, 2))
    fields = jnp.concatenate([high.reshape(-1), low.reshape(-1)])
    packed = jnp.concatenate(
        [
            jnp.broadcast_to(fields, (members,) + fields.shape).reshape(members, -1, 128),
            slices.reshape(members, -1, 128),
        ],
        axis=1,
    )
    extras, slots = gather_shards(extra, "space")
    packed = lax.all_to_all(packed, "ens", split_axis=0, concat_axis=0, tiled=True)
    size = channels * points // 128
    fields = (packed[:, :size].astype(jnp.float32) + packed[:, size : 2 * size]).reshape(
        members, channels, points
    )
    loss, slopes = ranked_score(fields, target, weight)
    slopes_b = slopes.astype(bf16)
    grad_out = jnp.einsum(
        "mcp,mpf->cf",
        slopes_b,
        packed[:, 2 * size :].reshape(members, points, depth),
        preferred_element_type=jnp.float32,
    )
    own_slopes = lax.dynamic_index_in_dim(slopes_b, member, 0, keepdims=False)
    d_hidden, d_queries, d_keys, d_values = backward(saved, own_slopes, weights)

    high = lax.reduce_precision(loss, 8, 7)
    low = lax.reduce_precision(loss - high, 8, 7)
    rest = loss - high - low
    small = jnp.concatenate([grad_out.astype(bf16).reshape(-1), jnp.stack([high, low, rest]).astype(bf16)])
    small = rows_of(small, width)
    blocks = jnp.concatenate([d_queries, d_keys, d_values, d_hidden], axis=0)
    blocks = jnp.transpose(blocks.reshape(-1, shards, width), (1, 0, 2))
    blocks = jnp.concatenate(
        [blocks, jnp.broadcast_to(small, (shards,) + small.shape)], axis=1
    )
    blocks = lax.all_to_all(blocks, "space", split_axis=0, concat_axis=0, tiled=True)
    small = blocks[:, 4 * points :].astype(jnp.float32).reshape(shards, -1)
    small = jnp.sum(small[:, : channels * depth + 3], axis=0)
    fair_ranked_score_loss = jnp.sum(small[-3:])
    d_all = blocks[:, : 4 * points].reshape(shards, 4, points, width)

    extras = in_shard_order(extras, slots, "space")
    tags = extras[:, 2 * points :].reshape(shards, -1)[:, : 2 * points].astype(jnp.int32)
    index = (tags[:, :points] * 128 + tags[:, points:]).reshape(-1)
    all_nodes = jnp.take(latents, index, axis=0)
    all_grid = extras[:, :points].reshape(-1, features)
    all_attended = extras[:, points : 2 * points].reshape(-1, features)
    pick = lambda i: d_all[:, i].reshape(-1, width)
    gradients = [
        dot32(rows, pick(i), ((0,), (0,))).astype(bf16).reshape(members, depth, width)
        for i, rows in enumerate((all_grid, all_nodes, all_nodes, all_attended))
    ]
    tail = rows_of(small[:-3].astype(bf16), width)
    gradients.append(jnp.broadcast_to(tail, (members,) + tail.shape))
    gradients = jnp.concatenate(gradients, axis=1)
    gradients = lax.all_to_all(gradients, "ens", split_axis=0, concat_axis=0, tiled=True)
    grad_out = gradients[:, 4 * depth :].reshape(members, -1)[:, : channels * depth]
    grad_out = jnp.transpose(grad_out.reshape(members, channels, depth), (1, 0, 2))
    grad_out = grad_out.reshape(channels, features).astype(jnp.float32)
    sums = jnp.sum(gradients[:, : 4 * depth].astype(jnp.float32), axis=0)
    grads = [sums[i * depth : (i + 1) * depth] for i in range(4)]
    return (fair_ranked_score_loss, grad_out, grads[0], grads[1], grads[2], grads[3])


def solution(mesh):
    in_specs = (
        P("ens", "space", None),
        P("ens", "space", None),
        P("space", None),
        P(None, "space"),
        P(),
        P(),
        P(),
        P(),
        P(),
    )
    out_specs = (
        P(),
        P(),
        P("ens", "space"),
        P("ens", "space"),
        P("ens", "space"),
        P("ens", "space"),
    )
    return jax.shard_map(body, mesh=mesh, in_specs=in_specs, out_specs=out_specs, check_vma=False)
```

```python
import functools

import jax
import jax.numpy as jnp
from jax import lax
from jax.experimental import pallas as pl
from jax.experimental.pallas import tpu as pltpu
from jax.sharding import PartitionSpec as P

HEADS = 16
EPS = 1e-06
SMOOTH = 0.01
LANES = 128
MISC = 8
BF16, F32 = jnp.bfloat16, jnp.float32
VMEM = pl.BlockSpec(memory_space=pltpu.VMEM)
SMEM = pl.BlockSpec(memory_space=pltpu.SMEM)
ANY = pl.BlockSpec(memory_space=pl.ANY)


def dot32(left, right, contract=(1, 0)):
    dims = (((contract[0],), (contract[1],)), ((), ()))
    return lax.dot_general(left, right, dims, preferred_element_type=F32)


def swap(value, axis, bits):
    size = lax.axis_size(axis)
    return lax.ppermute(value, axis, [(i, i ^ bits) for i in range(size)])


def gather_slots(value, axis):
    parts = [value]
    for k in range(1, lax.axis_size(axis)):
        parts.append(swap(parts[k - 1], axis, 1) if k % 2 else swap(value, axis, k))
    return parts


def halves(pair):
    lane = lax.broadcasted_iota(jnp.int32, pair.shape, 1)
    zero = jnp.zeros_like(pair)
    first = lane < pair.shape[1] // 2
    return jnp.concatenate([jnp.where(first, pair, zero), jnp.where(first, zero, pair)], axis=0)


def joined(blocks):
    rows = blocks.shape[0] // 2
    lane = lax.broadcasted_iota(jnp.int32, (rows, blocks.shape[1]), 1)
    return jnp.where(lane < blocks.shape[1] // 2, blocks[:rows], blocks[rows:])


def query_kernel(rows_ref, w_hbm, out_ref, w_ref, sem):
    chunks = w_ref.shape[0]
    step = w_ref.shape[2]
    copies = [
        pltpu.make_async_copy(w_hbm.at[:, pl.ds(c * step, step)], w_ref.at[c], sem.at[c])
        for c in range(chunks)
    ]
    for copy in copies:
        copy.start()
    for c, copy in enumerate(copies):
        copy.wait()
        out_ref[:, c * step : (c + 1) * step] = dot32(rows_ref[...], w_ref[c]).astype(BF16)


def project_queries(rows, weight):
    features = weight.shape[0]
    step = min(512, features)
    return pl.pallas_call(
        query_kernel,
        out_shape=jax.ShapeDtypeStruct(rows.shape, BF16),
        in_specs=[VMEM, ANY],
        out_specs=VMEM,
        scratch_shapes=[
            pltpu.VMEM((features // step, features, step), BF16),
            pltpu.SemaphoreType.DMA((features // step,)),
        ],
        cost_estimate=pl.CostEstimate(
            flops=2 * rows.size * features, bytes_accessed=2 * weight.size, transcendentals=0
        ),
        name="project_queries",
    )(rows, weight)


def forward_kernel(shards, members, *refs):
    position_ref, grid_ref, query_ref, readout_ref = refs[:4]
    latent_refs = refs[4 : 4 + shards]
    weights_hbm = refs[4 + shards : 7 + shards]
    (
        key_ref,
        value_ref,
        soft_ref,
        attended_ref,
        normed_ref,
        inverse_ref,
        packed_ref,
        *w_refs,
        sem,
    ) = refs[7 + shards :]
    copies = [pltpu.make_async_copy(s, d, sem.at[i]) for i, (s, d) in enumerate(zip(weights_hbm, w_refs))]
    for copy in copies:
        copy.start()
    points, features = grid_ref.shape
    latents = jnp.concatenate([ref[...] for ref in latent_refs], axis=0)
    node = lax.broadcasted_iota(jnp.int32, (points, latents.shape[0]), 1)
    chosen = jnp.where(node == position_ref[...], 1.0, 0.0).astype(BF16)
    nodes = dot32(chosen, latents).astype(BF16)
    copies[0].wait()
    key_ref[...] = dot32(nodes, w_refs[0][...]).astype(BF16)
    copies[1].wait()
    value_ref[...] = dot32(nodes, w_refs[1][...]).astype(BF16)
    factor = (features // HEADS) ** (-0.5)
    for pair in range(features // LANES):
        at = slice(pair * LANES, (pair + 1) * LANES)
        scores = dot32(query_ref[:, at], halves(key_ref[:, at]), (1, 1)) * factor
        soft = []
        for head in range(2):
            block = scores[:, head * LANES : (head + 1) * LANES]
            raised = jnp.exp(block - jnp.max(block, axis=-1, keepdims=True))
            soft.append(raised / jnp.sum(raised, axis=-1, keepdims=True))
        soft = jnp.concatenate(soft, axis=1)
        soft_ref[pair] = soft
        attended_ref[:, at] = dot32(soft.astype(BF16), halves(value_ref[:, at])).astype(BF16)
    copies[2].wait()
    hidden = grid_ref[...].astype(F32) + dot32(attended_ref[...], w_refs[2][...])
    inverse = lax.rsqrt(jnp.mean(hidden * hidden, axis=-1, keepdims=True) + EPS)
    normed = hidden * inverse
    normed_ref[...] = normed
    inverse_ref[...] = inverse
    normed_b = normed.astype(BF16)
    forecast = dot32(readout_ref[...], normed_b, (1, 1))
    high = forecast.astype(BF16)
    low = (forecast - high.astype(F32)).astype(BF16)
    channels = readout_ref.shape[0]
    depth = features // members
    pieces = LANES // depth
    part = points // pieces
    for m in range(members):
        packed_ref[m, :channels] = high
        packed_ref[m, channels : 2 * channels] = low
        for p in range(pieces):
            packed_ref[m, 2 * channels :, p * depth : (p + 1) * depth] = normed_b[
                p * part : (p + 1) * part, m * depth : (m + 1) * depth
            ]


def forward(position, grid_rows, queries, readout, latents, weights, members):
    points, features = grid_rows.shape
    channels = readout.shape[0]
    depth = features // members
    rows = 2 * channels + points * depth // LANES
    shape = jax.ShapeDtypeStruct
    return pl.pallas_call(
        functools.partial(forward_kernel, len(latents), members),
        out_shape=(
            shape((points, features), BF16),
            shape((points, features), BF16),
            shape((features // LANES, points, 2 * LANES), F32),
            shape((points, features), BF16),
            shape((points, features), F32),
            shape((points, 1), F32),
            shape((members, rows, LANES), BF16),
        ),
        in_specs=[VMEM] * (4 + len(latents)) + [ANY] * 3,
        out_specs=(VMEM,) * 7,
        scratch_shapes=[pltpu.VMEM((features, features), BF16)] * 3
        + [pltpu.SemaphoreType.DMA((3,))],
        cost_estimate=pl.CostEstimate(
            flops=8 * points * features * features,
            bytes_accessed=6 * features * features,
            transcendentals=points * LANES * HEADS,
        ),
        name="decoder_forward",
    )(position, grid_rows, queries, readout, *latents, *weights)


def backward_kernel(
    shards,
    channels_used,
    member_ref,
    packed_ref,
    target_ref,
    index_ref,
    query_ref,
    key_ref,
    value_ref,
    soft_ref,
    normed_ref,
    inverse_ref,
    readout_ref,
    w_hbm,
    out_ref,
    w_ref,
    slope_ref,
    d_attended_ref,
    small_ref,
    sem,
):
    copy = pltpu.make_async_copy(w_hbm, w_ref, sem)
    copy.start()
    members = packed_ref.shape[0]
    points, features = normed_ref.shape
    channels = readout_ref.shape[0]
    width, depth = features // shards, features // members
    weight = (channels_used * points * shards) ** (-0.5)
    pair_weight = 1.0 / (members * (members - 1))
    chunk = 16

    def crps(c, loss):
        at = pl.ds(pl.multiple_of(c * chunk, chunk), chunk)
        low_at = pl.ds(pl.multiple_of(c * chunk + channels, chunk), chunk)
        fields = [
            packed_ref[m, at].astype(F32) + packed_ref[m, low_at].astype(F32)
            for m in range(members)
        ]
        truth = target_ref[at]
        skill = jnp.zeros_like(truth)
        slopes = []
        for m in range(members):
            apart = fields[m] - truth
            square = apart * apart + SMOOTH
            root = lax.rsqrt(square)
            skill = skill + square * root
            slopes.append(apart * root * (weight / members))
        spread = jnp.zeros_like(truth)
        for m in range(members):
            for k in range(m):
                apart = fields[m] - fields[k]
                square = apart * apart + SMOOTH
                root = lax.rsqrt(square)
                spread = spread + square * root
                ratio = apart * root * (weight * pair_weight)
                slopes[m] = slopes[m] - ratio
                slopes[k] = slopes[k] + ratio
        for m in range(members):
            slope_ref[m, at] = slopes[m].astype(BF16)
        channel = c * chunk + lax.broadcasted_iota(jnp.int32, truth.shape, 0)
        term = skill * (1.0 / members) - spread * pair_weight
        return loss + jnp.where(channel < channels_used, term, 0.0)

    loss = lax.fori_loop(0, channels // chunk, crps, jnp.zeros((chunk, points), F32))
    loss = weight * jnp.sum(jnp.sum(loss, axis=0, keepdims=True), axis=1, keepdims=True)

    pieces = LANES // depth
    part = points // pieces
    total = jnp.zeros((channels, depth), F32)
    for m in range(members):
        tail = packed_ref[m, 2 * channels :]
        for p in range(pieces):
            total = total + dot32(
                slope_ref[m][:, p * part : (p + 1) * part], tail[:, p * depth : (p + 1) * depth]
            )
    rows = small_ref.shape[0] - MISC
    for p in range(channels // rows):
        small_ref[:rows, p * depth : (p + 1) * depth] = total[p * rows : (p + 1) * rows]
    first = loss.astype(BF16).astype(F32)
    second = (loss - first).astype(BF16).astype(F32)
    for i, value in enumerate((first, second, loss - first - second)):
        small_ref[rows + i : rows + i + 1] = jnp.broadcast_to(value, (1, width))
    small_ref[rows + 3 : rows + MISC] = jnp.zeros((MISC - 3, width), F32)
    small_ref[rows + 3 : rows + 3 + index_ref.shape[0]] = index_ref[...]
    small = small_ref[...].astype(BF16)
    for s in range(shards):
        out_ref[s, 4 * points :] = small

    def put(kind, column, value):
        step = min(width, value.shape[1])
        for c in range(0, value.shape[1], step):
            shard, lane = divmod(column + c, width)
            out_ref[shard, kind * points : (kind + 1) * points, lane : lane + step] = value[
                :, c : c + step
            ]

    own = slope_ref[member_ref[0]]
    normed = normed_ref[...]
    d_normed = dot32(own, readout_ref[...], (0, 0))
    mean = jnp.mean(d_normed * normed, axis=-1, keepdims=True)
    d_hidden = (inverse_ref[...] * (d_normed - normed * mean)).astype(BF16)
    put(3, 0, d_hidden)
    copy.wait()
    d_attended_ref[...] = dot32(d_hidden, w_ref[...], (1, 1)).astype(BF16)
    factor = (features // HEADS) ** (-0.5)
    for pair in range(features // LANES):
        at = slice(pair * LANES, (pair + 1) * LANES)
        soft = soft_ref[pair]
        d_out = d_attended_ref[:, at]
        d_probs = dot32(d_out, halves(value_ref[:, at]), (1, 1))
        put(2, pair * LANES, joined(dot32(soft.astype(BF16), d_out, (0, 0))).astype(BF16))
        product = d_probs * soft
        d_scores = []
        for head in range(2):
            block = slice(head * LANES, (head + 1) * LANES)
            summed = jnp.sum(product[:, block], axis=-1, keepdims=True)
            d_scores.append(soft[:, block] * (d_probs[:, block] - summed) * factor)
        d_scores = jnp.concatenate(d_scores, axis=1).astype(BF16)
        put(0, pair * LANES, dot32(d_scores, halves(key_ref[:, at])).astype(BF16))
        put(1, pair * LANES, joined(dot32(d_scores, query_ref[:, at], (0, 0))).astype(BF16))


def backward(member, packed, target, index, saved, readout, w_mix, shards, channels_used):
    members = packed.shape[0]
    features = w_mix.shape[0]
    points = saved[0].shape[0]
    channels = readout.shape[0]
    width, depth = features // shards, features // members
    small = channels * depth // width + MISC
    small = small + -small % 16
    return pl.pallas_call(
        functools.partial(backward_kernel, shards, channels_used),
        out_shape=jax.ShapeDtypeStruct((shards, 4 * points + small, width), BF16),
        in_specs=[SMEM] + [VMEM] * 10 + [ANY],
        out_specs=VMEM,
        scratch_shapes=[
            pltpu.VMEM((features, features), BF16),
            pltpu.VMEM((members, channels, points), BF16),
            pltpu.VMEM((points, features), BF16),
            pltpu.VMEM((channels * depth // width + MISC, width), F32)
            if small == channels * depth // width + MISC
            else pltpu.VMEM((small, width), F32),
            pltpu.SemaphoreType.DMA,
        ],
        cost_estimate=pl.CostEstimate(
            flops=4 * points * features * features,
            bytes_accessed=4 * features * features,
            transcendentals=0,
        ),
        name="decoder_backward",
    )(member, packed, target, index, *saved, readout, w_mix)


def gradient_kernel(shards, members, nodes, channels, shard_ref, blocks_ref, *refs):
    latent_refs, grid_refs, attended_refs = (refs[i * shards : (i + 1) * shards] for i in range(3))
    out_ref, loss_ref = refs[3 * shards :]
    points, features = grid_refs[0].shape
    width, depth = features // shards, features // members
    shard = shard_ref[0]
    rows = channels * depth // width
    start = 4 * points
    small = jnp.zeros((blocks_ref.shape[1] - start, width), F32)
    for s in range(shards):
        small = small + blocks_ref[s, start:].astype(F32)
    loss_ref[...] = jnp.sum(small[rows : rows + 3, :1], axis=0, keepdims=True)
    small = small.astype(BF16)
    for m in range(members):
        out_ref[m, 4 * depth :] = small

    def slots(kind):
        at = slice(kind * points, (kind + 1) * points)
        return jnp.concatenate([blocks_ref[shard ^ k, at] for k in range(shards)], axis=0)

    def put(kind, lefts, right):
        left = jnp.concatenate([ref[...] for ref in lefts], axis=0)
        total = dot32(left, right, (0, 0)).astype(BF16)
        for m in range(members):
            out_ref[m, kind * depth : (kind + 1) * depth] = total[m * depth : (m + 1) * depth]

    put(3, attended_refs, slots(3))
    chosen = []
    for k in range(shards):
        index = blocks_ref[shard ^ k, start + rows : start + rows + MISC].astype(jnp.int32)
        if width >= 2 * points:
            owner, offset = index[3:4, :points], index[3:4, points : 2 * points]
        else:
            lines = points // width
            owner, offset = (
                jnp.concatenate([index[3 + b + i : 4 + b + i] for i in range(lines)], axis=1)
                for b in (0, lines)
            )
        position = (owner ^ shard) * nodes + offset
        node = lax.broadcasted_iota(jnp.int32, (nodes * shards, points), 0)
        chosen.append(jnp.where(node == position, 1.0, 0.0).astype(BF16))
    chosen = jnp.concatenate(chosen, axis=1)
    put(1, latent_refs, dot32(chosen, slots(1)).astype(BF16))
    put(2, latent_refs, dot32(chosen, slots(2)).astype(BF16))
    put(0, grid_refs, slots(0))


def gradients(shard, blocks, latents, grids, attendeds, members, channels):
    shards, rows, width = blocks.shape
    points, features = grids[0].shape
    depth = features // members
    return pl.pallas_call(
        functools.partial(gradient_kernel, shards, members, latents[0].shape[0], channels),
        out_shape=(
            jax.ShapeDtypeStruct((members, 4 * depth + rows - 4 * points, width), BF16),
            jax.ShapeDtypeStruct((1, 1), F32),
        ),
        in_specs=[SMEM] + [VMEM] * (1 + 3 * shards),
        out_specs=(VMEM, VMEM),
        cost_estimate=pl.CostEstimate(
            flops=8 * points * shards * features * width,
            bytes_accessed=8 * points * shards * features,
            transcendentals=0,
        ),
        name="weight_gradients",
    )(shard, blocks, *latents, *grids, *attendeds)


def sum_kernel(channels, blocks_ref, out_ref, *grad_refs):
    members, _, width = blocks_ref.shape
    depth = grad_refs[0].shape[0]
    for i, ref in enumerate(grad_refs):
        at = slice(i * depth, (i + 1) * depth)
        total = blocks_ref[0, at].astype(F32)
        for m in range(1, members):
            total = total + blocks_ref[m, at].astype(F32)
        ref[...] = total
    rows = channels * depth // width
    for m in range(members):
        small = blocks_ref[m, 4 * depth :].astype(F32)
        for p in range(width // depth):
            last = min((p + 1) * rows, out_ref.shape[0])
            out_ref[p * rows : last, m * depth : (m + 1) * depth] = small[
                : last - p * rows, p * depth : (p + 1) * depth
            ]


def sum_members(blocks, channels, channels_used, depth):
    members, _, width = blocks.shape
    shape = jax.ShapeDtypeStruct
    return pl.pallas_call(
        functools.partial(sum_kernel, channels),
        out_shape=(shape((channels_used, depth * members), F32),) + (shape((depth, width), F32),) * 4,
        in_specs=[VMEM],
        out_specs=(VMEM,) * 5,
        name="sum_members",
    )(blocks)


def body(
    grid_hidden, latent, tile_neighbor_index, target, w_query, w_key, w_value, w_mix, readout_weight
):
    nodes, features = latent.shape[1:]
    points = grid_hidden.shape[1]
    channels_used = target.shape[0]
    shards, members = lax.axis_size("space"), lax.axis_size("ens")
    shard, member = lax.axis_index("space"), lax.axis_index("ens")
    width, depth = features // shards, features // members

    latents = gather_slots(latent[0], "space")
    grid_rows = grid_hidden[0]
    queries = project_queries(grid_rows, w_query)
    spare = ((0, -channels_used % 16), (0, 0))
    readout = jnp.pad(readout_weight, spare)
    truth = jnp.pad(target, spare)
    channels = readout.shape[0]
    index = tile_neighbor_index.reshape(-1)
    owner, offset = index // nodes, index % nodes
    tags = jnp.concatenate([owner, offset]).astype(F32).reshape(-1, width)
    position = ((owner ^ shard) * nodes + offset)[:, None]
    *saved, packed = forward(
        position, grid_rows, queries, readout, latents, (w_key, w_value, w_mix), members
    )
    keyset, valueset, soft, attended, normed, inverse = saved
    packed = lax.all_to_all(packed, "ens", split_axis=0, concat_axis=0, tiled=True)
    grids = gather_slots(grid_rows, "space")
    attendeds = gather_slots(attended, "space")
    saved = (queries, keyset, valueset, soft, normed, inverse)
    blocks = backward(
        member[None], packed, truth, tags, saved, readout, w_mix, shards, channels_used
    )
    blocks = lax.all_to_all(blocks, "space", split_axis=0, concat_axis=0, tiled=True)
    blocks, loss = gradients(shard[None], blocks, latents, grids, attendeds, members, channels)
    blocks = lax.all_to_all(blocks, "ens", split_axis=0, concat_axis=0, tiled=True)
    grad_out, *grads = sum_members(blocks, channels, channels_used, depth)
    return (loss.reshape(()), grad_out, *grads)


def solution(mesh):
    in_specs = (
        P("ens", "space", None),
        P("ens", "space", None),
        P("space", None),
        P(None, "space"),
        P(),
        P(),
        P(),
        P(),
        P(),
    )
    out_specs = (
        P(),
        P(),
        P("ens", "space"),
        P("ens", "space"),
        P("ens", "space"),
        P("ens", "space"),
    )
    return jax.shard_map(body, mesh=mesh, in_specs=in_specs, out_specs=out_specs, check_vma=False)
```

```python
import functools

import jax
import jax.numpy as jnp
from jax import lax
from jax.experimental import pallas as pl
from jax.experimental.pallas import tpu as pltpu
from jax.sharding import PartitionSpec as P


HEADS = 16
EPS = 1e-06
SMOOTH = 0.01
LANES = 128
MISC = 8
BF16, F32 = jnp.bfloat16, jnp.float32
VMEM = pl.BlockSpec(memory_space=pltpu.VMEM)
SMEM = pl.BlockSpec(memory_space=pltpu.SMEM)
ANY = pl.BlockSpec(memory_space=pl.ANY)


def dot32(left, right, contract=(1, 0)):
    dims = (((contract[0],), (contract[1],)), ((), ()))
    return lax.dot_general(left, right, dims, preferred_element_type=F32)


def swap(value, axis, bits):
    size = lax.axis_size(axis)
    return lax.ppermute(value, axis, [(i, i ^ bits) for i in range(size)])


def gather_slots(value, axis):
    parts = [value]
    for k in range(1, lax.axis_size(axis)):
        parts.append(swap(parts[k - 1], axis, 1) if k % 2 else swap(value, axis, k))
    return parts


def halves(pair):
    lane = lax.broadcasted_iota(jnp.int32, pair.shape, 1)
    zero = jnp.zeros_like(pair)
    first = lane < pair.shape[1] // 2
    return jnp.concatenate([jnp.where(first, pair, zero), jnp.where(first, zero, pair)], axis=0)


def joined(blocks):
    rows = blocks.shape[0] // 2
    lane = lax.broadcasted_iota(jnp.int32, (rows, blocks.shape[1]), 1)
    return jnp.where(lane < blocks.shape[1] // 2, blocks[:rows], blocks[rows:])


def query_kernel(rows_ref, w_hbm, out_ref, w_ref, sem):
    chunks = w_ref.shape[0]
    step = w_ref.shape[2]
    copies = [
        pltpu.make_async_copy(w_hbm.at[:, pl.ds(c * step, step)], w_ref.at[c], sem.at[c])
        for c in range(chunks)
    ]
    for copy in copies:
        copy.start()
    for c, copy in enumerate(copies):
        copy.wait()
        out_ref[:, c * step : (c + 1) * step] = dot32(rows_ref[...], w_ref[c]).astype(BF16)


def project_queries(rows, weight):
    features = weight.shape[0]
    step = min(512, features)
    return pl.pallas_call(
        query_kernel,
        out_shape=jax.ShapeDtypeStruct(rows.shape, BF16),
        in_specs=[VMEM, ANY],
        out_specs=VMEM,
        scratch_shapes=[
            pltpu.VMEM((features // step, features, step), BF16),
            pltpu.SemaphoreType.DMA((features // step,)),
        ],
        cost_estimate=pl.CostEstimate(
            flops=2 * rows.size * features, bytes_accessed=2 * weight.size, transcendentals=0
        ),
        name="project_queries",
    )(rows, weight)


def forward_kernel(shards, members, *refs):
    position_ref, grid_ref, query_ref, readout_ref = refs[:4]
    latent_refs = refs[4 : 4 + shards]
    weights_hbm = refs[4 + shards : 7 + shards]
    (
        key_ref,
        value_ref,
        soft_ref,
        attended_ref,
        normed_ref,
        inverse_ref,
        packed_ref,
        *w_refs,
        sem,
    ) = refs[7 + shards :]
    copies = [pltpu.make_async_copy(s, d, sem.at[i]) for i, (s, d) in enumerate(zip(weights_hbm, w_refs))]
    for copy in copies:
        copy.start()
    points, features = grid_ref.shape
    latents = jnp.concatenate([ref[...] for ref in latent_refs], axis=0)
    node = lax.broadcasted_iota(jnp.int32, (points, latents.shape[0]), 1)
    chosen = jnp.where(node == position_ref[...], 1.0, 0.0).astype(BF16)
    nodes = dot32(chosen, latents).astype(BF16)
    copies[0].wait()
    key_ref[...] = dot32(nodes, w_refs[0][...]).astype(BF16)
    copies[1].wait()
    value_ref[...] = dot32(nodes, w_refs[1][...]).astype(BF16)
    factor = (features // HEADS) ** (-0.5)
    for pair in range(features // LANES):
        at = slice(pair * LANES, (pair + 1) * LANES)
        scores = dot32(query_ref[:, at], halves(key_ref[:, at]), (1, 1)) * factor
        soft = []
        for head in range(2):
            block = scores[:, head * LANES : (head + 1) * LANES]
            raised = jnp.exp(block - jnp.max(block, axis=-1, keepdims=True))
            soft.append(raised / jnp.sum(raised, axis=-1, keepdims=True))
        soft = jnp.concatenate(soft, axis=1)
        soft_ref[pair] = soft
        attended_ref[:, at] = dot32(soft.astype(BF16), halves(value_ref[:, at])).astype(BF16)
    copies[2].wait()
    hidden = grid_ref[...].astype(F32) + dot32(attended_ref[...], w_refs[2][...])
    inverse = lax.rsqrt(jnp.mean(hidden * hidden, axis=-1, keepdims=True) + EPS)
    normed = hidden * inverse
    normed_ref[...] = normed
    inverse_ref[...] = inverse
    normed_b = normed.astype(BF16)
    forecast = dot32(readout_ref[...], normed_b, (1, 1))
    high = forecast.astype(BF16)
    low = (forecast - high.astype(F32)).astype(BF16)
    channels = readout_ref.shape[0]
    depth = features // members
    pieces = LANES // depth
    part = points // pieces
    for m in range(members):
        packed_ref[m, :channels] = high
        packed_ref[m, channels : 2 * channels] = low
        for p in range(pieces):
            packed_ref[m, 2 * channels :, p * depth : (p + 1) * depth] = normed_b[
                p * part : (p + 1) * part, m * depth : (m + 1) * depth
            ]


def forward(position, grid_rows, queries, readout, latents, weights, members):
    points, features = grid_rows.shape
    channels = readout.shape[0]
    depth = features // members
    rows = 2 * channels + points * depth // LANES
    shape = jax.ShapeDtypeStruct
    return pl.pallas_call(
        functools.partial(forward_kernel, len(latents), members),
        out_shape=(
            shape((points, features), BF16),
            shape((points, features), BF16),
            shape((features // LANES, points, 2 * LANES), F32),
            shape((points, features), BF16),
            shape((points, features), F32),
            shape((points, 1), F32),
            shape((members, rows, LANES), BF16),
        ),
        in_specs=[VMEM] * (4 + len(latents)) + [ANY] * 3,
        out_specs=(VMEM,) * 7,
        scratch_shapes=[pltpu.VMEM((features, features), BF16)] * 3
        + [pltpu.SemaphoreType.DMA((3,))],
        cost_estimate=pl.CostEstimate(
            flops=8 * points * features * features,
            bytes_accessed=6 * features * features,
            transcendentals=points * LANES * HEADS,
        ),
        name="decoder_forward",
    )(position, grid_rows, queries, readout, *latents, *weights)


def backward_kernel(
    shards,
    blocks,
    channels_used,
    member_ref,
    packed_ref,
    target_ref,
    index_ref,
    query_ref,
    key_ref,
    value_ref,
    soft_ref,
    normed_ref,
    inverse_ref,
    readout_ref,
    w_hbm,
    out_ref,
    w_ref,
    slope_ref,
    d_attended_ref,
    small_ref,
    sem,
):
    copy = pltpu.make_async_copy(w_hbm, w_ref, sem)
    copy.start()
    members = packed_ref.shape[0]
    points, features = normed_ref.shape
    channels = readout_ref.shape[0]
    width, depth = features // blocks, features // members
    weight = (channels_used * points * shards) ** (-0.5)
    pair_weight = 1.0 / (members * (members - 1))
    chunk = 16

    def crps(c, loss):
        at = pl.ds(pl.multiple_of(c * chunk, chunk), chunk)
        low_at = pl.ds(pl.multiple_of(c * chunk + channels, chunk), chunk)
        fields = [
            packed_ref[m, at].astype(F32) + packed_ref[m, low_at].astype(F32)
            for m in range(members)
        ]
        truth = target_ref[at]
        skill = jnp.zeros_like(truth)
        slopes = []
        for m in range(members):
            apart = fields[m] - truth
            square = apart * apart + SMOOTH
            root = lax.rsqrt(square)
            skill = skill + square * root
            slopes.append(apart * root * (weight / members))
        spread = jnp.zeros_like(truth)
        for m in range(members):
            for k in range(m):
                apart = fields[m] - fields[k]
                square = apart * apart + SMOOTH
                root = lax.rsqrt(square)
                spread = spread + square * root
                ratio = apart * root * (weight * pair_weight)
                slopes[m] = slopes[m] - ratio
                slopes[k] = slopes[k] + ratio
        for m in range(members):
            slope_ref[m, at] = slopes[m].astype(BF16)
        channel = c * chunk + lax.broadcasted_iota(jnp.int32, truth.shape, 0)
        term = skill * (1.0 / members) - spread * pair_weight
        return loss + jnp.where(channel < channels_used, term, 0.0)

    loss = lax.fori_loop(0, channels // chunk, crps, jnp.zeros((chunk, points), F32))
    loss = weight * jnp.sum(jnp.sum(loss, axis=0, keepdims=True), axis=1, keepdims=True)

    pieces = LANES // depth
    part = points // pieces
    total = jnp.zeros((channels, depth), F32)
    for m in range(members):
        tail = packed_ref[m, 2 * channels :]
        for p in range(pieces):
            total = total + dot32(
                slope_ref[m][:, p * part : (p + 1) * part], tail[:, p * depth : (p + 1) * depth]
            )
    rows = channels * depth // width
    for p in range(width // depth):
        small_ref[:rows, p * depth : (p + 1) * depth] = total[p * rows : (p + 1) * rows]
    first = loss.astype(BF16).astype(F32)
    second = (loss - first).astype(BF16).astype(F32)
    for i, value in enumerate((first, second, loss - first - second)):
        small_ref[rows + i : rows + i + 1] = jnp.broadcast_to(value, (1, width))
    spare = small_ref.shape[0] - rows - 3
    small_ref[rows + 3 :] = jnp.zeros((spare, width), F32)
    small_ref[rows + 3 : rows + 3 + index_ref.shape[0]] = index_ref[...]
    small = small_ref[...].astype(BF16)
    for b in range(blocks):
        out_ref[b, 4 * points :] = small

    def put(kind, column, value):
        step = min(width, value.shape[1])
        for c in range(0, value.shape[1], step):
            block, lane = divmod(column + c, width)
            out_ref[block, kind * points : (kind + 1) * points, lane : lane + step] = value[
                :, c : c + step
            ]

    own = slope_ref[member_ref[0]]
    normed = normed_ref[...]
    d_normed = dot32(own, readout_ref[...], (0, 0))
    mean = jnp.mean(d_normed * normed, axis=-1, keepdims=True)
    d_hidden = (inverse_ref[...] * (d_normed - normed * mean)).astype(BF16)
    put(3, 0, d_hidden)
    copy.wait()
    d_attended_ref[...] = dot32(d_hidden, w_ref[...], (1, 1)).astype(BF16)
    factor = (features // HEADS) ** (-0.5)
    for pair in range(features // LANES):
        at = slice(pair * LANES, (pair + 1) * LANES)
        soft = soft_ref[pair]
        d_out = d_attended_ref[:, at]
        d_probs = dot32(d_out, halves(value_ref[:, at]), (1, 1))
        put(2, pair * LANES, joined(dot32(soft.astype(BF16), d_out, (0, 0))).astype(BF16))
        product = d_probs * soft
        d_scores = []
        for head in range(2):
            block = slice(head * LANES, (head + 1) * LANES)
            summed = jnp.sum(product[:, block], axis=-1, keepdims=True)
            d_scores.append(soft[:, block] * (d_probs[:, block] - summed) * factor)
        d_scores = jnp.concatenate(d_scores, axis=1).astype(BF16)
        put(0, pair * LANES, dot32(d_scores, halves(key_ref[:, at])).astype(BF16))
        put(1, pair * LANES, joined(dot32(d_scores, query_ref[:, at], (0, 0))).astype(BF16))


def small_rows(channels, depth, width):
    rows = channels * depth // width + MISC
    return rows + -rows % 16


def backward(member, packed, target, index, saved, readout, w_mix, shards, blocks, channels_used):
    members = packed.shape[0]
    features = w_mix.shape[0]
    points = saved[0].shape[0]
    channels = readout.shape[0]
    width, depth = features // blocks, features // members
    small = small_rows(channels, depth, width)
    return pl.pallas_call(
        functools.partial(backward_kernel, shards, blocks, channels_used),
        out_shape=jax.ShapeDtypeStruct((blocks, 4 * points + small, width), BF16),
        in_specs=[SMEM] + [VMEM] * 10 + [ANY],
        out_specs=VMEM,
        scratch_shapes=[
            pltpu.VMEM((features, features), BF16),
            pltpu.VMEM((members, channels, points), BF16),
            pltpu.VMEM((points, features), BF16),
            pltpu.VMEM((small, width), F32),
            pltpu.SemaphoreType.DMA,
        ],
        cost_estimate=pl.CostEstimate(
            flops=4 * points * features * features,
            bytes_accessed=4 * features * features,
            transcendentals=0,
        ),
        name="decoder_backward",
    )(member, packed, target, index, *saved, readout, w_mix)


def gradient_kernel(shards, pair, members, nodes, channels, place_ref, blocks_ref, *refs):
    latent_refs, early_refs, late_refs = (refs[i * shards : (i + 1) * shards] for i in range(3))
    out_ref, loss_ref = refs[3 * shards :]
    width = blocks_ref.shape[2]
    features = late_refs[0].shape[1]
    points = late_refs[0].shape[0] // pair
    depth = features // members
    lanes = pair * depth
    shard, half = place_ref[0], place_ref[1]
    rows = channels * depth // width
    start = 4 * points
    loss = jnp.zeros((1, 1), F32)
    for t in range(pair):
        total = jnp.zeros((blocks_ref.shape[1] - start, width), F32)
        for s in range(shards):
            total = total + blocks_ref[s * pair + t, start:].astype(F32)
        if t == 0:
            loss = jnp.sum(total[rows : rows + 3, :1], axis=0, keepdims=True)
        total = total.astype(BF16)
        for z in range(members // pair):
            for p in range(width // depth):
                out_ref[z, 4 * width + p * rows : 4 * width + (p + 1) * rows, t * depth : (t + 1) * depth] = (
                    total[:rows, p * depth : (p + 1) * depth]
                )
    loss_ref[...] = loss

    def slots(kind, t):
        at = slice(kind * points, (kind + 1) * points)
        return [blocks_ref[(shard ^ k) * pair + (half ^ t), at] for k in range(shards)]

    def put(kind, total):
        total = total.astype(BF16)
        at = slice(kind * width, kind * width + total.shape[0])
        for z in range(members // pair):
            out_ref[z, at] = total[:, z * lanes : (z + 1) * lanes]

    def rows_of(ref_list, part):
        at = slice(part * points, (part + 1) * points)
        return [ref[at] for ref in ref_list]

    def product(kind, parts):
        left = jnp.concatenate([v for t in range(pair) for v in slots(kind, t)], axis=0)
        right = jnp.concatenate([v for part in parts for v in part], axis=0)
        put(kind, dot32(left, right, (0, 0)))

    product(3, [rows_of(late_refs, t) for t in range(pair)])
    chosen = []
    for k in range(shards):
        index = blocks_ref[(shard ^ k) * pair, start + rows : start + rows + MISC].astype(jnp.int32)
        lines = max(points // width, 1)
        if width >= 2 * points:
            owner, offset = index[3:4, :points], index[3:4, points : 2 * points]
        else:
            owner, offset = (
                jnp.concatenate([index[3 + b + i : 4 + b + i] for i in range(lines)], axis=1)
                for b in (0, lines)
            )
        position = (owner ^ shard) * nodes + offset
        node = lax.broadcasted_iota(jnp.int32, (nodes * shards, points), 0)
        chosen.append(jnp.where(node == position, 1.0, 0.0).astype(BF16))
    chosen = jnp.concatenate(chosen, axis=1)
    sums = []
    for t in range(pair):
        both = [jnp.concatenate(slots(kind, t), axis=0) for kind in (1, 2)]
        sums.append(dot32(chosen, jnp.concatenate(both, axis=1)).astype(BF16))
    others = [[ref[...] for ref in latent_refs]]
    if pair > 1:
        others.append([ref[points : points + nodes] for ref in early_refs])
    put(
        1,
        dot32(
            jnp.concatenate(sums, axis=0),
            jnp.concatenate([v for part in others for v in part], axis=0),
            (0, 0),
        ),
    )
    grids = [rows_of(early_refs, 0)]
    if pair > 1:
        grids.append([ref[points + nodes :] for ref in early_refs])
    product(0, grids)


def gradients(place, blocks, latents, early, late, members, pair, channels):
    count, _, width = blocks.shape
    shards = count // pair
    features = late[0].shape[1]
    points = late[0].shape[0] // pair
    depth = features // members
    rows = 4 * width + channels
    return pl.pallas_call(
        functools.partial(
            gradient_kernel, shards, pair, members, latents[0].shape[0], channels
        ),
        out_shape=(
            jax.ShapeDtypeStruct((members // pair, rows, pair * depth), BF16),
            jax.ShapeDtypeStruct((1, 1), F32),
        ),
        in_specs=[SMEM] + [VMEM] * (1 + 3 * shards),
        out_specs=(VMEM, VMEM),
        cost_estimate=pl.CostEstimate(
            flops=8 * points * count * features * width,
            bytes_accessed=8 * points * count * features,
            transcendentals=0,
        ),
        name="weight_gradients",
    )(place, blocks, *latents, *early, *late)


def sum_kernel(pair, half_ref, blocks_ref, out_ref, *refs):
    count, _, lanes = blocks_ref.shape
    depth = lanes // pair
    used = out_ref.shape[0]
    width = refs[0].shape[1]
    for z in range(count):
        out_ref[:, z * lanes : (z + 1) * lanes] = blocks_ref[z, 4 * width : 4 * width + used].astype(F32)
    for i in range(4):
        at = slice(i * width, (i + 1) * width)
        total = blocks_ref[0, at].astype(F32)
        for z in range(1, count):
            total = total + blocks_ref[z, at].astype(F32)
        if pair == 1:
            refs[i][...] = total.T
        else:
            first, second = total[:, :depth], total[:, depth:]
            own = jnp.where(half_ref[0] == 0, first, second)
            other = jnp.where(half_ref[0] == 0, second, first)
            refs[i][...] = own.T
            refs[4][i * depth : (i + 1) * depth] = other.T.astype(BF16)


def sum_groups(half, blocks, pair, channels_used):
    count, rows, lanes = blocks.shape
    depth = lanes // pair
    width = (rows - (channels_used + -channels_used % 16)) // 4
    shape = jax.ShapeDtypeStruct
    outs = (shape((channels_used, lanes * count), F32),) + (shape((depth, width), F32),) * 4
    if pair > 1:
        outs = outs + (shape((4 * depth, width), BF16),)
    return pl.pallas_call(
        functools.partial(sum_kernel, pair),
        out_shape=outs,
        in_specs=[SMEM, VMEM],
        out_specs=(VMEM,) * len(outs),
        name="sum_groups",
    )(half, blocks)


def join_kernel(half_ref, other_ref, *refs):
    keep_refs, out_refs = refs[:4], refs[4:]
    depth, width = keep_refs[0].shape
    first = half_ref[0] == 0
    for i in range(4):
        own = keep_refs[i][...]
        other = other_ref[i * depth : (i + 1) * depth].astype(F32)
        out_refs[i][:, :width] = jnp.where(first, own, other)
        out_refs[i][:, width:] = jnp.where(first, other, own)


def join_columns(half, other, keeps):
    depth, width = keeps[0].shape
    return pl.pallas_call(
        join_kernel,
        out_shape=(jax.ShapeDtypeStruct((depth, 2 * width), F32),) * 4,
        in_specs=[SMEM] + [VMEM] * 5,
        out_specs=(VMEM,) * 4,
        name="join_columns",
    )(half, other, *keeps)


def body(
    grid_hidden, latent, tile_neighbor_index, target, w_query, w_key, w_value, w_mix, readout_weight
):
    nodes, features = latent.shape[1:]
    channels_used = target.shape[0]
    shards, members = lax.axis_size("space"), lax.axis_size("ens")
    shard, member = lax.axis_index("space"), lax.axis_index("ens")
    pair = 2 if members % 2 == 0 and shards <= 8 else 1
    half = member % pair
    count = shards * pair
    width = features // count
    groups = [
        [(g + y) * shards + s for s in range(shards) for y in range(pair)]
        for g in range(0, members, pair)
    ]
    lines = [list(range(y, members, pair)) for y in range(pair)]

    own_latent, grid_rows = latent[0], grid_hidden[0]
    latents = gather_slots(own_latent, "space")
    early = grid_rows
    if pair > 1:
        partner = swap(jnp.concatenate([own_latent, grid_rows]), "ens", 1)
        early = jnp.concatenate([grid_rows, partner])
    queries = project_queries(grid_rows, w_query)
    spare = ((0, -channels_used % 16), (0, 0))
    readout = jnp.pad(readout_weight, spare)
    truth = jnp.pad(target, spare)
    channels = readout.shape[0]
    index = tile_neighbor_index.reshape(-1)
    owner, offset = index // nodes, index % nodes
    tags = jnp.concatenate([owner, offset]).astype(F32).reshape(-1, width)
    position = ((owner ^ shard) * nodes + offset)[:, None]
    *saved, packed = forward(
        position, grid_rows, queries, readout, latents, (w_key, w_value, w_mix), members
    )
    keyset, valueset, soft, attended, normed, inverse = saved
    packed = lax.all_to_all(packed, "ens", split_axis=0, concat_axis=0, tiled=True)
    late = attended
    if pair > 1:
        partner = swap(attended, "ens", 1)
        late = jnp.concatenate([attended, partner])
    early = gather_slots(early, "space")
    late = gather_slots(late, "space")
    packed, early, late = lax.optimization_barrier((packed, early, late))
    saved = (queries, keyset, valueset, soft, normed, inverse)
    blocks = backward(
        member[None], packed, truth, tags, saved, readout, w_mix, shards, count, channels_used
    )
    blocks = lax.all_to_all(
        blocks,
        ("ens", "space"),
        split_axis=0,
        concat_axis=0,
        axis_index_groups=groups,
        tiled=True,
    )
    place = jnp.stack([shard, half])
    blocks, loss = gradients(place, blocks, latents, early, late, members, pair, channels)
    blocks = lax.all_to_all(
        blocks, "ens", split_axis=0, concat_axis=0, axis_index_groups=lines, tiled=True
    )
    grad_out, *grads = sum_groups(half[None], blocks, pair, channels_used)
    if pair > 1:
        *keeps, other = grads
        grads = join_columns(half[None], swap(other, "ens", 1), keeps)
    return (loss.reshape(()), grad_out, *grads)


def solution(mesh):
    in_specs = (
        P("ens", "space", None),
        P("ens", "space", None),
        P("space", None),
        P(None, "space"),
        P(),
        P(),
        P(),
        P(),
        P(),
    )
    out_specs = (
        P(),
        P(),
        P("ens", "space"),
        P("ens", "space"),
        P("ens", "space"),
        P("ens", "space"),
    )

    return jax.shard_map(body, mesh=mesh, in_specs=in_specs, out_specs=out_specs, check_vma=False)
```

```python
import functools

import jax
import jax.numpy as jnp
from jax import lax
from jax.experimental import pallas as pl
from jax.experimental.pallas import tpu as pltpu
from jax.sharding import PartitionSpec as P


HEADS = 16
EPS = 1e-06
SMOOTH = 0.01
LANES = 128
MISC = 8
BF16, F32 = jnp.bfloat16, jnp.float32
VMEM = pl.BlockSpec(memory_space=pltpu.VMEM)
SMEM = pl.BlockSpec(memory_space=pltpu.SMEM)
ANY = pl.BlockSpec(memory_space=pl.ANY)


def dot32(left, right, contract=(1, 0)):
    dims = (((contract[0],), (contract[1],)), ((), ()))
    return lax.dot_general(left, right, dims, preferred_element_type=F32)


def swap(value, axis, bits):
    size = lax.axis_size(axis)
    return lax.ppermute(value, axis, [(i, i ^ bits) for i in range(size)])


def gather_slots(value, axis):
    parts = [value]
    for k in range(1, lax.axis_size(axis)):
        parts.append(swap(parts[k - 1], axis, 1) if k % 2 else swap(value, axis, k))
    return parts


def halves(pair):
    lane = lax.broadcasted_iota(jnp.int32, pair.shape, 1)
    zero = jnp.zeros_like(pair)
    first = lane < pair.shape[1] // 2
    return jnp.concatenate([jnp.where(first, pair, zero), jnp.where(first, zero, pair)], axis=0)


def joined(blocks):
    rows = blocks.shape[0] // 2
    lane = lax.broadcasted_iota(jnp.int32, (rows, blocks.shape[1]), 1)
    return jnp.where(lane < blocks.shape[1] // 2, blocks[:rows], blocks[rows:])


def query_kernel(latent_ref, rows_ref, w_hbm, out_ref, both_ref, w_ref, sem):
    chunks = w_ref.shape[0]
    step = w_ref.shape[2]
    copies = [
        pltpu.make_async_copy(w_hbm.at[:, pl.ds(c * step, step)], w_ref.at[c], sem.at[c])
        for c in range(chunks)
    ]
    for copy in copies:
        copy.start()
    nodes = latent_ref.shape[0]
    both_ref[:nodes] = latent_ref[...]
    both_ref[nodes:] = rows_ref[...]
    for c, copy in enumerate(copies):
        copy.wait()
        out_ref[:, c * step : (c + 1) * step] = dot32(rows_ref[...], w_ref[c]).astype(BF16)


def project_queries(latent, rows, weight):
    features = weight.shape[0]
    step = min(256, features)
    return pl.pallas_call(
        query_kernel,
        out_shape=(
            jax.ShapeDtypeStruct(rows.shape, BF16),
            jax.ShapeDtypeStruct((latent.shape[0] + rows.shape[0], features), BF16),
        ),
        in_specs=[VMEM, VMEM, ANY],
        out_specs=(VMEM, VMEM),
        scratch_shapes=[
            pltpu.VMEM((features // step, features, step), BF16),
            pltpu.SemaphoreType.DMA((features // step,)),
        ],
        cost_estimate=pl.CostEstimate(
            flops=2 * rows.size * features, bytes_accessed=2 * weight.size, transcendentals=0
        ),
        name="project_queries",
    )(latent, rows, weight)


def forward_kernel(shards, members, *refs):
    shard_ref, index_ref, grid_ref, query_ref, readout_ref = refs[:5]
    latent_refs = refs[5 : 5 + shards]
    weights_hbm = refs[5 + shards : 8 + shards]
    (
        key_ref,
        value_ref,
        soft_ref,
        attended_ref,
        normed_ref,
        inverse_ref,
        packed_ref,
        *w_refs,
        sem,
    ) = refs[8 + shards :]
    copies = [pltpu.make_async_copy(s, d, sem.at[i]) for i, (s, d) in enumerate(zip(weights_hbm, w_refs))]
    for copy in copies:
        copy.start()
    points, features = grid_ref.shape
    latents = jnp.concatenate([ref[...] for ref in latent_refs], axis=0)
    each = latent_refs[0].shape[0]
    index = index_ref[...]
    position = ((index // each) ^ shard_ref[0]) * each + index % each
    node = lax.broadcasted_iota(jnp.int32, (latents.shape[0], points), 0)
    chosen = jnp.where(node == position, 1.0, 0.0).astype(BF16)
    nodes = dot32(chosen, latents, (0, 0)).astype(BF16)
    copies[0].wait()
    key_ref[...] = dot32(nodes, w_refs[0][...]).astype(BF16)
    copies[1].wait()
    value_ref[...] = dot32(nodes, w_refs[1][...]).astype(BF16)
    factor = (features // HEADS) ** (-0.5)
    for pair in range(features // LANES):
        at = slice(pair * LANES, (pair + 1) * LANES)
        scores = dot32(query_ref[:, at], halves(key_ref[:, at]), (1, 1)) * factor
        soft = []
        for head in range(2):
            block = scores[:, head * LANES : (head + 1) * LANES]
            raised = jnp.exp(block - jnp.max(block, axis=-1, keepdims=True))
            soft.append(raised / jnp.sum(raised, axis=-1, keepdims=True))
        soft = jnp.concatenate(soft, axis=1)
        soft_ref[pair] = soft
        attended_ref[:, at] = dot32(soft.astype(BF16), halves(value_ref[:, at])).astype(BF16)
    copies[2].wait()
    hidden = grid_ref[...].astype(F32) + dot32(attended_ref[...], w_refs[2][...])
    inverse = lax.rsqrt(jnp.mean(hidden * hidden, axis=-1, keepdims=True) + EPS)
    normed = hidden * inverse
    normed_ref[...] = normed
    inverse_ref[...] = inverse
    normed_b = normed.astype(BF16)
    forecast = dot32(readout_ref[...], normed_b, (1, 1))
    high = forecast.astype(BF16)
    low = (forecast - high.astype(F32)).astype(BF16)
    depth = features // members
    pieces = LANES // depth
    part = points // pieces
    channels = (packed_ref.shape[1] - part) // 2
    spare = jnp.zeros((channels - readout_ref.shape[0], points), BF16)
    fields = jnp.concatenate([high, spare, low, spare], axis=0)
    for m in range(members):
        packed_ref[m, : 2 * channels] = fields
        for p in range(pieces):
            packed_ref[m, 2 * channels :, p * depth : (p + 1) * depth] = normed_b[
                p * part : (p + 1) * part, m * depth : (m + 1) * depth
            ]


def padded(channels):
    return channels + -channels % 16


def forward(shard, index, grid_rows, queries, readout, latents, weights, members):
    points, features = grid_rows.shape
    channels = padded(readout.shape[0])
    depth = features // members
    rows = 2 * channels + points * depth // LANES
    shape = jax.ShapeDtypeStruct
    return pl.pallas_call(
        functools.partial(forward_kernel, len(latents), members),
        out_shape=(
            shape((points, features), BF16),
            shape((points, features), BF16),
            shape((features // LANES, points, 2 * LANES), F32),
            shape((points, features), BF16),
            shape((points, features), F32),
            shape((points, 1), F32),
            shape((members, rows, LANES), BF16),
        ),
        in_specs=[SMEM] + [VMEM] * (4 + len(latents)) + [ANY] * 3,
        out_specs=(VMEM,) * 7,
        scratch_shapes=[pltpu.VMEM((features, features), BF16)] * 3
        + [pltpu.SemaphoreType.DMA((3,))],
        cost_estimate=pl.CostEstimate(
            flops=8 * points * features * features,
            bytes_accessed=6 * features * features,
            transcendentals=points * LANES * HEADS,
        ),
        name="decoder_forward",
    )(shard, index, grid_rows, queries, readout, *latents, *weights)


def backward_kernel(
    shards,
    blocks,
    nodes,
    member_ref,
    packed_ref,
    target_ref,
    index_ref,
    query_ref,
    key_ref,
    value_ref,
    soft_ref,
    normed_ref,
    inverse_ref,
    readout_ref,
    w_hbm,
    out_ref,
    w_ref,
    slope_ref,
    d_attended_ref,
    small_ref,
    truth_ref,
    weight_ref,
    sem,
):
    copy = pltpu.make_async_copy(w_hbm, w_ref, sem)
    copy.start()
    members = packed_ref.shape[0]
    points, features = normed_ref.shape
    channels_used = readout_ref.shape[0]
    channels = truth_ref.shape[0]
    for full, used in ((truth_ref, target_ref), (weight_ref, readout_ref)):
        full[:channels_used] = used[...]
        spare = (channels - channels_used, used.shape[1])
        full[channels_used:] = jnp.zeros(spare, used.dtype)
    width, depth = features // blocks, features // members
    weight = (channels_used * points * shards) ** (-0.5)
    pair_weight = 1.0 / (members * (members - 1))
    chunk = 16

    def crps(c, loss):
        at = pl.ds(pl.multiple_of(c * chunk, chunk), chunk)
        low_at = pl.ds(pl.multiple_of(c * chunk + channels, chunk), chunk)
        fields = [
            packed_ref[m, at].astype(F32) + packed_ref[m, low_at].astype(F32)
            for m in range(members)
        ]
        truth = truth_ref[at]
        skill = jnp.zeros_like(truth)
        slopes = []
        for m in range(members):
            apart = fields[m] - truth
            square = apart * apart + SMOOTH
            root = lax.rsqrt(square)
            skill = skill + square * root
            slopes.append(apart * root * (weight / members))
        spread = jnp.zeros_like(truth)
        for m in range(members):
            for k in range(m):
                apart = fields[m] - fields[k]
                square = apart * apart + SMOOTH
                root = lax.rsqrt(square)
                spread = spread + square * root
                ratio = apart * root * (weight * pair_weight)
                slopes[m] = slopes[m] - ratio
                slopes[k] = slopes[k] + ratio
        for m in range(members):
            slope_ref[m, at] = slopes[m].astype(BF16)
        channel = c * chunk + lax.broadcasted_iota(jnp.int32, truth.shape, 0)
        term = skill * (1.0 / members) - spread * pair_weight
        return loss + jnp.where(channel < channels_used, term, 0.0)

    loss = lax.fori_loop(0, channels // chunk, crps, jnp.zeros((chunk, points), F32))
    loss = weight * jnp.sum(jnp.sum(loss, axis=0, keepdims=True), axis=1, keepdims=True)

    pieces = LANES // depth
    part = points // pieces
    total = jnp.zeros((channels, depth), F32)
    for m in range(members):
        tail = packed_ref[m, 2 * channels :]
        for p in range(pieces):
            total = total + dot32(
                slope_ref[m][:, p * part : (p + 1) * part], tail[:, p * depth : (p + 1) * depth]
            )
    rows = channels * depth // width
    for p in range(width // depth):
        small_ref[:rows, p * depth : (p + 1) * depth] = total[p * rows : (p + 1) * rows]
    first = loss.astype(BF16).astype(F32)
    second = (loss - first).astype(BF16).astype(F32)
    for i, value in enumerate((first, second, loss - first - second)):
        small_ref[rows + i : rows + i + 1] = jnp.broadcast_to(value, (1, width))
    spare = small_ref.shape[0] - rows - 3
    small_ref[rows + 3 :] = jnp.zeros((spare, width), F32)
    index = index_ref[...]
    line = rows + 3
    for tag in (index // nodes, index % nodes):
        step = min(points, width)
        for c in range(0, points, step):
            small_ref[line : line + 1, :step] = tag[:, c : c + step].astype(F32)
            line = line + 1
    small = small_ref[...].astype(BF16)
    for b in range(blocks):
        out_ref[b, 4 * points :] = small

    def put(kind, column, value):
        step = min(width, value.shape[1])
        for c in range(0, value.shape[1], step):
            block, lane = divmod(column + c, width)
            out_ref[block, kind * points : (kind + 1) * points, lane : lane + step] = value[
                :, c : c + step
            ]

    own = slope_ref[member_ref[0]]
    normed = normed_ref[...]
    d_normed = dot32(own, weight_ref[...], (0, 0))
    mean = jnp.mean(d_normed * normed, axis=-1, keepdims=True)
    d_hidden = (inverse_ref[...] * (d_normed - normed * mean)).astype(BF16)
    put(3, 0, d_hidden)
    copy.wait()
    d_attended_ref[...] = dot32(d_hidden, w_ref[...], (1, 1)).astype(BF16)
    factor = (features // HEADS) ** (-0.5)
    for pair in range(features // LANES):
        at = slice(pair * LANES, (pair + 1) * LANES)
        soft = soft_ref[pair]
        d_out = d_attended_ref[:, at]
        d_probs = dot32(d_out, halves(value_ref[:, at]), (1, 1))
        put(2, pair * LANES, joined(dot32(soft.astype(BF16), d_out, (0, 0))).astype(BF16))
        product = d_probs * soft
        d_scores = []
        for head in range(2):
            block = slice(head * LANES, (head + 1) * LANES)
            summed = jnp.sum(product[:, block], axis=-1, keepdims=True)
            d_scores.append(soft[:, block] * (d_probs[:, block] - summed) * factor)
        d_scores = jnp.concatenate(d_scores, axis=1).astype(BF16)
        put(0, pair * LANES, dot32(d_scores, halves(key_ref[:, at])).astype(BF16))
        put(1, pair * LANES, joined(dot32(d_scores, query_ref[:, at], (0, 0))).astype(BF16))


def small_rows(channels, depth, width):
    rows = channels * depth // width + MISC
    return rows + -rows % 16


def backward(member, packed, target, index, saved, readout, w_mix, shards, blocks, nodes):
    members = packed.shape[0]
    features = w_mix.shape[0]
    points = saved[0].shape[0]
    channels = padded(readout.shape[0])
    width, depth = features // blocks, features // members
    small = small_rows(channels, depth, width)
    return pl.pallas_call(
        functools.partial(backward_kernel, shards, blocks, nodes),
        out_shape=jax.ShapeDtypeStruct((blocks, 4 * points + small, width), BF16),
        in_specs=[SMEM] + [VMEM] * 10 + [ANY],
        out_specs=VMEM,
        scratch_shapes=[
            pltpu.VMEM((features, features), BF16),
            pltpu.VMEM((members, channels, points), BF16),
            pltpu.VMEM((points, features), BF16),
            pltpu.VMEM((small, width), F32),
            pltpu.VMEM((channels, points), F32),
            pltpu.VMEM((channels, features), BF16),
            pltpu.SemaphoreType.DMA,
        ],
        cost_estimate=pl.CostEstimate(
            flops=4 * points * features * features,
            bytes_accessed=4 * features * features,
            transcendentals=0,
        ),
        name="decoder_backward",
    )(member, packed, target, index, *saved, readout, w_mix)


def gradient_kernel(shards, pair, members, nodes, channels, place_ref, blocks_ref, *refs):
    latent_refs, early_refs, late_refs = (refs[i * shards : (i + 1) * shards] for i in range(3))
    out_ref, loss_ref = refs[3 * shards :]
    width = blocks_ref.shape[2]
    features = late_refs[0].shape[1]
    points = late_refs[0].shape[0] // pair
    depth = features // members
    shard, half = place_ref[0], place_ref[1]
    rows = channels * depth // width
    start = 4 * points
    parts = []
    for t in range(pair):
        total = jnp.zeros((blocks_ref.shape[1] - start, width), F32)
        for s in range(shards):
            total = total + blocks_ref[s * pair + t, start:].astype(F32)
        if t == 0:
            loss = jnp.sum(total[rows : rows + 3, :1], axis=0, keepdims=True)
        parts.append(total[:rows])
    loss_ref[...] = loss
    small = parts[0]
    if pair > 1:
        small = jnp.where(half == 0, parts[0], parts[1])
    small = small.astype(BF16)
    for m in range(members):
        out_ref[m, 4 * width :] = small

    def slots(kind, t):
        at = slice(kind * points, (kind + 1) * points)
        return [blocks_ref[(shard ^ k) * pair + (half ^ t), at] for k in range(shards)]

    def put(kind, total):
        total = total.astype(BF16)
        at = slice(kind * width, kind * width + total.shape[0])
        for m in range(members):
            out_ref[m, at] = total[:, m * depth : (m + 1) * depth]

    def rows_of(ref_list, part):
        at = slice(part * points, (part + 1) * points)
        return [ref[at] for ref in ref_list]

    def product(kind, parts):
        left = jnp.concatenate([v for t in range(pair) for v in slots(kind, t)], axis=0)
        right = jnp.concatenate([v for part in parts for v in part], axis=0)
        put(kind, dot32(left, right, (0, 0)))

    product(3, [rows_of(late_refs, t) for t in range(pair)])
    chosen = []
    for k in range(shards):
        index = blocks_ref[(shard ^ k) * pair, start + rows : start + rows + MISC].astype(jnp.int32)
        lines = max(points // width, 1)
        owner, offset = (
            jnp.concatenate([index[3 + b + i : 4 + b + i] for i in range(lines)], axis=1)
            for b in (0, lines)
        )
        position = (owner ^ shard) * nodes + offset
        node = lax.broadcasted_iota(jnp.int32, (nodes * shards, points), 0)
        chosen.append(jnp.where(node == position, 1.0, 0.0).astype(BF16))
    chosen = jnp.concatenate(chosen, axis=1)
    sums = []
    for t in range(pair):
        both = [jnp.concatenate(slots(kind, t), axis=0) for kind in (1, 2)]
        sums.append(dot32(chosen, jnp.concatenate(both, axis=1)).astype(BF16))
    others = [[ref[...] for ref in latent_refs]]
    if pair > 1:
        others.append([ref[points : points + nodes] for ref in early_refs])
    put(
        1,
        dot32(
            jnp.concatenate(sums, axis=0),
            jnp.concatenate([v for part in others for v in part], axis=0),
            (0, 0),
        ),
    )
    grids = [rows_of(early_refs, 0)]
    if pair > 1:
        grids.append([ref[points + nodes :] for ref in early_refs])
    product(0, grids)


def gradients(place, blocks, latents, early, late, members, pair, channels):
    count, _, width = blocks.shape
    shards = count // pair
    features = late[0].shape[1]
    points = late[0].shape[0] // pair
    depth = features // members
    rows = 4 * width + channels
    return pl.pallas_call(
        functools.partial(
            gradient_kernel, shards, pair, members, latents[0].shape[0], channels
        ),
        out_shape=(
            jax.ShapeDtypeStruct((members, rows, depth), BF16),
            jax.ShapeDtypeStruct((1, 1), F32),
        ),
        in_specs=[SMEM] + [VMEM] * (1 + 3 * shards),
        out_specs=(VMEM, VMEM),
        cost_estimate=pl.CostEstimate(
            flops=8 * points * count * features * width,
            bytes_accessed=8 * points * count * features,
            transcendentals=0,
        ),
        name="weight_gradients",
    )(place, blocks, *latents, *early, *late)


def sum_kernel(pair, blocks_ref, out_ref, *refs):
    members, _, depth = blocks_ref.shape
    used = out_ref.shape[0]
    width = refs[0].shape[1] // pair
    for m in range(members):
        out_ref[:, m * depth : (m + 1) * depth] = blocks_ref[m, 4 * width : 4 * width + used].astype(F32)
    for i in range(4):
        at = slice(i * width, (i + 1) * width)
        for y in range(pair):
            total = blocks_ref[y, at].astype(F32)
            for m in range(y + pair, members, pair):
                total = total + blocks_ref[m, at].astype(F32)
            refs[i][:, y * width : (y + 1) * width] = total.T


def sum_groups(blocks, pair, channels_used):
    members, rows, depth = blocks.shape
    width = (rows - padded(channels_used)) // 4
    shape = jax.ShapeDtypeStruct
    return pl.pallas_call(
        functools.partial(sum_kernel, pair),
        out_shape=(shape((channels_used, depth * members), F32),)
        + (shape((depth, pair * width), F32),) * 4,
        in_specs=[VMEM],
        out_specs=(VMEM,) * 5,
        name="sum_groups",
    )(blocks)


def body(
    grid_hidden, latent, tile_neighbor_index, target, w_query, w_key, w_value, w_mix, readout_weight
):
    nodes, _ = latent.shape[1:]
    channels_used = target.shape[0]
    shards, members = lax.axis_size("space"), lax.axis_size("ens")
    shard, member = lax.axis_index("space"), lax.axis_index("ens")
    pair = 2 if members % 2 == 0 and shards <= 8 else 1
    half = member % pair
    count = shards * pair
    groups = [
        [(g + y) * shards + s for s in range(shards) for y in range(pair)]
        for g in range(0, members, pair)
    ]

    own_latent, grid_rows = latent[0], grid_hidden[0]
    latents = gather_slots(own_latent, "space")
    queries, both = project_queries(own_latent, grid_rows, w_query)
    early = grid_rows
    if pair > 1:
        partner = swap(both, "ens", 1)
        early = jnp.concatenate([grid_rows, partner])
    *saved, packed = forward(
        shard[None],
        tile_neighbor_index,
        grid_rows,
        queries,
        readout_weight,
        latents,
        (w_key, w_value, w_mix),
        members,
    )
    keyset, valueset, soft, attended, normed, inverse = saved
    packed = lax.all_to_all(packed, "ens", split_axis=0, concat_axis=0, tiled=True)
    late = attended
    if pair > 1:
        partner = swap(attended, "ens", 1)
        late = jnp.concatenate([attended, partner])
    early = gather_slots(early, "space")
    late = gather_slots(late, "space")
    saved = (queries, keyset, valueset, soft, normed, inverse)
    blocks = backward(
        member[None],
        packed,
        target,
        tile_neighbor_index,
        saved,
        readout_weight,
        w_mix,
        shards,
        count,
        nodes,
    )
    blocks = lax.all_to_all(
        blocks,
        ("ens", "space"),
        split_axis=0,
        concat_axis=0,
        axis_index_groups=groups,
        tiled=True,
    )
    place = jnp.stack([shard, half])
    channels = padded(channels_used)
    blocks, loss = gradients(place, blocks, latents, early, late, members, pair, channels)
    blocks = lax.all_to_all(blocks, "ens", split_axis=0, concat_axis=0, tiled=True)
    grad_out, *grads = sum_groups(blocks, pair, channels_used)
    return (loss.reshape(()), grad_out, *grads)


def solution(mesh):
    in_specs = (
        P("ens", "space", None),
        P("ens", "space", None),
        P("space", None),
        P(None, "space"),
        P(),
        P(),
        P(),
        P(),
        P(),
    )
    out_specs = (
        P(),
        P(),
        P("ens", "space"),
        P("ens", "space"),
        P("ens", "space"),
        P("ens", "space"),
    )

    return jax.shard_map(body, mesh=mesh, in_specs=in_specs, out_specs=out_specs, check_vma=False)
```

```python
import functools

import jax
import jax.numpy as jnp
from jax import lax
from jax.experimental import pallas as pl
from jax.experimental.pallas import tpu as pltpu
from jax.sharding import PartitionSpec as P


HEADS = 16
EPS = 1e-06
SMOOTH = 0.01
LANES = 128
MISC = 8
BF16, F32 = jnp.bfloat16, jnp.float32
VMEM = pl.BlockSpec(memory_space=pltpu.VMEM)
SMEM = pl.BlockSpec(memory_space=pltpu.SMEM)
ANY = pl.BlockSpec(memory_space=pl.ANY)


def dot32(left, right, contract=(1, 0)):
    dims = (((contract[0],), (contract[1],)), ((), ()))
    return lax.dot_general(left, right, dims, preferred_element_type=F32)


def swap(value, axis, bits):
    size = lax.axis_size(axis)
    return lax.ppermute(value, axis, [(i, i ^ bits) for i in range(size)])


def gather_slots(value, axis):
    parts = [value]
    for k in range(1, lax.axis_size(axis)):
        parts.append(swap(parts[k - 1], axis, 1) if k % 2 else swap(value, axis, k))
    return parts


def halves(pair):
    lane = lax.broadcasted_iota(jnp.int32, pair.shape, 1)
    zero = jnp.zeros_like(pair)
    first = lane < pair.shape[1] // 2
    return jnp.concatenate([jnp.where(first, pair, zero), jnp.where(first, zero, pair)], axis=0)


def joined(blocks):
    rows = blocks.shape[0] // 2
    lane = lax.broadcasted_iota(jnp.int32, (rows, blocks.shape[1]), 1)
    return jnp.where(lane < blocks.shape[1] // 2, blocks[:rows], blocks[rows:])


def query_kernel(latent_ref, rows_ref, w_hbm, out_ref, both_ref, w_ref, sem):
    chunks = w_ref.shape[0]
    step = w_ref.shape[2]
    copies = [
        pltpu.make_async_copy(w_hbm.at[:, pl.ds(c * step, step)], w_ref.at[c], sem.at[c])
        for c in range(chunks)
    ]
    for copy in copies:
        copy.start()
    nodes = latent_ref.shape[0]
    both_ref[:nodes] = latent_ref[...]
    both_ref[nodes:] = rows_ref[...]
    for c, copy in enumerate(copies):
        copy.wait()
        out_ref[:, c * step : (c + 1) * step] = dot32(rows_ref[...], w_ref[c]).astype(BF16)


def project_queries(latent, rows, weight):
    features = weight.shape[0]
    step = min(256, features)
    return pl.pallas_call(
        query_kernel,
        out_shape=(
            jax.ShapeDtypeStruct(rows.shape, BF16),
            jax.ShapeDtypeStruct((latent.shape[0] + rows.shape[0], features), BF16),
        ),
        in_specs=[VMEM, VMEM, ANY],
        out_specs=(VMEM, VMEM),
        scratch_shapes=[
            pltpu.VMEM((features // step, features, step), BF16),
            pltpu.SemaphoreType.DMA((features // step,)),
        ],
        cost_estimate=pl.CostEstimate(
            flops=2 * rows.size * features, bytes_accessed=2 * weight.size, transcendentals=0
        ),
        name="project_queries",
    )(latent, rows, weight)


def forward_kernel(shards, members, *refs):
    shard_ref, index_ref, grid_ref, query_ref, readout_ref = refs[:5]
    latent_refs = refs[5 : 5 + shards]
    weights_hbm = refs[5 + shards : 8 + shards]
    (
        key_ref,
        value_ref,
        soft_ref,
        attended_ref,
        normed_ref,
        inverse_ref,
        packed_ref,
        *w_refs,
        sem,
    ) = refs[8 + shards :]
    copies = [pltpu.make_async_copy(s, d, sem.at[i]) for i, (s, d) in enumerate(zip(weights_hbm, w_refs))]
    for copy in copies:
        copy.start()
    points, features = grid_ref.shape
    latents = jnp.concatenate([ref[...] for ref in latent_refs], axis=0)
    each = latent_refs[0].shape[0]
    index = index_ref[...]
    position = ((index // each) ^ shard_ref[0]) * each + index % each
    node = lax.broadcasted_iota(jnp.int32, (latents.shape[0], points), 0)
    chosen = jnp.where(node == position, 1.0, 0.0).astype(BF16)
    nodes = dot32(chosen, latents, (0, 0)).astype(BF16)
    copies[0].wait()
    key_ref[...] = dot32(nodes, w_refs[0][...]).astype(BF16)
    copies[1].wait()
    value_ref[...] = dot32(nodes, w_refs[1][...]).astype(BF16)
    factor = (features // HEADS) ** (-0.5)
    for pair in range(features // LANES):
        at = slice(pair * LANES, (pair + 1) * LANES)
        scores = dot32(query_ref[:, at], halves(key_ref[:, at]), (1, 1)) * factor
        soft = []
        for head in range(2):
            block = scores[:, head * LANES : (head + 1) * LANES]
            raised = jnp.exp(block - jnp.max(block, axis=-1, keepdims=True))
            soft.append(raised / jnp.sum(raised, axis=-1, keepdims=True))
        soft = jnp.concatenate(soft, axis=1)
        soft_ref[pair] = soft
        attended_ref[:, at] = dot32(soft.astype(BF16), halves(value_ref[:, at])).astype(BF16)
    copies[2].wait()
    hidden = grid_ref[...].astype(F32) + dot32(attended_ref[...], w_refs[2][...])
    inverse = lax.rsqrt(jnp.mean(hidden * hidden, axis=-1, keepdims=True) + EPS)
    normed = hidden * inverse
    normed_ref[...] = normed
    inverse_ref[...] = inverse
    normed_b = normed.astype(BF16)
    forecast = dot32(readout_ref[...], normed_b, (1, 1))
    high = forecast.astype(BF16)
    low = (forecast - high.astype(F32)).astype(BF16)
    channels = packed_ref.shape[1] // 2
    spare = jnp.zeros((channels - readout_ref.shape[0], points), BF16)
    fields = jnp.concatenate([high, spare, low, spare], axis=0)
    for m in range(members):
        packed_ref[m] = fields


def padded(channels):
    return channels + -channels % 16


def forward(shard, index, grid_rows, queries, readout, latents, weights, members):
    points, features = grid_rows.shape
    channels = padded(readout.shape[0])
    shape = jax.ShapeDtypeStruct
    return pl.pallas_call(
        functools.partial(forward_kernel, len(latents), members),
        out_shape=(
            shape((points, features), BF16),
            shape((points, features), BF16),
            shape((features // LANES, points, 2 * LANES), F32),
            shape((points, features), BF16),
            shape((points, features), F32),
            shape((points, 1), F32),
            shape((members, 2 * channels, points), BF16),
        ),
        in_specs=[SMEM] + [VMEM] * (4 + len(latents)) + [ANY] * 3,
        out_specs=(VMEM,) * 7,
        scratch_shapes=[pltpu.VMEM((features, features), BF16)] * 3
        + [pltpu.SemaphoreType.DMA((3,))],
        cost_estimate=pl.CostEstimate(
            flops=8 * points * features * features,
            bytes_accessed=6 * features * features,
            transcendentals=points * LANES * HEADS,
        ),
        name="decoder_forward",
    )(shard, index, grid_rows, queries, readout, *latents, *weights)


def backward_kernel(
    shards,
    blocks,
    nodes,
    place_ref,
    packed_ref,
    target_ref,
    index_ref,
    query_ref,
    key_ref,
    value_ref,
    soft_ref,
    normed_ref,
    inverse_ref,
    readout_ref,
    w_hbm,
    out_ref,
    outer_ref,
    w_ref,
    slope_ref,
    d_attended_ref,
    small_ref,
    truth_ref,
    weight_ref,
    sem,
):
    copy = pltpu.make_async_copy(w_hbm, w_ref, sem)
    copy.start()
    members = packed_ref.shape[0]
    points, features = normed_ref.shape
    channels_used = readout_ref.shape[0]
    channels = truth_ref.shape[0]
    for full, used in ((truth_ref, target_ref), (weight_ref, readout_ref)):
        full[:channels_used] = used[...]
        spare = (channels - channels_used, used.shape[1])
        full[channels_used:] = jnp.zeros(spare, used.dtype)
    width = features // blocks
    weight = (channels_used * points * shards) ** (-0.5)
    pair_weight = 1.0 / (members * (members - 1))
    chunk = 16

    def crps(c, loss):
        at = pl.ds(pl.multiple_of(c * chunk, chunk), chunk)
        low_at = pl.ds(pl.multiple_of(c * chunk + channels, chunk), chunk)
        fields = [
            packed_ref[m, at].astype(F32) + packed_ref[m, low_at].astype(F32)
            for m in range(members)
        ]
        truth = truth_ref[at]
        skill = jnp.zeros_like(truth)
        slopes = []
        for m in range(members):
            apart = fields[m] - truth
            square = apart * apart + SMOOTH
            root = lax.rsqrt(square)
            skill = skill + square * root
            slopes.append(apart * root * (weight / members))
        spread = jnp.zeros_like(truth)
        for m in range(members):
            for k in range(m):
                apart = fields[m] - fields[k]
                square = apart * apart + SMOOTH
                root = lax.rsqrt(square)
                spread = spread + square * root
                ratio = apart * root * (weight * pair_weight)
                slopes[m] = slopes[m] - ratio
                slopes[k] = slopes[k] + ratio
        for m in range(members):
            slope_ref[m, at] = slopes[m].astype(BF16)
        channel = c * chunk + lax.broadcasted_iota(jnp.int32, truth.shape, 0)
        term = skill * (1.0 / members) - spread * pair_weight
        return loss + jnp.where(channel < channels_used, term, 0.0)

    loss = lax.fori_loop(0, channels // chunk, crps, jnp.zeros((chunk, points), F32))
    loss = weight * jnp.sum(jnp.sum(loss, axis=0, keepdims=True), axis=1, keepdims=True)

    first = loss.astype(BF16).astype(F32)
    second = (loss - first).astype(BF16).astype(F32)
    for i, value in enumerate((first, second, loss - first - second)):
        small_ref[i : i + 1] = jnp.broadcast_to(value, (1, width))
    small_ref[3:] = jnp.zeros((small_ref.shape[0] - 3, width), F32)
    index = index_ref[...]
    line = 3
    for tag in (index // nodes, index % nodes):
        step = min(points, width)
        for c in range(0, points, step):
            small_ref[line : line + 1, :step] = tag[:, c : c + step].astype(F32)
            line = line + 1
    small = small_ref[...].astype(BF16)
    for b in range(blocks):
        out_ref[b, 4 * points :] = small

    def put(kind, column, value):
        step = min(width, value.shape[1])
        for c in range(0, value.shape[1], step):
            block, lane = divmod(column + c, width)
            out_ref[block, kind * points : (kind + 1) * points, lane : lane + step] = value[
                :, c : c + step
            ]

    own = slope_ref[place_ref[1]]
    normed = normed_ref[...]
    outer = dot32(own, normed.astype(BF16))
    columns = features // shards
    parts = [outer[:, s * columns : (s + 1) * columns] for s in range(shards)]
    for k in range(shards):
        part = parts[0]
        for s in range(1, shards):
            part = jnp.where((place_ref[0] ^ k) == s, parts[s], part)
        outer_ref[k] = part.astype(BF16)
    d_normed = dot32(own, weight_ref[...], (0, 0))
    mean = jnp.mean(d_normed * normed, axis=-1, keepdims=True)
    d_hidden = (inverse_ref[...] * (d_normed - normed * mean)).astype(BF16)
    put(3, 0, d_hidden)
    copy.wait()
    d_attended_ref[...] = dot32(d_hidden, w_ref[...], (1, 1)).astype(BF16)
    factor = (features // HEADS) ** (-0.5)
    for pair in range(features // LANES):
        at = slice(pair * LANES, (pair + 1) * LANES)
        soft = soft_ref[pair]
        d_out = d_attended_ref[:, at]
        d_probs = dot32(d_out, halves(value_ref[:, at]), (1, 1))
        put(2, pair * LANES, joined(dot32(soft.astype(BF16), d_out, (0, 0))).astype(BF16))
        product = d_probs * soft
        d_scores = []
        for head in range(2):
            block = slice(head * LANES, (head + 1) * LANES)
            summed = jnp.sum(product[:, block], axis=-1, keepdims=True)
            d_scores.append(soft[:, block] * (d_probs[:, block] - summed) * factor)
        d_scores = jnp.concatenate(d_scores, axis=1).astype(BF16)
        put(0, pair * LANES, dot32(d_scores, halves(key_ref[:, at])).astype(BF16))
        put(1, pair * LANES, joined(dot32(d_scores, query_ref[:, at], (0, 0))).astype(BF16))


def backward(place, packed, target, index, saved, readout, w_mix, shards, blocks, nodes):
    members = packed.shape[0]
    features = w_mix.shape[0]
    points = saved[0].shape[0]
    channels = padded(readout.shape[0])
    width = features // blocks
    small = 16
    return pl.pallas_call(
        functools.partial(backward_kernel, shards, blocks, nodes),
        out_shape=(
            jax.ShapeDtypeStruct((blocks, 4 * points + small, width), BF16),
            jax.ShapeDtypeStruct((shards, channels, features // shards), BF16),
        ),
        in_specs=[SMEM] + [VMEM] * 10 + [ANY],
        out_specs=(VMEM, VMEM),
        scratch_shapes=[
            pltpu.VMEM((features, features), BF16),
            pltpu.VMEM((members, channels, points), BF16),
            pltpu.VMEM((points, features), BF16),
            pltpu.VMEM((small, width), F32),
            pltpu.VMEM((channels, points), F32),
            pltpu.VMEM((channels, features), BF16),
            pltpu.SemaphoreType.DMA,
        ],
        cost_estimate=pl.CostEstimate(
            flops=4 * points * features * features,
            bytes_accessed=4 * features * features,
            transcendentals=0,
        ),
        name="decoder_backward",
    )(place, packed, target, index, *saved, readout, w_mix)


def gradient_kernel(shards, pair, members, nodes, place_ref, blocks_ref, *refs):
    latent_refs, early_refs, late_refs, grid_refs = (
        refs[i * shards : (i + 1) * shards] for i in range(4)
    )
    out_ref, loss_ref = refs[4 * shards :]
    width = blocks_ref.shape[2]
    features = late_refs[0].shape[1]
    points = late_refs[0].shape[0] // pair
    depth = features // members
    shard, half = place_ref[0], place_ref[1]
    start = 4 * points
    total = blocks_ref[0, start:].astype(F32)
    for s in range(1, shards):
        total = total + blocks_ref[s * pair, start:].astype(F32)
    loss_ref[...] = jnp.sum(total[:3, :1], axis=0, keepdims=True)

    def slots(kind, t):
        at = slice(kind * points, (kind + 1) * points)
        return [blocks_ref[(shard ^ k) * pair + (half ^ t), at] for k in range(shards)]

    def put(kind, total):
        total = total.astype(BF16)
        at = slice(kind * width, kind * width + total.shape[0])
        for m in range(members):
            out_ref[m, at] = total[:, m * depth : (m + 1) * depth]

    def rows_of(ref_list, part):
        at = slice(part * points, (part + 1) * points)
        return [ref[at] for ref in ref_list]

    def product(kind, parts):
        left = jnp.concatenate([v for t in range(pair) for v in slots(kind, t)], axis=0)
        right = jnp.concatenate([v for part in parts for v in part], axis=0)
        put(kind, dot32(left, right, (0, 0)))

    product(3, [rows_of(late_refs, t) for t in range(pair)])
    chosen = []
    for k in range(shards):
        index = blocks_ref[(shard ^ k) * pair, start : start + MISC].astype(jnp.int32)
        lines = max(points // width, 1)
        owner, offset = (
            jnp.concatenate([index[3 + b + i : 4 + b + i] for i in range(lines)], axis=1)
            for b in (0, lines)
        )
        position = (owner ^ shard) * nodes + offset
        node = lax.broadcasted_iota(jnp.int32, (nodes * shards, points), 0)
        chosen.append(jnp.where(node == position, 1.0, 0.0).astype(BF16))
    chosen = jnp.concatenate(chosen, axis=1)
    sums = []
    for t in range(pair):
        both = [jnp.concatenate(slots(kind, t), axis=0) for kind in (1, 2)]
        sums.append(dot32(chosen, jnp.concatenate(both, axis=1)).astype(BF16))
    others = [[ref[...] for ref in latent_refs]]
    if pair > 1:
        others.append([ref[:nodes] for ref in early_refs])
    put(
        1,
        dot32(
            jnp.concatenate(sums, axis=0),
            jnp.concatenate([v for part in others for v in part], axis=0),
            (0, 0),
        ),
    )
    grids = [[ref[...] for ref in grid_refs]]
    if pair > 1:
        grids.append([ref[nodes:] for ref in early_refs])
    product(0, grids)


def gradients(place, blocks, latents, early, late, grids, members, pair):
    count, _, width = blocks.shape
    shards = count // pair
    features = late[0].shape[1]
    points = late[0].shape[0] // pair
    depth = features // members
    return pl.pallas_call(
        functools.partial(
            gradient_kernel, shards, pair, members, latents[0].shape[0]
        ),
        out_shape=(
            jax.ShapeDtypeStruct((members, 4 * width, depth), BF16),
            jax.ShapeDtypeStruct((1, 1), F32),
        ),
        in_specs=[SMEM] + [VMEM] * (1 + 4 * shards),
        out_specs=(VMEM, VMEM),
        cost_estimate=pl.CostEstimate(
            flops=8 * points * count * features * width,
            bytes_accessed=8 * points * count * features,
            transcendentals=0,
        ),
        name="weight_gradients",
    )(place, blocks, *latents, *early, *late, *grids)


def sum_kernel(pair, blocks_ref, *refs):
    members, rows, _ = blocks_ref.shape
    width = rows // len(refs)
    for i, ref in enumerate(refs):
        at = slice(i * width, (i + 1) * width)
        for y in range(pair):
            total = blocks_ref[y, at].astype(F32)
            for m in range(y + pair, members, pair):
                total = total + blocks_ref[m, at].astype(F32)
            ref[:, y * width : (y + 1) * width] = total.T


def sum_groups(blocks, pair):
    _, rows, depth = blocks.shape
    return pl.pallas_call(
        functools.partial(sum_kernel, pair),
        out_shape=(jax.ShapeDtypeStruct((depth, pair * rows // 4), F32),) * 4,
        in_specs=[VMEM],
        out_specs=(VMEM,) * 4,
        name="sum_groups",
    )(blocks)


def join_kernel(shard_ref, *refs):
    *slot_refs, out_ref = refs
    used, columns = out_ref.shape[0], slot_refs[0].shape[1]
    values = [ref[...].astype(F32) for ref in slot_refs]
    for s in range(len(values)):
        value = values[0]
        for k in range(1, len(values)):
            value = jnp.where((shard_ref[0] ^ k) == s, values[k], value)
        out_ref[:, s * columns : (s + 1) * columns] = value[:used]


def join_columns(shard, parts, channels_used):
    columns = parts[0].shape[1] * len(parts)
    return pl.pallas_call(
        join_kernel,
        out_shape=jax.ShapeDtypeStruct((channels_used, columns), F32),
        in_specs=[SMEM] + [VMEM] * len(parts),
        out_specs=VMEM,
        name="join_columns",
    )(shard, *parts)


def sum_outer(parts):
    total = parts[0].astype(F32)
    received = []
    for k in range(1, parts.shape[0]):
        received.append(swap(parts[k], "space", k))
    for value in received:
        total = total + value.astype(F32)
    total = total.astype(BF16)
    bit = 1
    while bit < lax.axis_size("ens"):
        other = swap(total, "ens", bit)
        total = (total.astype(F32) + other.astype(F32)).astype(BF16)
        bit = 2 * bit
    return gather_slots(total, "space")


def body(
    grid_hidden, latent, tile_neighbor_index, target, w_query, w_key, w_value, w_mix, readout_weight
):
    nodes, _ = latent.shape[1:]
    channels_used = target.shape[0]
    shards, members = lax.axis_size("space"), lax.axis_size("ens")
    shard, member = lax.axis_index("space"), lax.axis_index("ens")
    pair = 2 if members % 2 == 0 and shards <= 8 else 1
    half = member % pair
    count = shards * pair
    groups = [
        [(g + y) * shards + s for s in range(shards) for y in range(pair)]
        for g in range(0, members, pair)
    ]

    own_latent, grid_rows = latent[0], grid_hidden[0]
    latents = gather_slots(own_latent, "space")
    grids = gather_slots(grid_rows, "space")
    queries, both = project_queries(own_latent, grid_rows, w_query)
    early = latents
    if pair > 1:
        early = swap(both, "ens", 1)
        early = gather_slots(early, "space")
    *saved, packed = forward(
        shard[None],
        tile_neighbor_index,
        grid_rows,
        queries,
        readout_weight,
        latents,
        (w_key, w_value, w_mix),
        members,
    )
    keyset, valueset, soft, attended, normed, inverse = saved
    packed = lax.all_to_all(packed, "ens", split_axis=0, concat_axis=0, tiled=True)
    late = attended
    if pair > 1:
        partner = swap(attended, "ens", 1)
        late = jnp.concatenate([attended, partner])
    late = gather_slots(late, "space")
    saved = (queries, keyset, valueset, soft, normed, inverse)
    blocks, outer = backward(
        jnp.stack([shard, member]),
        packed,
        target,
        tile_neighbor_index,
        saved,
        readout_weight,
        w_mix,
        shards,
        count,
        nodes,
    )
    blocks = lax.all_to_all(
        blocks,
        ("ens", "space"),
        split_axis=0,
        concat_axis=0,
        axis_index_groups=groups,
        tiled=True,
    )
    place = jnp.stack([shard, half])
    outer = sum_outer(outer)
    blocks, loss = gradients(place, blocks, latents, early, late, grids, members, pair)
    blocks = lax.all_to_all(blocks, "ens", split_axis=0, concat_axis=0, tiled=True)
    grad_out = join_columns(shard[None], outer, channels_used)
    grads = sum_groups(blocks, pair)
    return (loss.reshape(()), grad_out, *grads)


def solution(mesh):
    in_specs = (
        P("ens", "space", None),
        P("ens", "space", None),
        P("space", None),
        P(None, "space"),
        P(),
        P(),
        P(),
        P(),
        P(),
    )
    out_specs = (
        P(),
        P(),
        P("ens", "space"),
        P("ens", "space"),
        P("ens", "space"),
        P("ens", "space"),
    )

    return jax.shard_map(body, mesh=mesh, in_specs=in_specs, out_specs=out_specs, check_vma=False)
```

```python
import functools

import jax
import jax.numpy as jnp
from jax import lax
from jax.experimental import pallas as pl
from jax.experimental.pallas import tpu as pltpu
from jax.sharding import PartitionSpec as P


HEADS = 16
EPS = 1e-06
SMOOTH = 0.01
LANES = 128
MISC = 8
BF16, F32 = jnp.bfloat16, jnp.float32
VMEM = pl.BlockSpec(memory_space=pltpu.VMEM)
SMEM = pl.BlockSpec(memory_space=pltpu.SMEM)
ANY = pl.BlockSpec(memory_space=pl.ANY)


def dot32(left, right, contract=(1, 0)):
    dims = (((contract[0],), (contract[1],)), ((), ()))
    return lax.dot_general(left, right, dims, preferred_element_type=F32)


def swap(value, axis, bits):
    size = lax.axis_size(axis)
    return lax.ppermute(value, axis, [(i, i ^ bits) for i in range(size)])


def gather_slots(value, axis):
    parts = [value]
    for k in range(1, lax.axis_size(axis)):
        parts.append(swap(parts[k - 1], axis, 1) if k % 2 else swap(value, axis, k))
    return parts


def halves(pair):
    lane = lax.broadcasted_iota(jnp.int32, pair.shape, 1)
    zero = jnp.zeros_like(pair)
    first = lane < pair.shape[1] // 2
    return jnp.concatenate([jnp.where(first, pair, zero), jnp.where(first, zero, pair)], axis=0)


def joined(blocks):
    rows = blocks.shape[0] // 2
    lane = lax.broadcasted_iota(jnp.int32, (rows, blocks.shape[1]), 1)
    return jnp.where(lane < blocks.shape[1] // 2, blocks[:rows], blocks[rows:])


def query_kernel(latent_ref, rows_ref, w_hbm, out_ref, both_ref, w_ref, sem):
    chunks = w_ref.shape[0]
    step = w_ref.shape[2]
    copies = [
        pltpu.make_async_copy(w_hbm.at[:, pl.ds(c * step, step)], w_ref.at[c], sem.at[c])
        for c in range(chunks)
    ]
    for copy in copies:
        copy.start()
    nodes = latent_ref.shape[0]
    both_ref[:nodes] = latent_ref[...]
    both_ref[nodes:] = rows_ref[...]
    for c, copy in enumerate(copies):
        copy.wait()
        out_ref[:, c * step : (c + 1) * step] = dot32(rows_ref[...], w_ref[c]).astype(BF16)


def project_queries(latent, rows, weight):
    features = weight.shape[0]
    step = min(256, features)
    return pl.pallas_call(
        query_kernel,
        out_shape=(
            jax.ShapeDtypeStruct(rows.shape, BF16),
            jax.ShapeDtypeStruct((latent.shape[0] + rows.shape[0], features), BF16),
        ),
        in_specs=[VMEM, VMEM, ANY],
        out_specs=(VMEM, VMEM),
        scratch_shapes=[
            pltpu.VMEM((features // step, features, step), BF16),
            pltpu.SemaphoreType.DMA((features // step,)),
        ],
        cost_estimate=pl.CostEstimate(
            flops=2 * rows.size * features, bytes_accessed=2 * weight.size, transcendentals=0
        ),
        name="project_queries",
    )(latent, rows, weight)


def forward_kernel(shards, members, *refs):
    shard_ref, index_ref, grid_ref, query_ref, readout_ref = refs[:5]
    latent_refs = refs[5 : 5 + shards]
    weights_hbm = refs[5 + shards : 8 + shards]
    (
        key_ref,
        value_ref,
        soft_ref,
        attended_ref,
        normed_ref,
        inverse_ref,
        packed_ref,
        *w_refs,
        sem,
    ) = refs[8 + shards :]
    copies = [pltpu.make_async_copy(s, d, sem.at[i]) for i, (s, d) in enumerate(zip(weights_hbm, w_refs))]
    for copy in copies:
        copy.start()
    points, features = grid_ref.shape
    latents = jnp.concatenate([ref[...] for ref in latent_refs], axis=0)
    each = latent_refs[0].shape[0]
    index = index_ref[...]
    position = ((index // each) ^ shard_ref[0]) * each + index % each
    node = lax.broadcasted_iota(jnp.int32, (latents.shape[0], points), 0)
    chosen = jnp.where(node == position, 1.0, 0.0).astype(BF16)
    nodes = dot32(chosen, latents, (0, 0)).astype(BF16)
    copies[0].wait()
    key_ref[...] = dot32(nodes, w_refs[0][...]).astype(BF16)
    copies[1].wait()
    value_ref[...] = dot32(nodes, w_refs[1][...]).astype(BF16)
    factor = (features // HEADS) ** (-0.5)
    for pair in range(features // LANES):
        at = slice(pair * LANES, (pair + 1) * LANES)
        scores = dot32(query_ref[:, at], halves(key_ref[:, at]), (1, 1)) * factor
        soft = []
        for head in range(2):
            block = scores[:, head * LANES : (head + 1) * LANES]
            raised = jnp.exp(block - jnp.max(block, axis=-1, keepdims=True))
            soft.append(raised / jnp.sum(raised, axis=-1, keepdims=True))
        soft = jnp.concatenate(soft, axis=1)
        soft_ref[pair] = soft
        attended_ref[:, at] = dot32(soft.astype(BF16), halves(value_ref[:, at])).astype(BF16)
    copies[2].wait()
    hidden = grid_ref[...].astype(F32) + dot32(attended_ref[...], w_refs[2][...])
    inverse = lax.rsqrt(jnp.mean(hidden * hidden, axis=-1, keepdims=True) + EPS)
    normed = hidden * inverse
    normed_ref[...] = normed
    inverse_ref[...] = inverse
    normed_b = normed.astype(BF16)
    forecast = dot32(readout_ref[...], normed_b, (1, 1))
    high = forecast.astype(BF16)
    low = (forecast - high.astype(F32)).astype(BF16)
    channels = packed_ref.shape[1] // 2
    spare = jnp.zeros((channels - readout_ref.shape[0], points), BF16)
    fields = jnp.concatenate([high, spare, low, spare], axis=0)
    for m in range(members):
        packed_ref[m] = fields


def padded(channels):
    return channels + -channels % 16


def forward(shard, index, grid_rows, queries, readout, latents, weights, members):
    points, features = grid_rows.shape
    channels = padded(readout.shape[0])
    shape = jax.ShapeDtypeStruct
    return pl.pallas_call(
        functools.partial(forward_kernel, len(latents), members),
        out_shape=(
            shape((points, features), BF16),
            shape((points, features), BF16),
            shape((features // LANES, points, 2 * LANES), F32),
            shape((points, features), BF16),
            shape((points, features), F32),
            shape((points, 1), F32),
            shape((members, 2 * channels, points), BF16),
        ),
        in_specs=[SMEM] + [VMEM] * (4 + len(latents)) + [ANY] * 3,
        out_specs=(VMEM,) * 7,
        scratch_shapes=[pltpu.VMEM((features, features), BF16)] * 3
        + [pltpu.SemaphoreType.DMA((3,))],
        cost_estimate=pl.CostEstimate(
            flops=8 * points * features * features,
            bytes_accessed=6 * features * features,
            transcendentals=points * LANES * HEADS,
        ),
        name="decoder_forward",
    )(shard, index, grid_rows, queries, readout, *latents, *weights)


def backward_kernel(
    shards,
    blocks,
    nodes,
    place_ref,
    packed_ref,
    target_ref,
    index_ref,
    query_ref,
    key_ref,
    value_ref,
    soft_ref,
    normed_ref,
    inverse_ref,
    readout_ref,
    w_hbm,
    out_ref,
    outer_ref,
    w_ref,
    slope_ref,
    d_attended_ref,
    small_ref,
    truth_ref,
    weight_ref,
    sem,
):
    copy = pltpu.make_async_copy(w_hbm, w_ref, sem)
    copy.start()
    members = packed_ref.shape[0]
    points, features = normed_ref.shape
    channels_used = readout_ref.shape[0]
    channels = truth_ref.shape[0]
    for full, used in ((truth_ref, target_ref), (weight_ref, readout_ref)):
        full[:channels_used] = used[...]
        spare = (channels - channels_used, used.shape[1])
        full[channels_used:] = jnp.zeros(spare, used.dtype)
    width = features // blocks
    weight = (channels_used * points * shards) ** (-0.5)
    pair_weight = 1.0 / (members * (members - 1))
    chunk = 16

    def crps(c, loss):
        at = pl.ds(pl.multiple_of(c * chunk, chunk), chunk)
        low_at = pl.ds(pl.multiple_of(c * chunk + channels, chunk), chunk)
        fields = [
            packed_ref[m, at].astype(F32) + packed_ref[m, low_at].astype(F32)
            for m in range(members)
        ]
        truth = truth_ref[at]
        skill = jnp.zeros_like(truth)
        slopes = []
        for m in range(members):
            apart = fields[m] - truth
            square = apart * apart + SMOOTH
            root = lax.rsqrt(square)
            skill = skill + square * root
            slopes.append(apart * root * (weight / members))
        spread = jnp.zeros_like(truth)
        for m in range(members):
            for k in range(m):
                apart = fields[m] - fields[k]
                square = apart * apart + SMOOTH
                root = lax.rsqrt(square)
                spread = spread + square * root
                ratio = apart * root * (weight * pair_weight)
                slopes[m] = slopes[m] - ratio
                slopes[k] = slopes[k] + ratio
        for m in range(members):
            slope_ref[m, at] = slopes[m].astype(BF16)
        channel = c * chunk + lax.broadcasted_iota(jnp.int32, truth.shape, 0)
        term = skill * (1.0 / members) - spread * pair_weight
        return loss + jnp.where(channel < channels_used, term, 0.0)

    loss = lax.fori_loop(0, channels // chunk, crps, jnp.zeros((chunk, points), F32))
    loss = weight * jnp.sum(jnp.sum(loss, axis=0, keepdims=True), axis=1, keepdims=True)

    first = loss.astype(BF16).astype(F32)
    second = (loss - first).astype(BF16).astype(F32)
    for i, value in enumerate((first, second, loss - first - second)):
        small_ref[i : i + 1] = jnp.broadcast_to(value, (1, width))
    small_ref[3:] = jnp.zeros((small_ref.shape[0] - 3, width), F32)
    index = index_ref[...]
    line = 3
    for tag in (index // nodes, index % nodes):
        step = min(points, width)
        for c in range(0, points, step):
            small_ref[line : line + 1, :step] = tag[:, c : c + step].astype(F32)
            line = line + 1
    small = small_ref[...].astype(BF16)
    for b in range(blocks):
        out_ref[b, 4 * points :] = small

    def put(kind, column, value):
        step = min(width, value.shape[1])
        for c in range(0, value.shape[1], step):
            block, lane = divmod(column + c, width)
            out_ref[block, kind * points : (kind + 1) * points, lane : lane + step] = value[
                :, c : c + step
            ]

    own = slope_ref[place_ref[1]]
    normed = normed_ref[...]
    outer = dot32(own, normed.astype(BF16))
    columns = features // shards
    parts = [outer[:, s * columns : (s + 1) * columns] for s in range(shards)]
    for k in range(shards):
        part = parts[0]
        for s in range(1, shards):
            part = jnp.where((place_ref[0] ^ k) == s, parts[s], part)
        outer_ref[k] = part.astype(BF16)
    d_normed = dot32(own, weight_ref[...], (0, 0))
    mean = jnp.mean(d_normed * normed, axis=-1, keepdims=True)
    d_hidden = (inverse_ref[...] * (d_normed - normed * mean)).astype(BF16)
    put(3, 0, d_hidden)
    copy.wait()
    d_attended_ref[...] = dot32(d_hidden, w_ref[...], (1, 1)).astype(BF16)
    factor = (features // HEADS) ** (-0.5)
    for pair in range(features // LANES):
        at = slice(pair * LANES, (pair + 1) * LANES)
        soft = soft_ref[pair]
        d_out = d_attended_ref[:, at]
        d_probs = dot32(d_out, halves(value_ref[:, at]), (1, 1))
        put(2, pair * LANES, joined(dot32(soft.astype(BF16), d_out, (0, 0))).astype(BF16))
        product = d_probs * soft
        d_scores = []
        for head in range(2):
            block = slice(head * LANES, (head + 1) * LANES)
            summed = jnp.sum(product[:, block], axis=-1, keepdims=True)
            d_scores.append(soft[:, block] * (d_probs[:, block] - summed) * factor)
        d_scores = jnp.concatenate(d_scores, axis=1).astype(BF16)
        put(0, pair * LANES, dot32(d_scores, halves(key_ref[:, at])).astype(BF16))
        put(1, pair * LANES, joined(dot32(d_scores, query_ref[:, at], (0, 0))).astype(BF16))


def backward(place, packed, target, index, saved, readout, w_mix, shards, blocks, nodes):
    members = packed.shape[0]
    features = w_mix.shape[0]
    points = saved[0].shape[0]
    channels = padded(readout.shape[0])
    width = features // blocks
    small = 16
    return pl.pallas_call(
        functools.partial(backward_kernel, shards, blocks, nodes),
        out_shape=(
            jax.ShapeDtypeStruct((blocks, 4 * points + small, width), BF16),
            jax.ShapeDtypeStruct((shards, channels, features // shards), BF16),
        ),
        in_specs=[SMEM] + [VMEM] * 10 + [ANY],
        out_specs=(VMEM, VMEM),
        scratch_shapes=[
            pltpu.VMEM((features, features), BF16),
            pltpu.VMEM((members, channels, points), BF16),
            pltpu.VMEM((points, features), BF16),
            pltpu.VMEM((small, width), F32),
            pltpu.VMEM((channels, points), F32),
            pltpu.VMEM((channels, features), BF16),
            pltpu.SemaphoreType.DMA,
        ],
        cost_estimate=pl.CostEstimate(
            flops=4 * points * features * features,
            bytes_accessed=4 * features * features,
            transcendentals=0,
        ),
        name="decoder_backward",
    )(place, packed, target, index, *saved, readout, w_mix)


def gradient_kernel(shards, pair, members, nodes, place_ref, blocks_ref, *refs):
    latent_refs, early_refs, late_refs, other_refs, grid_refs = (
        refs[i * shards : (i + 1) * shards] for i in range(5)
    )
    out_ref, loss_ref = refs[5 * shards :]
    width = blocks_ref.shape[2]
    features = late_refs[0].shape[1]
    points = late_refs[0].shape[0]
    depth = features // members
    shard, half = place_ref[0], place_ref[1]
    start = 4 * points
    total = blocks_ref[0, start:].astype(F32)
    for s in range(1, shards):
        total = total + blocks_ref[s * pair, start:].astype(F32)
    loss_ref[...] = jnp.sum(total[:3, :1], axis=0, keepdims=True)

    def slots(kind, t):
        at = slice(kind * points, (kind + 1) * points)
        return [blocks_ref[(shard ^ k) * pair + (half ^ t), at] for k in range(shards)]

    def put(kind, total):
        total = total.astype(BF16)
        at = slice(kind * width, kind * width + total.shape[0])
        for m in range(members):
            out_ref[m, at] = total[:, m * depth : (m + 1) * depth]

    def product(kind, parts):
        left = jnp.concatenate([v for t in range(pair) for v in slots(kind, t)], axis=0)
        right = jnp.concatenate([v for part in parts for v in part], axis=0)
        put(kind, dot32(left, right, (0, 0)))

    product(3, [[ref[...] for ref in part] for part in (late_refs, other_refs)[:pair]])
    chosen = []
    for k in range(shards):
        index = blocks_ref[(shard ^ k) * pair, start : start + MISC].astype(jnp.int32)
        lines = max(points // width, 1)
        owner, offset = (
            jnp.concatenate([index[3 + b + i : 4 + b + i] for i in range(lines)], axis=1)
            for b in (0, lines)
        )
        position = (owner ^ shard) * nodes + offset
        node = lax.broadcasted_iota(jnp.int32, (nodes * shards, points), 0)
        chosen.append(jnp.where(node == position, 1.0, 0.0).astype(BF16))
    chosen = jnp.concatenate(chosen, axis=1)
    sums = []
    for t in range(pair):
        both = [jnp.concatenate(slots(kind, t), axis=0) for kind in (1, 2)]
        sums.append(dot32(chosen, jnp.concatenate(both, axis=1)).astype(BF16))
    others = [[ref[...] for ref in latent_refs]]
    if pair > 1:
        others.append([ref[:nodes] for ref in early_refs])
    put(
        1,
        dot32(
            jnp.concatenate(sums, axis=0),
            jnp.concatenate([v for part in others for v in part], axis=0),
            (0, 0),
        ),
    )
    grids = [[ref[...] for ref in grid_refs]]
    if pair > 1:
        grids.append([ref[nodes:] for ref in early_refs])
    product(0, grids)


def gradients(place, blocks, latents, early, late, other, grids, members, pair):
    count, _, width = blocks.shape
    shards = count // pair
    features = late[0].shape[1]
    points = late[0].shape[0]
    depth = features // members
    return pl.pallas_call(
        functools.partial(
            gradient_kernel, shards, pair, members, latents[0].shape[0]
        ),
        out_shape=(
            jax.ShapeDtypeStruct((members, 4 * width, depth), BF16),
            jax.ShapeDtypeStruct((1, 1), F32),
        ),
        in_specs=[SMEM] + [VMEM] * (1 + 5 * shards),
        out_specs=(VMEM, VMEM),
        cost_estimate=pl.CostEstimate(
            flops=8 * points * count * features * width,
            bytes_accessed=8 * points * count * features,
            transcendentals=0,
        ),
        name="weight_gradients",
    )(place, blocks, *latents, *early, *late, *other, *grids)


def sum_kernel(pair, blocks_ref, *refs):
    members, rows, _ = blocks_ref.shape
    width = rows // len(refs)
    for i, ref in enumerate(refs):
        at = slice(i * width, (i + 1) * width)
        for y in range(pair):
            total = blocks_ref[y, at].astype(F32)
            for m in range(y + pair, members, pair):
                total = total + blocks_ref[m, at].astype(F32)
            ref[:, y * width : (y + 1) * width] = total.T


def sum_groups(blocks, pair):
    _, rows, depth = blocks.shape
    return pl.pallas_call(
        functools.partial(sum_kernel, pair),
        out_shape=(jax.ShapeDtypeStruct((depth, pair * rows // 4), F32),) * 4,
        in_specs=[VMEM],
        out_specs=(VMEM,) * 4,
        name="sum_groups",
    )(blocks)


def join_kernel(shard_ref, *refs):
    *slot_refs, out_ref = refs
    used, columns = out_ref.shape[0], slot_refs[0].shape[1]
    values = [ref[...].astype(F32) for ref in slot_refs]
    for s in range(len(values)):
        value = values[0]
        for k in range(1, len(values)):
            value = jnp.where((shard_ref[0] ^ k) == s, values[k], value)
        out_ref[:, s * columns : (s + 1) * columns] = value[:used]


def join_columns(shard, parts, channels_used):
    columns = parts[0].shape[1] * len(parts)
    return pl.pallas_call(
        join_kernel,
        out_shape=jax.ShapeDtypeStruct((channels_used, columns), F32),
        in_specs=[SMEM] + [VMEM] * len(parts),
        out_specs=VMEM,
        name="join_columns",
    )(shard, *parts)


def sum_outer(parts):
    total = parts[0].astype(F32)
    received = []
    for k in range(1, parts.shape[0]):
        received.append(swap(parts[k], "space", k))
    for value in received:
        total = total + value.astype(F32)
    total = total.astype(BF16)
    size = lax.axis_size("ens")
    for bit in [1 << i for i in range(1, size.bit_length() - 1)] + [1]:
        other = swap(total, "ens", bit)
        total = (total.astype(F32) + other.astype(F32)).astype(BF16)
    return gather_slots(total, "space")


def body(
    grid_hidden, latent, tile_neighbor_index, target, w_query, w_key, w_value, w_mix, readout_weight
):
    nodes, _ = latent.shape[1:]
    channels_used = target.shape[0]
    shards, members = lax.axis_size("space"), lax.axis_size("ens")
    shard, member = lax.axis_index("space"), lax.axis_index("ens")
    pair = 2 if members % 2 == 0 and shards <= 8 else 1
    half = member % pair
    count = shards * pair
    groups = [
        [(g + y) * shards + s for s in range(shards) for y in range(pair)]
        for g in range(0, members, pair)
    ]

    own_latent, grid_rows = latent[0], grid_hidden[0]
    latents = gather_slots(own_latent, "space")
    grids = gather_slots(grid_rows, "space")
    queries, both = project_queries(own_latent, grid_rows, w_query)
    early = latents
    if pair > 1:
        early = swap(both, "ens", 1)
        early = gather_slots(early, "space")
    *saved, packed = forward(
        shard[None],
        tile_neighbor_index,
        grid_rows,
        queries,
        readout_weight,
        latents,
        (w_key, w_value, w_mix),
        members,
    )
    keyset, valueset, soft, attended, normed, inverse = saved
    packed = lax.all_to_all(packed, "ens", split_axis=0, concat_axis=0, tiled=True)
    late = gather_slots(attended, "space")
    other = late
    if pair > 1:
        other = []
        for k, part in enumerate(late):
            other.append(swap(other[k - 1], "space", 1) if k % 2 else swap(part, "ens", 1))
    saved = (queries, keyset, valueset, soft, normed, inverse)
    blocks, outer = backward(
        jnp.stack([shard, member]),
        packed,
        target,
        tile_neighbor_index,
        saved,
        readout_weight,
        w_mix,
        shards,
        count,
        nodes,
    )
    blocks = lax.all_to_all(
        blocks,
        ("ens", "space"),
        split_axis=0,
        concat_axis=0,
        axis_index_groups=groups,
        tiled=True,
    )
    place = jnp.stack([shard, half])
    outer = sum_outer(outer)
    blocks, loss = gradients(
        place, blocks, latents, early, late, other, grids, members, pair
    )
    blocks = lax.all_to_all(blocks, "ens", split_axis=0, concat_axis=0, tiled=True)
    grad_out = join_columns(shard[None], outer, channels_used)
    grads = sum_groups(blocks, pair)
    return (loss.reshape(()), grad_out, *grads)


def solution(mesh):
    in_specs = (
        P("ens", "space", None),
        P("ens", "space", None),
        P("space", None),
        P(None, "space"),
        P(),
        P(),
        P(),
        P(),
        P(),
    )
    out_specs = (
        P(),
        P(),
        P("ens", "space"),
        P("ens", "space"),
        P("ens", "space"),
        P("ens", "space"),
    )

    return jax.shard_map(body, mesh=mesh, in_specs=in_specs, out_specs=out_specs, check_vma=False)
```

```python
import functools

import jax
import jax.numpy as jnp
from jax import lax
from jax.experimental import pallas as pl
from jax.experimental.pallas import tpu as pltpu
from jax.sharding import PartitionSpec as P


HEADS = 16
EPS = 1e-06
SMOOTH = 0.01
LANES = 128
BF16, F32 = jnp.bfloat16, jnp.float32
VMEM = pl.BlockSpec(memory_space=pltpu.VMEM)
SMEM = pl.BlockSpec(memory_space=pltpu.SMEM)
ANY = pl.BlockSpec(memory_space=pl.ANY)


def dot32(left, right, contract=(1, 0)):
    dims = (((contract[0],), (contract[1],)), ((), ()))
    return lax.dot_general(left, right, dims, preferred_element_type=F32)


def swap(value, axis, bits):
    size = lax.axis_size(axis)
    return lax.ppermute(value, axis, [(i, i ^ bits) for i in range(size)])


def gather_slots(value, axis):
    parts = [value]
    for k in range(1, lax.axis_size(axis)):
        parts.append(swap(parts[k - 1], axis, 1) if k % 2 else swap(value, axis, k))
    return parts


def halves(pair):
    lane = lax.broadcasted_iota(jnp.int32, pair.shape, 1)
    zero = jnp.zeros_like(pair)
    first = lane < pair.shape[1] // 2
    return jnp.concatenate([jnp.where(first, pair, zero), jnp.where(first, zero, pair)], axis=0)


def joined(blocks):
    rows = blocks.shape[0] // 2
    lane = lax.broadcasted_iota(jnp.int32, (rows, blocks.shape[1]), 1)
    return jnp.where(lane < blocks.shape[1] // 2, blocks[:rows], blocks[rows:])


def query_kernel(latent_ref, rows_ref, w_hbm, out_ref, both_ref, w_ref, sem):
    chunks = w_ref.shape[0]
    step = w_ref.shape[2]
    copies = [
        pltpu.make_async_copy(w_hbm.at[:, pl.ds(c * step, step)], w_ref.at[c], sem.at[c])
        for c in range(chunks)
    ]
    for copy in copies:
        copy.start()
    nodes = latent_ref.shape[0]
    both_ref[:nodes] = latent_ref[...]
    both_ref[nodes:] = rows_ref[...]
    for c, copy in enumerate(copies):
        copy.wait()
        out_ref[:, c * step : (c + 1) * step] = dot32(rows_ref[...], w_ref[c]).astype(BF16)


def project_queries(latent, rows, weight):
    features = weight.shape[0]
    step = min(256, features)
    return pl.pallas_call(
        query_kernel,
        out_shape=(
            jax.ShapeDtypeStruct(rows.shape, BF16),
            jax.ShapeDtypeStruct((latent.shape[0] + rows.shape[0], features), BF16),
        ),
        in_specs=[VMEM, VMEM, ANY],
        out_specs=(VMEM, VMEM),
        scratch_shapes=[
            pltpu.VMEM((features // step, features, step), BF16),
            pltpu.SemaphoreType.DMA((features // step,)),
        ],
        cost_estimate=pl.CostEstimate(
            flops=2 * rows.size * features, bytes_accessed=2 * weight.size, transcendentals=0
        ),
        name="project_queries",
    )(latent, rows, weight)


def forward_kernel(shards, members, *refs):
    shard_ref, index_ref, grid_ref, query_ref, readout_ref = refs[:5]
    latent_refs = refs[5 : 5 + shards]
    weights_hbm = refs[5 + shards : 8 + shards]
    (
        key_ref,
        value_ref,
        soft_ref,
        attended_ref,
        normed_ref,
        inverse_ref,
        packed_ref,
        *w_refs,
        sem,
    ) = refs[8 + shards :]
    copies = [pltpu.make_async_copy(s, d, sem.at[i]) for i, (s, d) in enumerate(zip(weights_hbm, w_refs))]
    for copy in copies:
        copy.start()
    points, features = grid_ref.shape
    latents = jnp.concatenate([ref[...] for ref in latent_refs], axis=0)
    each = latent_refs[0].shape[0]
    index = index_ref[...]
    position = ((index // each) ^ shard_ref[0]) * each + index % each
    node = lax.broadcasted_iota(jnp.int32, (latents.shape[0], points), 0)
    chosen = jnp.where(node == position, 1.0, 0.0).astype(BF16)
    nodes = dot32(chosen, latents, (0, 0)).astype(BF16)
    copies[0].wait()
    key_ref[...] = dot32(nodes, w_refs[0][...]).astype(BF16)
    copies[1].wait()
    value_ref[...] = dot32(nodes, w_refs[1][...]).astype(BF16)
    factor = (features // HEADS) ** (-0.5)
    for pair in range(features // LANES):
        at = slice(pair * LANES, (pair + 1) * LANES)
        scores = dot32(query_ref[:, at], halves(key_ref[:, at]), (1, 1)) * factor
        soft = []
        for head in range(2):
            block = scores[:, head * LANES : (head + 1) * LANES]
            raised = jnp.exp(block - jnp.max(block, axis=-1, keepdims=True))
            soft.append(raised / jnp.sum(raised, axis=-1, keepdims=True))
        soft = jnp.concatenate(soft, axis=1)
        soft_ref[pair] = soft
        attended_ref[:, at] = dot32(soft.astype(BF16), halves(value_ref[:, at])).astype(BF16)
    copies[2].wait()
    hidden = grid_ref[...].astype(F32) + dot32(attended_ref[...], w_refs[2][...])
    inverse = lax.rsqrt(jnp.mean(hidden * hidden, axis=-1, keepdims=True) + EPS)
    normed = hidden * inverse
    normed_ref[...] = normed
    inverse_ref[...] = inverse
    normed_b = normed.astype(BF16)
    forecast = dot32(readout_ref[...], normed_b, (1, 1))
    high = forecast.astype(BF16)
    low = (forecast - high.astype(F32)).astype(BF16)
    channels = packed_ref.shape[1] // 2
    spare = jnp.zeros((channels - readout_ref.shape[0], points), BF16)
    fields = jnp.concatenate([high, spare, low, spare], axis=0)
    for m in range(members):
        packed_ref[m] = fields


def padded(channels):
    return channels + -channels % 16


def forward(shard, index, grid_rows, queries, readout, latents, weights, members):
    points, features = grid_rows.shape
    channels = padded(readout.shape[0])
    shape = jax.ShapeDtypeStruct
    return pl.pallas_call(
        functools.partial(forward_kernel, len(latents), members),
        out_shape=(
            shape((points, features), BF16),
            shape((points, features), BF16),
            shape((features // LANES, points, 2 * LANES), F32),
            shape((points, features), BF16),
            shape((points, features), F32),
            shape((points, 1), F32),
            shape((members, 2 * channels, points), BF16),
        ),
        in_specs=[SMEM] + [VMEM] * (4 + len(latents)) + [ANY] * 3,
        out_specs=(VMEM,) * 7,
        scratch_shapes=[pltpu.VMEM((features, features), BF16)] * 3
        + [pltpu.SemaphoreType.DMA((3,))],
        cost_estimate=pl.CostEstimate(
            flops=8 * points * features * features,
            bytes_accessed=6 * features * features,
            transcendentals=points * LANES * HEADS,
        ),
        name="decoder_forward",
    )(shard, index, grid_rows, queries, readout, *latents, *weights)


def put(out_ref, kind, column, value):
    points, width = value.shape[0], out_ref.shape[2]
    step = min(width, value.shape[1])
    for c in range(0, value.shape[1], step):
        block, lane = divmod(column + c, width)
        out_ref[block, kind * points : (kind + 1) * points, lane : lane + step] = value[
            :, c : c + step
        ]


def tag_lines(index_ref, nodes, width):
    index = index_ref[...]
    points = index.shape[1]
    step = min(points, width)
    lines = []
    for tag in (index // nodes, index % nodes):
        for c in range(0, points, step):
            line = tag[:, c : c + step].astype(F32)
            if step < width:
                line = jnp.concatenate([line, jnp.zeros((1, width - step), F32)], axis=1)
            lines.append(line)
    return lines


def stacked(lines, rows):
    spare = jnp.zeros((rows - len(lines), lines[0].shape[1]), F32)
    return jnp.concatenate(lines + [spare], axis=0).astype(BF16)


def slopes_kernel(
    shards,
    blocks,
    nodes,
    place_ref,
    fields_ref,
    target_ref,
    index_ref,
    value_ref,
    soft_ref,
    normed_ref,
    inverse_ref,
    readout_ref,
    w_hbm,
    out_ref,
    d_attended_ref,
    *refs,
):
    outer_refs, (slope_ref, w_ref, truth_ref, weight_ref, sem) = refs[:shards], refs[shards:]
    copy = pltpu.make_async_copy(w_hbm, w_ref, sem)
    copy.start()
    members = fields_ref.shape[0]
    points, features = normed_ref.shape
    channels_used = readout_ref.shape[0]
    channels = truth_ref.shape[0]
    for full, used in ((truth_ref, target_ref), (weight_ref, readout_ref)):
        full[:channels_used] = used[...]
        spare = (channels - channels_used, used.shape[1])
        full[channels_used:] = jnp.zeros(spare, used.dtype)
    width = features // blocks
    weight = (channels_used * points * shards) ** (-0.5)
    pair_weight = 1.0 / (members * (members - 1))
    chunk = 16

    def crps(c, loss):
        at = pl.ds(pl.multiple_of(c * chunk, chunk), chunk)
        low_at = pl.ds(pl.multiple_of(c * chunk + channels, chunk), chunk)
        fields = [
            fields_ref[m, at].astype(F32) + fields_ref[m, low_at].astype(F32)
            for m in range(members)
        ]
        truth = truth_ref[at]
        skill = jnp.zeros_like(truth)
        slopes = []
        for m in range(members):
            apart = fields[m] - truth
            square = apart * apart + SMOOTH
            root = lax.rsqrt(square)
            skill = skill + square * root
            slopes.append(apart * root * (weight / members))
        spread = jnp.zeros_like(truth)
        for m in range(members):
            for k in range(m):
                apart = fields[m] - fields[k]
                square = apart * apart + SMOOTH
                root = lax.rsqrt(square)
                spread = spread + square * root
                ratio = apart * root * (weight * pair_weight)
                slopes[m] = slopes[m] - ratio
                slopes[k] = slopes[k] + ratio
        for m in range(members):
            slope_ref[m, at] = slopes[m].astype(BF16)
        channel = c * chunk + lax.broadcasted_iota(jnp.int32, truth.shape, 0)
        term = skill * (1.0 / members) - spread * pair_weight
        return loss + jnp.where(channel < channels_used, term, 0.0)

    loss = lax.fori_loop(0, channels // chunk, crps, jnp.zeros((chunk, points), F32))
    loss = weight * jnp.sum(jnp.sum(loss, axis=0, keepdims=True), axis=1, keepdims=True)
    high = loss.astype(BF16).astype(F32)
    low = (loss - high).astype(BF16).astype(F32)
    lines = [jnp.broadcast_to(value, (1, width)) for value in (high, low, loss - high - low)]
    lines = lines + tag_lines(index_ref, nodes, width)
    tags = stacked(lines, out_ref.shape[1] - 2 * points)
    for b in range(blocks):
        out_ref[b, 2 * points :] = tags
    own = slope_ref[place_ref[1]]
    normed = normed_ref[...]
    outer = dot32(own, normed.astype(BF16))
    columns = features // shards
    parts = [outer[:, s * columns : (s + 1) * columns] for s in range(shards)]
    for k in range(shards):
        part = parts[0]
        for s in range(1, shards):
            part = jnp.where((place_ref[0] ^ k) == s, parts[s], part)
        outer_refs[k][...] = part.astype(BF16)
    d_normed = dot32(own, weight_ref[...], (0, 0))
    mean = jnp.mean(d_normed * normed, axis=-1, keepdims=True)
    d_hidden = (inverse_ref[...] * (d_normed - normed * mean)).astype(BF16)
    put(out_ref, 0, 0, d_hidden)
    copy.wait()
    d_attended_ref[...] = dot32(d_hidden, w_ref[...], (1, 1)).astype(BF16)
    for pair in range(features // LANES):
        at = slice(pair * LANES, (pair + 1) * LANES)
        d_value = joined(dot32(soft_ref[pair].astype(BF16), d_attended_ref[:, at], (0, 0)))
        put(out_ref, 1, pair * LANES, d_value.astype(BF16))


def backward_slopes(place, fields, target, index, saved, readout, w_mix, shards, blocks, nodes):
    members, points = fields.shape[0], target.shape[1]
    features = w_mix.shape[0]
    channels = padded(readout.shape[0])
    shape = jax.ShapeDtypeStruct
    return pl.pallas_call(
        functools.partial(slopes_kernel, shards, blocks, nodes),
        out_shape=(
            shape((blocks, 2 * points + 16, features // blocks), BF16),
            shape((points, features), BF16),
        )
        + (shape((channels, features // shards), BF16),) * shards,
        in_specs=[SMEM] + [VMEM] * 8 + [ANY],
        out_specs=(VMEM,) * (2 + shards),
        scratch_shapes=[
            pltpu.VMEM((members, channels, points), BF16),
            pltpu.VMEM((features, features), BF16),
            pltpu.VMEM((channels, points), F32),
            pltpu.VMEM((channels, features), BF16),
            pltpu.SemaphoreType.DMA,
        ],
        cost_estimate=pl.CostEstimate(
            flops=2 * points * features * features,
            bytes_accessed=2 * features * features,
            transcendentals=0,
        ),
        name="backward_slopes",
    )(place, fields, target, index, *saved, readout, w_mix)


def scores_kernel(pair, place_ref, query_ref, key_ref, value_ref, soft_ref, d_attended_ref, *refs):
    *out_refs, block_ref = refs
    features = query_ref.shape[1]
    factor = (features // HEADS) ** (-0.5)
    for heads in range(features // LANES):
        at = slice(heads * LANES, (heads + 1) * LANES)
        soft = soft_ref[heads]
        d_probs = dot32(d_attended_ref[:, at], halves(value_ref[:, at]), (1, 1))
        product = d_probs * soft
        d_scores = []
        for head in range(2):
            block = slice(head * LANES, (head + 1) * LANES)
            summed = jnp.sum(product[:, block], axis=-1, keepdims=True)
            d_scores.append(soft[:, block] * (d_probs[:, block] - summed) * factor)
        d_scores = jnp.concatenate(d_scores, axis=1).astype(BF16)
        put(block_ref, 0, heads * LANES, dot32(d_scores, halves(key_ref[:, at])).astype(BF16))
        d_key = joined(dot32(d_scores, query_ref[:, at], (0, 0)))
        put(block_ref, 1, heads * LANES, d_key.astype(BF16))
    for i, ref in enumerate(out_refs):
        k, t = divmod(i, pair)
        ref[...] = block_ref[(place_ref[0] ^ k) * pair + (place_ref[1] ^ t)]


def backward_scores(place, saved, d_attended, blocks, pair):
    points, features = d_attended.shape
    block = (2 * points, features // blocks)
    return pl.pallas_call(
        functools.partial(scores_kernel, pair),
        out_shape=(jax.ShapeDtypeStruct(block, BF16),) * blocks,
        in_specs=[SMEM] + [VMEM] * 5,
        out_specs=(VMEM,) * blocks,
        scratch_shapes=[pltpu.VMEM((blocks,) + block, BF16)],
        cost_estimate=pl.CostEstimate(
            flops=12 * points * points * features,
            bytes_accessed=8 * points * features,
            transcendentals=0,
        ),
        name="backward_scores",
    )(place, *saved, d_attended)


def product_of(lefts, rights):
    left = jnp.concatenate(lefts, axis=0)
    return dot32(left, jnp.concatenate(rights, axis=0), (0, 0)).astype(BF16)


def node_sums(lefts, chosen, shards):
    return [
        dot32(chosen, jnp.concatenate(lefts[t : t + shards], axis=0)).astype(BF16)
        for t in range(0, len(lefts), shards)
    ]


def first_gradients_kernel(shards, pair, nodes, place_ref, blocks_ref, *refs):
    latent_refs, early_refs, late_refs, other_refs = (
        refs[i * shards : (i + 1) * shards] for i in range(4)
    )
    out_ref, chosen_ref, loss_ref = refs[4 * shards :]
    members, _, depth = out_ref.shape
    width = blocks_ref.shape[2]
    points = late_refs[0].shape[0]
    shard, half = place_ref[0], place_ref[1]
    start = 2 * points
    total = blocks_ref[0, start:].astype(F32)
    for s in range(1, shards):
        total = total + blocks_ref[s * pair, start:].astype(F32)
    loss_ref[...] = jnp.sum(total[:3, :1], axis=0, keepdims=True)

    def slots(kind):
        at = slice(kind * points, (kind + 1) * points)
        return [
            blocks_ref[(shard ^ k) * pair + (half ^ t), at]
            for t in range(pair)
            for k in range(shards)
        ]

    def store(kind, total):
        for m in range(members):
            out_ref[m, kind * width : (kind + 1) * width] = total[:, m * depth : (m + 1) * depth]

    rights = [ref[...] for part in (late_refs, other_refs)[:pair] for ref in part]
    store(0, product_of(slots(0), rights))
    lines = max(points // width, 1)
    for k in range(shards):
        index = blocks_ref[(shard ^ k) * pair, start:].astype(jnp.int32)
        owner, offset = (
            jnp.concatenate([index[3 + b + i : 4 + b + i] for i in range(lines)], axis=1)
            for b in (0, lines)
        )
        position = (owner ^ shard) * nodes + offset
        node = lax.broadcasted_iota(jnp.int32, (nodes * shards, points), 0)
        chosen_ref[:, k * points : (k + 1) * points] = jnp.where(node == position, 1.0, 0.0).astype(
            BF16
        )
    rights = [ref[...] for ref in latent_refs]
    if pair > 1:
        rights = rights + [ref[:nodes] for ref in early_refs]
    store(1, product_of(node_sums(slots(1), chosen_ref[...], shards), rights))


def first_gradients(place, blocks, latents, early, late, other, members, pair):
    count, _, width = blocks.shape
    shards = count // pair
    points, features = late[0].shape
    nodes = latents[0].shape[0]
    shape = jax.ShapeDtypeStruct
    return pl.pallas_call(
        functools.partial(first_gradients_kernel, shards, pair, nodes),
        out_shape=(
            shape((members, 2 * width, features // members), BF16),
            shape((nodes * shards, points * shards), BF16),
            shape((1, 1), F32),
        ),
        in_specs=[SMEM] + [VMEM] * (1 + 4 * shards),
        out_specs=(VMEM,) * 3,
        cost_estimate=pl.CostEstimate(
            flops=4 * points * count * features * width,
            bytes_accessed=4 * points * count * features,
            transcendentals=0,
        ),
        name="first_gradients",
    )(place, blocks, *latents, *early, *late, *other)


def last_gradients_kernel(shards, pair, members, nodes, place_ref, chosen_ref, *refs):
    count = shards * pair
    left_refs, refs = refs[:count], refs[count:]
    latent_refs, early_refs, grid_refs = (refs[i * shards : (i + 1) * shards] for i in range(3))
    *out_refs, block_ref = refs[3 * shards :]
    points = grid_refs[0].shape[0]
    width = left_refs[0].shape[1]
    depth = block_ref.shape[2]

    def slots(kind):
        at = slice(kind * points, (kind + 1) * points)
        return [left_refs[k * pair + t][at] for t in range(pair) for k in range(shards)]

    def store(kind, total):
        for m in range(members):
            block_ref[m, kind * width : (kind + 1) * width] = total[:, m * depth : (m + 1) * depth]

    rights = [ref[...] for ref in grid_refs]
    if pair > 1:
        rights = rights + [ref[nodes:] for ref in early_refs]
    store(0, product_of(slots(0), rights))
    rights = [ref[...] for ref in latent_refs]
    if pair > 1:
        rights = rights + [ref[:nodes] for ref in early_refs]
    store(1, product_of(node_sums(slots(1), chosen_ref[...], shards), rights))
    for k, ref in enumerate(out_refs):
        ref[...] = block_ref[place_ref[2] ^ k]


def last_gradients(place, lefts, chosen, latents, early, grids, members, pair):
    count, width = len(lefts), lefts[0].shape[1]
    shards = count // pair
    points, features = grids[0].shape
    nodes = latents[0].shape[0]
    block = (2 * width, features // members)
    return pl.pallas_call(
        functools.partial(last_gradients_kernel, shards, pair, members, nodes),
        out_shape=(jax.ShapeDtypeStruct(block, BF16),) * members,
        in_specs=[SMEM] + [VMEM] * (1 + count + 3 * shards),
        out_specs=(VMEM,) * members,
        scratch_shapes=[pltpu.VMEM((members,) + block, BF16)],
        cost_estimate=pl.CostEstimate(
            flops=4 * points * count * features * width,
            bytes_accessed=4 * points * count * features,
            transcendentals=0,
        ),
        name="last_gradients",
    )(place, chosen, *lefts, *latents, *early, *grids)


def sum_kernel(pair, blocks_ref, *refs):
    members, rows, _ = blocks_ref.shape
    width = rows // len(refs)
    for i, ref in enumerate(refs):
        at = slice(i * width, (i + 1) * width)
        for y in range(pair):
            total = blocks_ref[y, at].astype(F32)
            for m in range(y + pair, members, pair):
                total = total + blocks_ref[m, at].astype(F32)
            ref[:, y * width : (y + 1) * width] = total.T


def sum_groups(blocks, pair):
    _, rows, depth = blocks.shape
    return pl.pallas_call(
        functools.partial(sum_kernel, pair),
        out_shape=(jax.ShapeDtypeStruct((depth, pair * rows // 2), F32),) * 2,
        in_specs=[VMEM],
        out_specs=(VMEM,) * 2,
        cost_estimate=pl.CostEstimate(
            flops=blocks.size, bytes_accessed=4 * blocks.size, transcendentals=0
        ),
        name="sum_groups",
    )(blocks)


def sum_slots_kernel(pair, place_ref, *refs):
    slot_refs, out_refs = refs[:-2], refs[-2:]
    width = slot_refs[0].shape[0] // 2
    for i, ref in enumerate(out_refs):
        at = slice(i * width, (i + 1) * width)
        totals = []
        for y in range(pair):
            total = slot_refs[y][at].astype(F32)
            for k in range(y + pair, len(slot_refs), pair):
                total = total + slot_refs[k][at].astype(F32)
            totals.append(total.T)
        for y in range(pair):
            value = totals[y]
            if pair > 1:
                value = jnp.where(place_ref[1] == y, totals[0], totals[1])
            ref[:, y * width : (y + 1) * width] = value


def sum_slots(place, parts, pair):
    rows, depth = parts[0].shape
    return pl.pallas_call(
        functools.partial(sum_slots_kernel, pair),
        out_shape=(jax.ShapeDtypeStruct((depth, pair * rows // 2), F32),) * 2,
        in_specs=[SMEM] + [VMEM] * len(parts),
        out_specs=(VMEM,) * 2,
        name="sum_slots",
    )(place, *parts)


def join_kernel(shard_ref, *refs):
    *slot_refs, out_ref = refs
    used, columns = out_ref.shape[0], slot_refs[0].shape[1]
    values = [ref[...].astype(F32) for ref in slot_refs]
    for s in range(len(values)):
        value = values[0]
        for k in range(1, len(values)):
            value = jnp.where((shard_ref[0] ^ k) == s, values[k], value)
        out_ref[:, s * columns : (s + 1) * columns] = value[:used]


def join_columns(shard, parts, channels_used):
    columns = parts[0].shape[1] * len(parts)
    return pl.pallas_call(
        join_kernel,
        out_shape=jax.ShapeDtypeStruct((channels_used, columns), F32),
        in_specs=[SMEM] + [VMEM] * len(parts),
        out_specs=VMEM,
        name="join_columns",
    )(shard, *parts)


def sum_outer(parts):
    total = parts[0].astype(F32)
    received = []
    for k in range(1, len(parts)):
        received.append(swap(parts[k], "space", k))
    for value in received:
        total = total + value.astype(F32)
    total = total.astype(BF16)
    size = lax.axis_size("ens")
    for bit in [1 << i for i in range(1, size.bit_length() - 1)] + [1]:
        other = swap(total, "ens", bit)
        total = (total.astype(F32) + other.astype(F32)).astype(BF16)
    return gather_slots(total, "space")


def body(
    grid_hidden, latent, tile_neighbor_index, target, w_query, w_key, w_value, w_mix, readout_weight
):
    nodes, _ = latent.shape[1:]
    channels_used = target.shape[0]
    shards, members = lax.axis_size("space"), lax.axis_size("ens")
    shard, member = lax.axis_index("space"), lax.axis_index("ens")
    pair = 2 if members % 2 == 0 and shards <= 8 else 1
    half = member % pair
    count = shards * pair
    groups = [
        [(g + y) * shards + s for s in range(shards) for y in range(pair)]
        for g in range(0, members, pair)
    ]

    own_latent, grid_rows = latent[0], grid_hidden[0]
    latents = gather_slots(own_latent, "space")
    grids = gather_slots(grid_rows, "space")
    queries, both = project_queries(own_latent, grid_rows, w_query)
    early = latents
    if pair > 1:
        early = swap(both, "ens", 1)
        early = gather_slots(early, "space")
    *saved, packed = forward(
        shard[None],
        tile_neighbor_index,
        grid_rows,
        queries,
        readout_weight,
        latents,
        (w_key, w_value, w_mix),
        members,
    )
    keyset, valueset, soft, attended, normed, inverse = saved
    packed = lax.all_to_all(packed, "ens", split_axis=0, concat_axis=0, tiled=True)
    late = gather_slots(attended, "space")
    other = late
    if pair > 1:
        other = []
        for k, part in enumerate(late):
            other.append(swap(other[k - 1], "space", 1) if k % 2 else swap(part, "ens", 1))
    saved = (queries, keyset, valueset, soft, normed, inverse)
    place = jnp.stack([shard, half, member])
    blocks, d_attended, *outer = backward_slopes(
        jnp.stack([shard, member]),
        packed,
        target,
        tile_neighbor_index,
        (valueset, soft, normed, inverse),
        readout_weight,
        w_mix,
        shards,
        count,
        nodes,
    )
    blocks = lax.all_to_all(
        blocks,
        ("ens", "space"),
        split_axis=0,
        concat_axis=0,
        axis_index_groups=groups,
        tiled=True,
    )
    saved = (queries, keyset, valueset, soft)
    parts = backward_scores(place, saved, d_attended, count, pair)
    lefts = [parts[0]]
    for i in range(1, count):
        k, t = divmod(i, pair)
        moves = [
            (m * shards + s, (m ^ t) * shards + (s ^ k))
            for m in range(members)
            for s in range(shards)
        ]
        lefts.append(lax.ppermute(parts[i], ("ens", "space"), moves))
    outer = sum_outer(outer)
    blocks, chosen, loss = first_gradients(
        place, blocks, latents, early, late, other, members, pair
    )
    blocks = lax.all_to_all(blocks, "ens", split_axis=0, concat_axis=0, tiled=True)
    parts = last_gradients(place, lefts, chosen, latents, early, grids, members, pair)
    sums = [parts[0]]
    for k in range(1, members):
        sums.append(swap(parts[k], "ens", k))
    grad_out = join_columns(shard[None], outer, channels_used)
    grad_mix, grad_value = sum_groups(blocks, pair)
    grad_query, grad_key = sum_slots(place, sums, pair)
    return (loss.reshape(()), grad_out, grad_query, grad_key, grad_value, grad_mix)


def solution(mesh):
    in_specs = (
        P("ens", "space", None),
        P("ens", "space", None),
        P("space", None),
        P(None, "space"),
        P(),
        P(),
        P(),
        P(),
        P(),
    )
    out_specs = (
        P(),
        P(),
        P("ens", "space"),
        P("ens", "space"),
        P("ens", "space"),
        P("ens", "space"),
    )

    return jax.shard_map(body, mesh=mesh, in_specs=in_specs, out_specs=out_specs, check_vma=False)
```

```python
import functools

import jax
import jax.numpy as jnp
from jax import lax
from jax.experimental import pallas as pl
from jax.experimental.pallas import tpu as pltpu
from jax.sharding import PartitionSpec as P


HEADS = 16
EPS = 1e-06
SMOOTH = 0.01
LANES = 128
MISC = 8
BF16, F32 = jnp.bfloat16, jnp.float32
VMEM = pl.BlockSpec(memory_space=pltpu.VMEM)
SMEM = pl.BlockSpec(memory_space=pltpu.SMEM)
ANY = pl.BlockSpec(memory_space=pl.ANY)
HBM = pl.BlockSpec(memory_space=pltpu.HBM)


def dot32(left, right, contract=(1, 0)):
    dims = (((contract[0],), (contract[1],)), ((), ()))
    return lax.dot_general(left, right, dims, preferred_element_type=F32)


def swap(value, axis, bits):
    size = lax.axis_size(axis)
    return lax.ppermute(value, axis, [(i, i ^ bits) for i in range(size)])


def gather_slots(value, axis):
    parts = [value]
    for k in range(1, lax.axis_size(axis)):
        parts.append(swap(parts[k - 1], axis, 1) if k % 2 else swap(value, axis, k))
    return parts


def halves(pair):
    lane = lax.broadcasted_iota(jnp.int32, pair.shape, 1)
    zero = jnp.zeros_like(pair)
    first = lane < pair.shape[1] // 2
    return jnp.concatenate([jnp.where(first, pair, zero), jnp.where(first, zero, pair)], axis=0)


def joined(blocks):
    rows = blocks.shape[0] // 2
    lane = lax.broadcasted_iota(jnp.int32, (rows, blocks.shape[1]), 1)
    return jnp.where(lane < blocks.shape[1] // 2, blocks[:rows], blocks[rows:])


def query_kernel(latent_ref, rows_ref, w_hbm, out_ref, both_ref, w_ref, sem):
    chunks = w_ref.shape[0]
    step = w_ref.shape[2]
    copies = [
        pltpu.make_async_copy(w_hbm.at[:, pl.ds(c * step, step)], w_ref.at[c], sem.at[c])
        for c in range(chunks)
    ]
    for copy in copies:
        copy.start()
    nodes = latent_ref.shape[0]
    both_ref[:nodes] = latent_ref[...]
    both_ref[nodes:] = rows_ref[...]
    for c, copy in enumerate(copies):
        copy.wait()
        out_ref[:, c * step : (c + 1) * step] = dot32(rows_ref[...], w_ref[c]).astype(BF16)


def project_queries(latent, rows, weight):
    features = weight.shape[0]
    step = min(256, features)
    return pl.pallas_call(
        query_kernel,
        out_shape=(
            jax.ShapeDtypeStruct(rows.shape, BF16),
            jax.ShapeDtypeStruct((latent.shape[0] + rows.shape[0], features), BF16),
        ),
        in_specs=[VMEM, VMEM, ANY],
        out_specs=(VMEM, VMEM),
        scratch_shapes=[
            pltpu.VMEM((features // step, features, step), BF16),
            pltpu.SemaphoreType.DMA((features // step,)),
        ],
        cost_estimate=pl.CostEstimate(
            flops=2 * rows.size * features, bytes_accessed=2 * weight.size, transcendentals=0
        ),
        name="proj",
    )(latent, rows, weight)


def forward_kernel(shards, members, *refs):
    shard_ref, index_ref, grid_ref, query_ref, readout_ref = refs[:5]
    latent_refs = refs[5 : 5 + shards]
    weights_hbm = refs[5 + shards : 8 + shards]
    (
        key_ref,
        value_ref,
        soft_ref,
        attended_ref,
        normed_ref,
        inverse_ref,
        packed_ref,
        *w_refs,
        sem,
    ) = refs[8 + shards :]
    copies = [pltpu.make_async_copy(s, d, sem.at[i]) for i, (s, d) in enumerate(zip(weights_hbm, w_refs))]
    for copy in copies:
        copy.start()
    points, features = grid_ref.shape
    latents = jnp.concatenate([ref[...] for ref in latent_refs], axis=0)
    each = latent_refs[0].shape[0]
    index = index_ref[...]
    position = ((index // each) ^ shard_ref[0]) * each + index % each
    node = lax.broadcasted_iota(jnp.int32, (latents.shape[0], points), 0)
    chosen = jnp.where(node == position, 1.0, 0.0).astype(BF16)
    nodes = dot32(chosen, latents, (0, 0)).astype(BF16)
    copies[0].wait()
    key_ref[...] = dot32(nodes, w_refs[0][...]).astype(BF16)
    copies[1].wait()
    value_ref[...] = dot32(nodes, w_refs[1][...]).astype(BF16)
    factor = (features // HEADS) ** (-0.5)
    for pair in range(features // LANES):
        at = slice(pair * LANES, (pair + 1) * LANES)
        scores = dot32(query_ref[:, at], halves(key_ref[:, at]), (1, 1)) * factor
        soft = []
        for head in range(2):
            block = scores[:, head * LANES : (head + 1) * LANES]
            raised = jnp.exp(block - jnp.max(block, axis=-1, keepdims=True))
            soft.append(raised / jnp.sum(raised, axis=-1, keepdims=True))
        soft = jnp.concatenate(soft, axis=1)
        soft_ref[pair] = soft
        attended_ref[:, at] = dot32(soft.astype(BF16), halves(value_ref[:, at])).astype(BF16)
    copies[2].wait()
    hidden = grid_ref[...].astype(F32) + dot32(attended_ref[...], w_refs[2][...])
    inverse = lax.rsqrt(jnp.mean(hidden * hidden, axis=-1, keepdims=True) + EPS)
    normed = hidden * inverse
    normed_ref[...] = normed
    inverse_ref[...] = inverse
    normed_b = normed.astype(BF16)
    forecast = dot32(readout_ref[...], normed_b, (1, 1))
    high = forecast.astype(BF16)
    low = (forecast - high.astype(F32)).astype(BF16)
    channels = packed_ref.shape[1] // 2
    spare = jnp.zeros((channels - readout_ref.shape[0], points), BF16)
    fields = jnp.concatenate([high, spare, low, spare], axis=0)
    for m in range(members):
        packed_ref[m] = fields


def padded(channels):
    return channels + -channels % 16


def forward(shard, index, grid_rows, queries, readout, latents, weights, members):
    points, features = grid_rows.shape
    channels = padded(readout.shape[0])
    shape = jax.ShapeDtypeStruct
    return pl.pallas_call(
        functools.partial(forward_kernel, len(latents), members),
        out_shape=(
            shape((points, features), BF16),
            shape((points, features), BF16),
            shape((features // LANES, points, 2 * LANES), F32),
            shape((points, features), BF16),
            shape((points, features), F32),
            shape((points, 1), F32),
            shape((members, 2 * channels, points), BF16),
        ),
        in_specs=[SMEM] + [VMEM] * (4 + len(latents)) + [ANY] * 3,
        out_specs=(VMEM,) * 7,
        scratch_shapes=[pltpu.VMEM((features, features), BF16)] * 3
        + [pltpu.SemaphoreType.DMA((3,))],
        cost_estimate=pl.CostEstimate(
            flops=8 * points * features * features,
            bytes_accessed=6 * features * features,
            transcendentals=points * LANES * HEADS,
        ),
        name="fwd",
    )(shard, index, grid_rows, queries, readout, *latents, *weights)


def backward_kernel(
    shards,
    blocks,
    nodes,
    place_ref,
    packed_ref,
    target_ref,
    index_ref,
    query_ref,
    key_ref,
    value_ref,
    soft_ref,
    normed_ref,
    inverse_ref,
    readout_ref,
    w_hbm,
    out_ref,
    *refs,
):
    outer_refs = refs[:shards]
    slope_ref, d_attended_ref, small_ref, truth_ref, weight_ref, w_ref, sem = refs[shards:]
    copy = pltpu.make_async_copy(w_hbm, w_ref, sem)
    copy.start()
    members = packed_ref.shape[0]
    points, features = normed_ref.shape
    channels_used = readout_ref.shape[0]
    channels = truth_ref.shape[0]
    for full, used in ((truth_ref, target_ref), (weight_ref, readout_ref)):
        full[:channels_used] = used[...]
        spare = (channels - channels_used, used.shape[1])
        full[channels_used:] = jnp.zeros(spare, used.dtype)
    width = features // blocks
    weight = (channels_used * points * shards) ** (-0.5)
    pair_weight = 1.0 / (members * (members - 1))
    chunk = 16

    def crps(c, loss):
        at = pl.ds(pl.multiple_of(c * chunk, chunk), chunk)
        low_at = pl.ds(pl.multiple_of(c * chunk + channels, chunk), chunk)
        fields = [
            packed_ref[m, at].astype(F32) + packed_ref[m, low_at].astype(F32)
            for m in range(members)
        ]
        truth = truth_ref[at]
        skill = jnp.zeros_like(truth)
        slopes = []
        for m in range(members):
            apart = fields[m] - truth
            square = apart * apart + SMOOTH
            root = lax.rsqrt(square)
            skill = skill + square * root
            slopes.append(apart * root * (weight / members))
        spread = jnp.zeros_like(truth)
        for m in range(members):
            for k in range(m):
                apart = fields[m] - fields[k]
                square = apart * apart + SMOOTH
                root = lax.rsqrt(square)
                spread = spread + square * root
                ratio = apart * root * (weight * pair_weight)
                slopes[m] = slopes[m] - ratio
                slopes[k] = slopes[k] + ratio
        for m in range(members):
            slope_ref[m, at] = slopes[m].astype(BF16)
        channel = c * chunk + lax.broadcasted_iota(jnp.int32, truth.shape, 0)
        term = skill * (1.0 / members) - spread * pair_weight
        return loss + jnp.where(channel < channels_used, term, 0.0)

    loss = lax.fori_loop(0, channels // chunk, crps, jnp.zeros((chunk, points), F32))
    loss = weight * jnp.sum(jnp.sum(loss, axis=0, keepdims=True), axis=1, keepdims=True)

    first = loss.astype(BF16).astype(F32)
    second = (loss - first).astype(BF16).astype(F32)
    for i, value in enumerate((first, second, loss - first - second)):
        small_ref[i : i + 1] = jnp.broadcast_to(value, (1, width))
    small_ref[3:] = jnp.zeros((small_ref.shape[0] - 3, width), F32)
    index = index_ref[...]
    line = 3
    for tag in (index // nodes, index % nodes):
        step = min(points, width)
        for c in range(0, points, step):
            small_ref[line : line + 1, :step] = tag[:, c : c + step].astype(F32)
            line = line + 1
    small = small_ref[...].astype(BF16)
    for b in range(blocks):
        out_ref[b, 4 * points :] = small

    def put(kind, column, value):
        step = min(width, value.shape[1])
        for c in range(0, value.shape[1], step):
            block, lane = divmod(column + c, width)
            out_ref[block, kind * points : (kind + 1) * points, lane : lane + step] = value[
                :, c : c + step
            ]

    own = slope_ref[place_ref[1]]
    normed = normed_ref[...]
    outer = dot32(own, normed.astype(BF16))
    columns = features // shards
    parts = [outer[:, s * columns : (s + 1) * columns] for s in range(shards)]
    for k in range(shards):
        part = parts[0]
        for s in range(1, shards):
            part = jnp.where((place_ref[0] ^ k) == s, parts[s], part)
        outer_refs[k][...] = part.astype(BF16)
    d_normed = dot32(own, weight_ref[...], (0, 0))
    mean = jnp.mean(d_normed * normed, axis=-1, keepdims=True)
    d_hidden = (inverse_ref[...] * (d_normed - normed * mean)).astype(BF16)
    put(3, 0, d_hidden)
    copy.wait()
    d_attended_ref[...] = dot32(d_hidden, w_ref[...], (1, 1)).astype(BF16)
    factor = (features // HEADS) ** (-0.5)
    for pair in range(features // LANES):
        at = slice(pair * LANES, (pair + 1) * LANES)
        soft = soft_ref[pair]
        d_out = d_attended_ref[:, at]
        d_probs = dot32(d_out, halves(value_ref[:, at]), (1, 1))
        put(2, pair * LANES, joined(dot32(soft.astype(BF16), d_out, (0, 0))).astype(BF16))
        product = d_probs * soft
        d_scores = []
        for head in range(2):
            block = slice(head * LANES, (head + 1) * LANES)
            summed = jnp.sum(product[:, block], axis=-1, keepdims=True)
            d_scores.append(soft[:, block] * (d_probs[:, block] - summed) * factor)
        d_scores = jnp.concatenate(d_scores, axis=1).astype(BF16)
        put(0, pair * LANES, dot32(d_scores, halves(key_ref[:, at])).astype(BF16))
        put(1, pair * LANES, joined(dot32(d_scores, query_ref[:, at], (0, 0))).astype(BF16))


def backward(place, packed, target, index, saved, readout, w_mix, shards, blocks, nodes):
    members = packed.shape[0]
    features = w_mix.shape[0]
    points = saved[0].shape[0]
    channels = padded(readout.shape[0])
    width = features // blocks
    small = 16
    return pl.pallas_call(
        functools.partial(backward_kernel, shards, blocks, nodes),
        out_shape=(
            jax.ShapeDtypeStruct((blocks, 4 * points + small, width), BF16),
        )
        + (jax.ShapeDtypeStruct((channels, features // shards), BF16),) * shards,
        in_specs=[SMEM] + [VMEM] * 10 + [ANY],
        out_specs=(VMEM,) * (1 + shards),
        scratch_shapes=[
            pltpu.VMEM((members, channels, points), BF16),
            pltpu.VMEM((points, features), BF16),
            pltpu.VMEM((small, width), F32),
            pltpu.VMEM((channels, points), F32),
            pltpu.VMEM((channels, features), BF16),
            pltpu.VMEM((features, features), BF16),
            pltpu.SemaphoreType.DMA,
        ],
        cost_estimate=pl.CostEstimate(
            flops=4 * points * features * features,
            bytes_accessed=4 * features * features,
            transcendentals=0,
        ),
        name="bwd",
    )(place, packed, target, index, *saved, readout, w_mix)


def gradient_kernel(shards, pair, members, nodes, place_ref, blocks_hbm, *refs):
    latent_refs, early_refs, late_refs, other_refs, grid_refs = (
        refs[i * shards : (i + 1) * shards] for i in range(5)
    )
    out_ref, loss_ref, blocks_ref, late_ref, node_ref, grid_ref, sems = refs[5 * shards :]
    sources = [late_refs, latent_refs, grid_refs]
    if pair > 1:
        sources = [
            late_refs + other_refs,
            latent_refs + tuple(ref.at[:nodes] for ref in early_refs),
            grid_refs + tuple(ref.at[nodes:] for ref in early_refs),
        ]
    first = pltpu.make_async_copy(blocks_hbm, blocks_ref, sems.at[0, 0])
    first.start()
    copies = []
    for i, (parts, full) in enumerate(zip(sources, (late_ref, node_ref, grid_ref))):
        step = full.shape[0] // len(parts)
        copies.append(
            [
                pltpu.make_async_copy(part, full.at[pl.ds(k * step, step)], sems.at[i + 1, k])
                for k, part in enumerate(parts)
            ]
        )
        for copy in copies[-1]:
            copy.start()
    first.wait()
    width = blocks_ref.shape[2]
    features = late_ref.shape[1]
    points = grid_ref.shape[0] // (shards * pair)
    depth = features // members
    shard, half = place_ref[0], place_ref[1]
    start = 4 * points
    total = blocks_ref[0, start:].astype(F32)
    for s in range(1, shards):
        total = total + blocks_ref[s * pair, start:].astype(F32)
    loss_ref[...] = jnp.sum(total[:3, :1], axis=0, keepdims=True)

    def slots(kind, t):
        at = slice(kind * points, (kind + 1) * points)
        return [blocks_ref[(shard ^ k) * pair + (half ^ t), at] for k in range(shards)]

    def put(kind, total):
        total = total.astype(BF16)
        at = slice(kind * width, kind * width + total.shape[0])
        for m in range(members):
            out_ref[m, at] = total[:, m * depth : (m + 1) * depth]

    def product(kind, full, group):
        left = jnp.concatenate([v for t in range(pair) for v in slots(kind, t)], axis=0)
        for copy in copies[group]:
            copy.wait()
        put(kind, dot32(left, full[...], (0, 0)))

    product(3, late_ref, 0)
    chosen = []
    for k in range(shards):
        index = blocks_ref[(shard ^ k) * pair, start : start + MISC].astype(jnp.int32)
        lines = max(points // width, 1)
        owner, offset = (
            jnp.concatenate([index[3 + b + i : 4 + b + i] for i in range(lines)], axis=1)
            for b in (0, lines)
        )
        position = (owner ^ shard) * nodes + offset
        node = lax.broadcasted_iota(jnp.int32, (nodes * shards, points), 0)
        chosen.append(jnp.where(node == position, 1.0, 0.0).astype(BF16))
    chosen = jnp.concatenate(chosen, axis=1)
    sums = []
    for t in range(pair):
        both = [jnp.concatenate(slots(kind, t), axis=0) for kind in (1, 2)]
        sums.append(dot32(chosen, jnp.concatenate(both, axis=1)).astype(BF16))
    for copy in copies[1]:
        copy.wait()
    put(1, dot32(jnp.concatenate(sums, axis=0), node_ref[...], (0, 0)))
    product(0, grid_ref, 2)


def gradients(place, blocks, latents, early, late, other, grids, members, pair):
    count, _, width = blocks.shape
    shards = count // pair
    features = late[0].shape[1]
    points = late[0].shape[0]
    depth = features // members
    return pl.pallas_call(
        functools.partial(
            gradient_kernel, shards, pair, members, latents[0].shape[0]
        ),
        out_shape=(
            jax.ShapeDtypeStruct((members, 4 * width, depth), BF16),
            jax.ShapeDtypeStruct((1, 1), F32),
        ),
        in_specs=[SMEM] + [HBM] * (1 + 5 * shards),
        out_specs=(VMEM, VMEM),
        scratch_shapes=[pltpu.VMEM(blocks.shape, BF16)]
        + [
            pltpu.VMEM((count * rows, features), BF16)
            for rows in (points, latents[0].shape[0], points)
        ]
        + [pltpu.SemaphoreType.DMA((4, count))],
        cost_estimate=pl.CostEstimate(
            flops=8 * points * count * features * width,
            bytes_accessed=8 * points * count * features,
            transcendentals=0,
        ),
        name="wgrad",
    )(place, blocks, *latents, *early, *late, *other, *grids)


def sum_kernel(pair, blocks_hbm, *refs):
    *refs, blocks_ref, sem = refs
    members, rows, _ = blocks_ref.shape
    width = rows // len(refs)
    copies = [
        pltpu.make_async_copy(blocks_hbm.at[:, pl.ds(i * width, width)], blocks_ref.at[:, pl.ds(i * width, width)], sem.at[i])
        for i in range(len(refs))
    ]
    for copy in copies:
        copy.start()
    for i, ref in enumerate(refs):
        copies[i].wait()
        at = slice(i * width, (i + 1) * width)
        for y in range(pair):
            total = blocks_ref[y, at].astype(F32)
            for m in range(y + pair, members, pair):
                total = total + blocks_ref[m, at].astype(F32)
            ref[:, y * width : (y + 1) * width] = total.T


def sum_groups(blocks, pair):
    _, rows, depth = blocks.shape
    return pl.pallas_call(
        functools.partial(sum_kernel, pair),
        out_shape=(jax.ShapeDtypeStruct((depth, pair * rows // 4), F32),) * 4,
        in_specs=[HBM],
        out_specs=(VMEM,) * 4,
        scratch_shapes=[pltpu.VMEM(blocks.shape, BF16), pltpu.SemaphoreType.DMA((4,))],
        name="sums",
    )(blocks)


def join_kernel(shard_ref, *refs):
    *slot_refs, out_ref = refs
    used, columns = out_ref.shape[0], slot_refs[0].shape[1]
    values = [ref[...].astype(F32) for ref in slot_refs]
    for s in range(len(values)):
        value = values[0]
        for k in range(1, len(values)):
            value = jnp.where((shard_ref[0] ^ k) == s, values[k], value)
        out_ref[:, s * columns : (s + 1) * columns] = value[:used]


def join_columns(shard, parts, channels_used):
    columns = parts[0].shape[1] * len(parts)
    return pl.pallas_call(
        join_kernel,
        out_shape=jax.ShapeDtypeStruct((channels_used, columns), F32),
        in_specs=[SMEM] + [VMEM] * len(parts),
        out_specs=VMEM,
        name="join",
    )(shard, *parts)


def sum_outer(parts):
    total = parts[0].astype(F32)
    received = []
    for k in range(1, len(parts)):
        received.append(swap(parts[k], "space", k))
    for value in received:
        total = total + value.astype(F32)
    total = total.astype(BF16)
    size = lax.axis_size("ens")
    for bit in [1 << i for i in range(1, size.bit_length() - 1)] + [1]:
        other = swap(total, "ens", bit)
        total = (total.astype(F32) + other.astype(F32)).astype(BF16)
    return gather_slots(total, "space")


def body(
    grid_hidden, latent, tile_neighbor_index, target, w_query, w_key, w_value, w_mix, readout_weight
):
    nodes, _ = latent.shape[1:]
    channels_used = target.shape[0]
    shards, members = lax.axis_size("space"), lax.axis_size("ens")
    shard, member = lax.axis_index("space"), lax.axis_index("ens")
    pair = 2 if members % 2 == 0 and shards <= 8 else 1
    half = member % pair
    count = shards * pair
    groups = [
        [(g + y) * shards + s for s in range(shards) for y in range(pair)]
        for g in range(0, members, pair)
    ]

    own_latent, grid_rows = latent[0], grid_hidden[0]
    latents = gather_slots(own_latent, "space")
    grids = gather_slots(grid_rows, "space")
    queries, both = project_queries(own_latent, grid_rows, w_query)
    early = latents
    if pair > 1:
        early = swap(both, "ens", 1)
        early = gather_slots(early, "space")
    *saved, packed = forward(
        shard[None],
        tile_neighbor_index,
        grid_rows,
        queries,
        readout_weight,
        latents,
        (w_key, w_value, w_mix),
        members,
    )
    keyset, valueset, soft, attended, normed, inverse = saved
    packed = lax.all_to_all(packed, "ens", split_axis=0, concat_axis=0, tiled=True)
    late = gather_slots(attended, "space")
    other = late
    if pair > 1:
        other = []
        for k, part in enumerate(late):
            other.append(swap(other[k - 1], "space", 1) if k % 2 else swap(part, "ens", 1))
    saved = (queries, keyset, valueset, soft, normed, inverse)
    blocks, *outer = backward(
        jnp.stack([shard, member]),
        packed,
        target,
        tile_neighbor_index,
        saved,
        readout_weight,
        w_mix,
        shards,
        count,
        nodes,
    )
    blocks = lax.all_to_all(
        blocks,
        ("ens", "space"),
        split_axis=0,
        concat_axis=0,
        axis_index_groups=groups,
        tiled=True,
    )
    place = jnp.stack([shard, half])
    outer = sum_outer(outer)
    blocks, loss = gradients(
        place, blocks, latents, early, late, other, grids, members, pair
    )
    blocks = lax.all_to_all(blocks, "ens", split_axis=0, concat_axis=0, tiled=True)
    grad_out = join_columns(shard[None], outer, channels_used)
    grads = sum_groups(blocks, pair)
    return (loss.reshape(()), grad_out, *grads)


def solution(mesh):
    in_specs = (
        P("ens", "space", None),
        P("ens", "space", None),
        P("space", None),
        P(None, "space"),
        P(),
        P(),
        P(),
        P(),
        P(),
    )
    out_specs = (
        P(),
        P(),
        P("ens", "space"),
        P("ens", "space"),
        P("ens", "space"),
        P("ens", "space"),
    )

    return jax.shard_map(body, mesh=mesh, in_specs=in_specs, out_specs=out_specs, check_vma=False)
```

```python
import functools

import jax
import jax.numpy as jnp
from jax import lax
from jax.experimental import pallas as pl
from jax.experimental.pallas import tpu as pltpu
from jax.sharding import PartitionSpec as P


HEADS = 16
EPS = 1e-06
SMOOTH = 0.01
LANES = 128
MISC = 8
BF16, F32 = jnp.bfloat16, jnp.float32
VMEM = pl.BlockSpec(memory_space=pltpu.VMEM)
SMEM = pl.BlockSpec(memory_space=pltpu.SMEM)
ANY = pl.BlockSpec(memory_space=pl.ANY)
HBM = pl.BlockSpec(memory_space=pltpu.HBM)


def dot32(left, right, contract=(1, 0)):
    dims = (((contract[0],), (contract[1],)), ((), ()))
    return lax.dot_general(left, right, dims, preferred_element_type=F32)


def swap(value, axis, bits):
    size = lax.axis_size(axis)
    return lax.ppermute(value, axis, [(i, i ^ bits) for i in range(size)])


def gather_slots(value, axis):
    parts = [value]
    for k in range(1, lax.axis_size(axis)):
        parts.append(swap(parts[k - 1], axis, 1) if k % 2 else swap(value, axis, k))
    return parts


def halves(pair):
    lane = lax.broadcasted_iota(jnp.int32, pair.shape, 1)
    zero = jnp.zeros_like(pair)
    first = lane < pair.shape[1] // 2
    return jnp.concatenate([jnp.where(first, pair, zero), jnp.where(first, zero, pair)], axis=0)


def joined(blocks):
    rows = blocks.shape[0] // 2
    lane = lax.broadcasted_iota(jnp.int32, (rows, blocks.shape[1]), 1)
    return jnp.where(lane < blocks.shape[1] // 2, blocks[:rows], blocks[rows:])


def query_kernel(latent_ref, rows_ref, w_hbm, out_ref, both_ref, w_ref, sem):
    chunks = w_ref.shape[0]
    step = w_ref.shape[2]
    copies = [
        pltpu.make_async_copy(w_hbm.at[:, pl.ds(c * step, step)], w_ref.at[c], sem.at[c])
        for c in range(chunks)
    ]
    for copy in copies:
        copy.start()
    nodes = latent_ref.shape[0]
    both_ref[:nodes] = latent_ref[...]
    both_ref[nodes:] = rows_ref[...]
    for c, copy in enumerate(copies):
        copy.wait()
        out_ref[:, c * step : (c + 1) * step] = dot32(rows_ref[...], w_ref[c]).astype(BF16)


def project_queries(latent, rows, weight):
    features = weight.shape[0]
    step = min(256, features)
    return pl.pallas_call(
        query_kernel,
        out_shape=(
            jax.ShapeDtypeStruct(rows.shape, BF16),
            jax.ShapeDtypeStruct((latent.shape[0] + rows.shape[0], features), BF16),
        ),
        in_specs=[VMEM, VMEM, ANY],
        out_specs=(VMEM, VMEM),
        scratch_shapes=[
            pltpu.VMEM((features // step, features, step), BF16),
            pltpu.SemaphoreType.DMA((features // step,)),
        ],
        cost_estimate=pl.CostEstimate(
            flops=2 * rows.size * features, bytes_accessed=2 * weight.size, transcendentals=0
        ),
        name="proj",
    )(latent, rows, weight)


def forward_kernel(shards, members, *refs):
    shard_ref, index_ref, grid_ref, query_ref, readout_ref = refs[:5]
    latent_refs = refs[5 : 5 + shards]
    weights_hbm = refs[5 + shards : 8 + shards]
    (
        key_hbm,
        value_hbm,
        soft_hbm,
        attended_ref,
        normed_hbm,
        inverse_ref,
        packed_ref,
        key_ref,
        value_ref,
        soft_ref,
        normed_ref,
        *w_refs,
        sem,
        out_sem,
    ) = refs[8 + shards :]
    copies = [pltpu.make_async_copy(s, d, sem.at[i]) for i, (s, d) in enumerate(zip(weights_hbm, w_refs))]
    for copy in copies:
        copy.start()
    key_copy, value_copy, normed_copy = (
        pltpu.make_async_copy(full, out, out_sem.at[i])
        for i, (full, out) in enumerate(
            ((key_ref, key_hbm), (value_ref, value_hbm), (normed_ref, normed_hbm))
        )
    )
    soft_copies = [
        pltpu.make_async_copy(soft_ref.at[i], soft_hbm.at[i], out_sem.at[3 + i])
        for i in range(soft_ref.shape[0])
    ]
    points, features = grid_ref.shape
    latents = jnp.concatenate([ref[...] for ref in latent_refs], axis=0)
    each = latent_refs[0].shape[0]
    index = index_ref[...]
    position = ((index // each) ^ shard_ref[0]) * each + index % each
    node = lax.broadcasted_iota(jnp.int32, (latents.shape[0], points), 0)
    chosen = jnp.where(node == position, 1.0, 0.0).astype(BF16)
    nodes = dot32(chosen, latents, (0, 0)).astype(BF16)
    copies[0].wait()
    key_ref[...] = dot32(nodes, w_refs[0][...]).astype(BF16)
    key_copy.start()
    copies[1].wait()
    value_ref[...] = dot32(nodes, w_refs[1][...]).astype(BF16)
    value_copy.start()
    factor = (features // HEADS) ** (-0.5)
    for pair in range(features // LANES):
        at = slice(pair * LANES, (pair + 1) * LANES)
        scores = dot32(query_ref[:, at], halves(key_ref[:, at]), (1, 1)) * factor
        soft = []
        for head in range(2):
            block = scores[:, head * LANES : (head + 1) * LANES]
            raised = jnp.exp(block - jnp.max(block, axis=-1, keepdims=True))
            soft.append(raised / jnp.sum(raised, axis=-1, keepdims=True))
        soft = jnp.concatenate(soft, axis=1)
        soft_ref[pair] = soft
        soft_copies[pair].start()
        attended_ref[:, at] = dot32(soft.astype(BF16), halves(value_ref[:, at])).astype(BF16)
    copies[2].wait()
    hidden = grid_ref[...].astype(F32) + dot32(attended_ref[...], w_refs[2][...])
    inverse = lax.rsqrt(jnp.mean(hidden * hidden, axis=-1, keepdims=True) + EPS)
    normed = hidden * inverse
    normed_ref[...] = normed
    normed_copy.start()
    inverse_ref[...] = inverse
    normed_b = normed.astype(BF16)
    forecast = dot32(readout_ref[...], normed_b, (1, 1))
    high = forecast.astype(BF16)
    low = (forecast - high.astype(F32)).astype(BF16)
    channels = packed_ref.shape[1] // 2
    spare = jnp.zeros((channels - readout_ref.shape[0], points), BF16)
    fields = jnp.concatenate([high, spare, low, spare], axis=0)
    for m in range(members):
        packed_ref[m] = fields
    for copy in (key_copy, value_copy, normed_copy, *soft_copies):
        copy.wait()


def padded(channels):
    return channels + -channels % 16


def forward(shard, index, grid_rows, queries, readout, latents, weights, members):
    points, features = grid_rows.shape
    channels = padded(readout.shape[0])
    shape = jax.ShapeDtypeStruct
    return pl.pallas_call(
        functools.partial(forward_kernel, len(latents), members),
        out_shape=(
            shape((points, features), BF16),
            shape((points, features), BF16),
            shape((features // LANES, points, 2 * LANES), F32),
            shape((points, features), BF16),
            shape((points, features), F32),
            shape((points, 1), F32),
            shape((members, 2 * channels, points), BF16),
        ),
        in_specs=[SMEM] + [VMEM] * (4 + len(latents)) + [ANY] * 3,
        out_specs=(HBM, HBM, HBM, VMEM, HBM, VMEM, VMEM),
        scratch_shapes=[
            pltpu.VMEM((points, features), BF16),
            pltpu.VMEM((points, features), BF16),
            pltpu.VMEM((features // LANES, points, 2 * LANES), F32),
            pltpu.VMEM((points, features), F32),
        ]
        + [pltpu.VMEM((features, features), BF16)] * 3
        + [
            pltpu.SemaphoreType.DMA((3,)),
            pltpu.SemaphoreType.DMA((3 + features // LANES,)),
        ],
        cost_estimate=pl.CostEstimate(
            flops=8 * points * features * features,
            bytes_accessed=6 * features * features,
            transcendentals=points * LANES * HEADS,
        ),
        name="fwd",
    )(shard, index, grid_rows, queries, readout, *latents, *weights)


def backward_kernel(
    shards,
    blocks,
    nodes,
    place_ref,
    packed_ref,
    target_ref,
    index_ref,
    query_hbm,
    key_hbm,
    value_hbm,
    soft_hbm,
    normed_hbm,
    inverse_ref,
    readout_ref,
    w_hbm,
    out_ref,
    *refs,
):
    outer_refs, refs = refs[:shards], refs[shards:]
    slope_ref, d_attended_ref, small_ref, truth_ref, weight_ref, *full_refs, sem = refs
    sources = (normed_hbm, w_hbm, value_hbm, soft_hbm, key_hbm, query_hbm)
    copies = [
        pltpu.make_async_copy(part, full, sem.at[i])
        for i, (part, full) in enumerate(zip(sources, full_refs))
    ]
    for copy in copies:
        copy.start()
    normed_ref, w_ref, value_ref, soft_ref, key_ref, query_ref = full_refs
    members = packed_ref.shape[0]
    points, features = normed_ref.shape
    channels_used = readout_ref.shape[0]
    channels = truth_ref.shape[0]
    for full, used in ((truth_ref, target_ref), (weight_ref, readout_ref)):
        full[:channels_used] = used[...]
        spare = (channels - channels_used, used.shape[1])
        full[channels_used:] = jnp.zeros(spare, used.dtype)
    width = features // blocks
    weight = (channels_used * points * shards) ** (-0.5)
    pair_weight = 1.0 / (members * (members - 1))
    chunk = 16

    def crps(c, loss):
        at = pl.ds(pl.multiple_of(c * chunk, chunk), chunk)
        low_at = pl.ds(pl.multiple_of(c * chunk + channels, chunk), chunk)
        fields = [
            packed_ref[m, at].astype(F32) + packed_ref[m, low_at].astype(F32)
            for m in range(members)
        ]
        truth = truth_ref[at]
        skill = jnp.zeros_like(truth)
        slopes = []
        for m in range(members):
            apart = fields[m] - truth
            square = apart * apart + SMOOTH
            root = lax.rsqrt(square)
            skill = skill + square * root
            slopes.append(apart * root * (weight / members))
        spread = jnp.zeros_like(truth)
        for m in range(members):
            for k in range(m):
                apart = fields[m] - fields[k]
                square = apart * apart + SMOOTH
                root = lax.rsqrt(square)
                spread = spread + square * root
                ratio = apart * root * (weight * pair_weight)
                slopes[m] = slopes[m] - ratio
                slopes[k] = slopes[k] + ratio
        for m in range(members):
            slope_ref[m, at] = slopes[m].astype(BF16)
        channel = c * chunk + lax.broadcasted_iota(jnp.int32, truth.shape, 0)
        term = skill * (1.0 / members) - spread * pair_weight
        return loss + jnp.where(channel < channels_used, term, 0.0)

    loss = lax.fori_loop(0, channels // chunk, crps, jnp.zeros((chunk, points), F32))
    loss = weight * jnp.sum(jnp.sum(loss, axis=0, keepdims=True), axis=1, keepdims=True)

    first = loss.astype(BF16).astype(F32)
    second = (loss - first).astype(BF16).astype(F32)
    for i, value in enumerate((first, second, loss - first - second)):
        small_ref[i : i + 1] = jnp.broadcast_to(value, (1, width))
    small_ref[3:] = jnp.zeros((small_ref.shape[0] - 3, width), F32)
    index = index_ref[...]
    line = 3
    for tag in (index // nodes, index % nodes):
        step = min(points, width)
        for c in range(0, points, step):
            small_ref[line : line + 1, :step] = tag[:, c : c + step].astype(F32)
            line = line + 1
    small = small_ref[...].astype(BF16)
    for b in range(blocks):
        out_ref[b, 4 * points :] = small

    def put(kind, column, value):
        step = min(width, value.shape[1])
        for c in range(0, value.shape[1], step):
            block, lane = divmod(column + c, width)
            out_ref[block, kind * points : (kind + 1) * points, lane : lane + step] = value[
                :, c : c + step
            ]

    own = slope_ref[place_ref[1]]
    copies[0].wait()
    normed = normed_ref[...]
    outer = dot32(own, normed.astype(BF16))
    columns = features // shards
    parts = [outer[:, s * columns : (s + 1) * columns] for s in range(shards)]
    for k in range(shards):
        part = parts[0]
        for s in range(1, shards):
            part = jnp.where((place_ref[0] ^ k) == s, parts[s], part)
        outer_refs[k][...] = part.astype(BF16)
    d_normed = dot32(own, weight_ref[...], (0, 0))
    mean = jnp.mean(d_normed * normed, axis=-1, keepdims=True)
    d_hidden = (inverse_ref[...] * (d_normed - normed * mean)).astype(BF16)
    put(3, 0, d_hidden)
    copies[1].wait()
    d_attended_ref[...] = dot32(d_hidden, w_ref[...], (1, 1)).astype(BF16)
    factor = (features // HEADS) ** (-0.5)
    for copy in copies[2:]:
        copy.wait()
    for pair in range(features // LANES):
        at = slice(pair * LANES, (pair + 1) * LANES)
        soft = soft_ref[pair]
        d_out = d_attended_ref[:, at]
        d_probs = dot32(d_out, halves(value_ref[:, at]), (1, 1))
        put(2, pair * LANES, joined(dot32(soft.astype(BF16), d_out, (0, 0))).astype(BF16))
        product = d_probs * soft
        d_scores = []
        for head in range(2):
            block = slice(head * LANES, (head + 1) * LANES)
            summed = jnp.sum(product[:, block], axis=-1, keepdims=True)
            d_scores.append(soft[:, block] * (d_probs[:, block] - summed) * factor)
        d_scores = jnp.concatenate(d_scores, axis=1).astype(BF16)
        put(0, pair * LANES, dot32(d_scores, halves(key_ref[:, at])).astype(BF16))
        put(1, pair * LANES, joined(dot32(d_scores, query_ref[:, at], (0, 0))).astype(BF16))


def backward(place, packed, target, index, saved, readout, w_mix, shards, blocks, nodes):
    members = packed.shape[0]
    features = w_mix.shape[0]
    points = saved[0].shape[0]
    channels = padded(readout.shape[0])
    width = features // blocks
    small = 16
    return pl.pallas_call(
        functools.partial(backward_kernel, shards, blocks, nodes),
        out_shape=(
            jax.ShapeDtypeStruct((blocks, 4 * points + small, width), BF16),
        )
        + (jax.ShapeDtypeStruct((channels, features // shards), BF16),) * shards,
        in_specs=[SMEM] + [VMEM] * 3 + [HBM] * 5 + [VMEM] * 2 + [HBM],
        out_specs=(VMEM,) * (1 + shards),
        scratch_shapes=[
            pltpu.VMEM((members, channels, points), BF16),
            pltpu.VMEM((points, features), BF16),
            pltpu.VMEM((small, width), F32),
            pltpu.VMEM((channels, points), F32),
            pltpu.VMEM((channels, features), BF16),
            pltpu.VMEM((points, features), F32),
            pltpu.VMEM((features, features), BF16),
            pltpu.VMEM((points, features), BF16),
            pltpu.VMEM((features // LANES, points, 2 * LANES), F32),
            pltpu.VMEM((points, features), BF16),
            pltpu.VMEM((points, features), BF16),
            pltpu.SemaphoreType.DMA((6,)),
        ],
        cost_estimate=pl.CostEstimate(
            flops=4 * points * features * features,
            bytes_accessed=4 * features * features,
            transcendentals=0,
        ),
        name="bwd",
    )(place, packed, target, index, *saved, readout, w_mix)


def gradient_kernel(shards, pair, members, nodes, place_ref, blocks_hbm, *refs):
    latent_refs, early_refs, late_refs, other_refs, grid_refs = (
        refs[i * shards : (i + 1) * shards] for i in range(5)
    )
    out_ref, loss_ref, blocks_ref, late_ref, node_ref, grid_ref, sems = refs[5 * shards :]
    sources = [late_refs, latent_refs, grid_refs]
    if pair > 1:
        sources = [
            late_refs + other_refs,
            latent_refs + tuple(ref.at[:nodes] for ref in early_refs),
            grid_refs + tuple(ref.at[nodes:] for ref in early_refs),
        ]
    first = pltpu.make_async_copy(blocks_hbm, blocks_ref, sems.at[0, 0])
    first.start()
    copies = []
    for i, (parts, full) in enumerate(zip(sources, (late_ref, node_ref, grid_ref))):
        step = full.shape[0] // len(parts)
        copies.append(
            [
                pltpu.make_async_copy(part, full.at[pl.ds(k * step, step)], sems.at[i + 1, k])
                for k, part in enumerate(parts)
            ]
        )
        for copy in copies[-1]:
            copy.start()
    first.wait()
    width = blocks_ref.shape[2]
    features = late_ref.shape[1]
    points = grid_ref.shape[0] // (shards * pair)
    depth = features // members
    shard, half = place_ref[0], place_ref[1]
    start = 4 * points
    total = blocks_ref[0, start:].astype(F32)
    for s in range(1, shards):
        total = total + blocks_ref[s * pair, start:].astype(F32)
    loss_ref[...] = jnp.sum(total[:3, :1], axis=0, keepdims=True)

    def slots(kind, t):
        at = slice(kind * points, (kind + 1) * points)
        return [blocks_ref[(shard ^ k) * pair + (half ^ t), at] for k in range(shards)]

    def put(kind, total):
        total = total.astype(BF16)
        at = slice(kind * width, kind * width + total.shape[0])
        for m in range(members):
            out_ref[m, at] = total[:, m * depth : (m + 1) * depth]

    def product(kind, full, group):
        left = jnp.concatenate([v for t in range(pair) for v in slots(kind, t)], axis=0)
        for copy in copies[group]:
            copy.wait()
        put(kind, dot32(left, full[...], (0, 0)))

    product(3, late_ref, 0)
    chosen = []
    for k in range(shards):
        index = blocks_ref[(shard ^ k) * pair, start : start + MISC].astype(jnp.int32)
        lines = max(points // width, 1)
        owner, offset = (
            jnp.concatenate([index[3 + b + i : 4 + b + i] for i in range(lines)], axis=1)
            for b in (0, lines)
        )
        position = (owner ^ shard) * nodes + offset
        node = lax.broadcasted_iota(jnp.int32, (nodes * shards, points), 0)
        chosen.append(jnp.where(node == position, 1.0, 0.0).astype(BF16))
    chosen = jnp.concatenate(chosen, axis=1)
    sums = []
    for t in range(pair):
        both = [jnp.concatenate(slots(kind, t), axis=0) for kind in (1, 2)]
        sums.append(dot32(chosen, jnp.concatenate(both, axis=1)).astype(BF16))
    for copy in copies[1]:
        copy.wait()
    put(1, dot32(jnp.concatenate(sums, axis=0), node_ref[...], (0, 0)))
    product(0, grid_ref, 2)


def gradients(place, blocks, latents, early, late, other, grids, members, pair):
    count, _, width = blocks.shape
    shards = count // pair
    features = late[0].shape[1]
    points = late[0].shape[0]
    depth = features // members
    return pl.pallas_call(
        functools.partial(
            gradient_kernel, shards, pair, members, latents[0].shape[0]
        ),
        out_shape=(
            jax.ShapeDtypeStruct((members, 4 * width, depth), BF16),
            jax.ShapeDtypeStruct((1, 1), F32),
        ),
        in_specs=[SMEM, ANY] + [HBM] * (5 * shards),
        out_specs=(VMEM, VMEM),
        scratch_shapes=[pltpu.VMEM(blocks.shape, BF16)]
        + [
            pltpu.VMEM((count * rows, features), BF16)
            for rows in (points, latents[0].shape[0], points)
        ]
        + [pltpu.SemaphoreType.DMA((4, count))],
        cost_estimate=pl.CostEstimate(
            flops=8 * points * count * features * width,
            bytes_accessed=8 * points * count * features,
            transcendentals=0,
        ),
        name="wgrad",
    )(place, blocks, *latents, *early, *late, *other, *grids)


def sum_kernel(pair, blocks_hbm, *refs):
    *refs, blocks_ref, sem = refs
    members, rows, _ = blocks_ref.shape
    width = rows // len(refs)
    copies = [
        pltpu.make_async_copy(blocks_hbm.at[:, pl.ds(i * width, width)], blocks_ref.at[:, pl.ds(i * width, width)], sem.at[i])
        for i in range(len(refs))
    ]
    for copy in copies:
        copy.start()
    for i, ref in enumerate(refs):
        copies[i].wait()
        at = slice(i * width, (i + 1) * width)
        for y in range(pair):
            total = blocks_ref[y, at].astype(F32)
            for m in range(y + pair, members, pair):
                total = total + blocks_ref[m, at].astype(F32)
            ref[:, y * width : (y + 1) * width] = total.T


def sum_groups(blocks, pair):
    _, rows, depth = blocks.shape
    return pl.pallas_call(
        functools.partial(sum_kernel, pair),
        out_shape=(jax.ShapeDtypeStruct((depth, pair * rows // 4), F32),) * 4,
        in_specs=[ANY],
        out_specs=(VMEM,) * 4,
        scratch_shapes=[pltpu.VMEM(blocks.shape, BF16), pltpu.SemaphoreType.DMA((4,))],
        compiler_params=pltpu.CompilerParams(vmem_limit_bytes=8 << 20),
        name="sums",
    )(blocks)


def join_kernel(shard_ref, *refs):
    *slot_refs, out_ref = refs
    used, columns = out_ref.shape[0], slot_refs[0].shape[1]
    values = [ref[...].astype(F32) for ref in slot_refs]
    for s in range(len(values)):
        value = values[0]
        for k in range(1, len(values)):
            value = jnp.where((shard_ref[0] ^ k) == s, values[k], value)
        out_ref[:, s * columns : (s + 1) * columns] = value[:used]


def join_columns(shard, parts, channels_used):
    columns = parts[0].shape[1] * len(parts)
    return pl.pallas_call(
        join_kernel,
        out_shape=jax.ShapeDtypeStruct((channels_used, columns), F32),
        in_specs=[SMEM] + [VMEM] * len(parts),
        out_specs=VMEM,
        name="join",
    )(shard, *parts)


def sum_outer(parts):
    total = parts[0].astype(F32)
    received = []
    for k in range(1, len(parts)):
        received.append(swap(parts[k], "space", k))
    for value in received:
        total = total + value.astype(F32)
    total = total.astype(BF16)
    size = lax.axis_size("ens")
    for bit in [1 << i for i in range(1, size.bit_length() - 1)] + [1]:
        other = swap(total, "ens", bit)
        total = (total.astype(F32) + other.astype(F32)).astype(BF16)
    return gather_slots(total, "space")


def body(
    grid_hidden, latent, tile_neighbor_index, target, w_query, w_key, w_value, w_mix, readout_weight
):
    nodes, _ = latent.shape[1:]
    channels_used = target.shape[0]
    shards, members = lax.axis_size("space"), lax.axis_size("ens")
    shard, member = lax.axis_index("space"), lax.axis_index("ens")
    pair = 2 if members % 2 == 0 and shards <= 8 else 1
    half = member % pair
    count = shards * pair
    groups = [
        [(g + y) * shards + s for s in range(shards) for y in range(pair)]
        for g in range(0, members, pair)
    ]

    own_latent, grid_rows = latent[0], grid_hidden[0]
    latents = gather_slots(own_latent, "space")
    grids = gather_slots(grid_rows, "space")
    queries, both = project_queries(own_latent, grid_rows, w_query)
    early = latents
    if pair > 1:
        early = swap(both, "ens", 1)
        early = gather_slots(early, "space")
    *saved, packed = forward(
        shard[None],
        tile_neighbor_index,
        grid_rows,
        queries,
        readout_weight,
        latents,
        (w_key, w_value, w_mix),
        members,
    )
    keyset, valueset, soft, attended, normed, inverse = saved
    packed = lax.all_to_all(packed, "ens", split_axis=0, concat_axis=0, tiled=True)
    late = gather_slots(attended, "space")
    other = late
    if pair > 1:
        other = []
        for k, part in enumerate(late):
            other.append(swap(other[k - 1], "space", 1) if k % 2 else swap(part, "ens", 1))
    saved = (queries, keyset, valueset, soft, normed, inverse)
    blocks, *outer = backward(
        jnp.stack([shard, member]),
        packed,
        target,
        tile_neighbor_index,
        saved,
        readout_weight,
        w_mix,
        shards,
        count,
        nodes,
    )
    blocks = lax.all_to_all(
        blocks,
        ("ens", "space"),
        split_axis=0,
        concat_axis=0,
        axis_index_groups=groups,
        tiled=True,
    )
    place = jnp.stack([shard, half])
    outer = sum_outer(outer)
    blocks, loss = gradients(
        place, blocks, latents, early, late, other, grids, members, pair
    )
    blocks = lax.all_to_all(blocks, "ens", split_axis=0, concat_axis=0, tiled=True)
    grad_out = join_columns(shard[None], outer, channels_used)
    grads = sum_groups(blocks, pair)
    return (loss.reshape(()), grad_out, *grads)


def solution(mesh):
    in_specs = (
        P("ens", "space", None),
        P("ens", "space", None),
        P("space", None),
        P(None, "space"),
        P(),
        P(),
        P(),
        P(),
        P(),
    )
    out_specs = (
        P(),
        P(),
        P("ens", "space"),
        P("ens", "space"),
        P("ens", "space"),
        P("ens", "space"),
    )

    return jax.shard_map(body, mesh=mesh, in_specs=in_specs, out_specs=out_specs, check_vma=False)
```

```python
import functools

import jax
import jax.numpy as jnp
from jax import lax
from jax.experimental import pallas as pl
from jax.experimental.pallas import tpu as pltpu
from jax.sharding import PartitionSpec as P


HEADS = 16
EPS = 1e-06
SMOOTH = 0.01
LANES = 128
MISC = 8
BF16, F32 = jnp.bfloat16, jnp.float32
VMEM = pl.BlockSpec(memory_space=pltpu.VMEM)
SMEM = pl.BlockSpec(memory_space=pltpu.SMEM)
ANY = pl.BlockSpec(memory_space=pl.ANY)
HBM = pl.BlockSpec(memory_space=pltpu.HBM)


def dot32(left, right, contract=(1, 0)):
    dims = (((contract[0],), (contract[1],)), ((), ()))
    return lax.dot_general(left, right, dims, preferred_element_type=F32)


def swap(value, axis, bits):
    size = lax.axis_size(axis)
    return lax.ppermute(value, axis, [(i, i ^ bits) for i in range(size)])


def gather_slots(value, axis):
    parts = [value]
    for k in range(1, lax.axis_size(axis)):
        parts.append(swap(parts[k - 1], axis, 1) if k % 2 else swap(value, axis, k))
    return parts


def halves(pair):
    lane = lax.broadcasted_iota(jnp.int32, pair.shape, 1)
    zero = jnp.zeros_like(pair)
    first = lane < pair.shape[1] // 2
    return jnp.concatenate([jnp.where(first, pair, zero), jnp.where(first, zero, pair)], axis=0)


def joined(blocks):
    rows = blocks.shape[0] // 2
    lane = lax.broadcasted_iota(jnp.int32, (rows, blocks.shape[1]), 1)
    return jnp.where(lane < blocks.shape[1] // 2, blocks[:rows], blocks[rows:])


def query_kernel(latent_ref, rows_ref, w_hbm, out_ref, both_ref, w_ref, sem):
    chunks = w_ref.shape[0]
    step = w_ref.shape[2]
    copies = [
        pltpu.make_async_copy(w_hbm.at[:, pl.ds(c * step, step)], w_ref.at[c], sem.at[c])
        for c in range(chunks)
    ]
    for copy in copies:
        copy.start()
    nodes = latent_ref.shape[0]
    both_ref[:nodes] = latent_ref[...]
    both_ref[nodes:] = rows_ref[...]
    for c, copy in enumerate(copies):
        copy.wait()
        out_ref[:, c * step : (c + 1) * step] = dot32(rows_ref[...], w_ref[c]).astype(BF16)


def project_queries(latent, rows, weight):
    features = weight.shape[0]
    step = min(256, features)
    return pl.pallas_call(
        query_kernel,
        out_shape=(
            jax.ShapeDtypeStruct(rows.shape, BF16),
            jax.ShapeDtypeStruct((latent.shape[0] + rows.shape[0], features), BF16),
        ),
        in_specs=[VMEM, VMEM, ANY],
        out_specs=(VMEM, VMEM),
        scratch_shapes=[
            pltpu.VMEM((features // step, features, step), BF16),
            pltpu.SemaphoreType.DMA((features // step,)),
        ],
        cost_estimate=pl.CostEstimate(
            flops=2 * rows.size * features, bytes_accessed=2 * weight.size, transcendentals=0
        ),
        name="proj",
    )(latent, rows, weight)


def forward_kernel(shards, members, *refs):
    shard_ref, index_ref, grid_ref, query_ref, readout_ref = refs[:5]
    latent_refs = refs[5 : 5 + shards]
    weights_hbm = refs[5 + shards : 8 + shards]
    (
        key_ref,
        value_ref,
        soft_ref,
        attended_ref,
        normed_ref,
        inverse_ref,
        packed_ref,
        *w_refs,
        sem,
    ) = refs[8 + shards :]
    copies = [pltpu.make_async_copy(s, d, sem.at[i]) for i, (s, d) in enumerate(zip(weights_hbm, w_refs))]
    for copy in copies:
        copy.start()
    points, features = grid_ref.shape
    latents = jnp.concatenate([ref[...] for ref in latent_refs], axis=0)
    each = latent_refs[0].shape[0]
    index = index_ref[...]
    position = ((index // each) ^ shard_ref[0]) * each + index % each
    node = lax.broadcasted_iota(jnp.int32, (latents.shape[0], points), 0)
    chosen = jnp.where(node == position, 1.0, 0.0).astype(BF16)
    nodes = dot32(chosen, latents, (0, 0)).astype(BF16)
    copies[0].wait()
    key_ref[...] = dot32(nodes, w_refs[0][...]).astype(BF16)
    copies[1].wait()
    value_ref[...] = dot32(nodes, w_refs[1][...]).astype(BF16)
    factor = (features // HEADS) ** (-0.5)
    for pair in range(features // LANES):
        at = slice(pair * LANES, (pair + 1) * LANES)
        scores = dot32(query_ref[:, at], halves(key_ref[:, at]), (1, 1)) * factor
        soft = []
        for head in range(2):
            block = scores[:, head * LANES : (head + 1) * LANES]
            raised = jnp.exp(block - jnp.max(block, axis=-1, keepdims=True))
            soft.append(raised / jnp.sum(raised, axis=-1, keepdims=True))
        soft = jnp.concatenate(soft, axis=1)
        soft_ref[pair] = soft
        attended_ref[:, at] = dot32(soft.astype(BF16), halves(value_ref[:, at])).astype(BF16)
    copies[2].wait()
    hidden = grid_ref[...].astype(F32) + dot32(attended_ref[...], w_refs[2][...])
    inverse = lax.rsqrt(jnp.mean(hidden * hidden, axis=-1, keepdims=True) + EPS)
    normed = hidden * inverse
    normed_ref[...] = normed
    inverse_ref[...] = inverse
    normed_b = normed.astype(BF16)
    forecast = dot32(readout_ref[...], normed_b, (1, 1))
    high = forecast.astype(BF16)
    low = (forecast - high.astype(F32)).astype(BF16)
    channels = packed_ref.shape[1] // 2
    spare = jnp.zeros((channels - readout_ref.shape[0], points), BF16)
    fields = jnp.concatenate([high, spare, low, spare], axis=0)
    for m in range(members):
        packed_ref[m] = fields


def padded(channels):
    return channels + -channels % 8


def forward(shard, index, grid_rows, queries, readout, latents, weights, members):
    points, features = grid_rows.shape
    channels = padded(readout.shape[0])
    shape = jax.ShapeDtypeStruct
    return pl.pallas_call(
        functools.partial(forward_kernel, len(latents), members),
        out_shape=(
            shape((points, features), BF16),
            shape((points, features), BF16),
            shape((features // LANES, points, 2 * LANES), F32),
            shape((points, features), BF16),
            shape((points, features), F32),
            shape((points, 1), F32),
            shape((members, 2 * channels, points), BF16),
        ),
        in_specs=[SMEM] + [VMEM] * (4 + len(latents)) + [ANY] * 3,
        out_specs=(VMEM,) * 7,
        scratch_shapes=[pltpu.VMEM((features, features), BF16)] * 3
        + [pltpu.SemaphoreType.DMA((3,))],
        cost_estimate=pl.CostEstimate(
            flops=8 * points * features * features,
            bytes_accessed=6 * features * features,
            transcendentals=points * LANES * HEADS,
        ),
        name="fwd",
    )(shard, index, grid_rows, queries, readout, *latents, *weights)


def backward_kernel(
    shards,
    blocks,
    nodes,
    place_ref,
    packed_ref,
    target_ref,
    index_ref,
    query_hbm,
    key_hbm,
    value_hbm,
    soft_hbm,
    normed_hbm,
    inverse_ref,
    readout_ref,
    w_hbm,
    out_ref,
    *refs,
):
    outer_refs, refs = refs[:shards], refs[shards:]
    slope_ref, d_attended_ref, small_ref, truth_ref, weight_ref, *full_refs, sem = refs
    sources = (normed_hbm, w_hbm, value_hbm, soft_hbm, key_hbm, query_hbm)
    copies = [
        pltpu.make_async_copy(part, full, sem.at[i])
        for i, (part, full) in enumerate(zip(sources, full_refs))
    ]
    for copy in copies:
        copy.start()
    normed_ref, w_ref, value_ref, soft_ref, key_ref, query_ref = full_refs
    members = packed_ref.shape[0]
    points, features = normed_ref.shape
    channels_used = readout_ref.shape[0]
    channels = truth_ref.shape[0]
    for full, used in ((truth_ref, target_ref), (weight_ref, readout_ref)):
        full[:channels_used] = used[...]
        spare = (channels - channels_used, used.shape[1])
        full[channels_used:] = jnp.zeros(spare, used.dtype)
    width = features // blocks
    weight = (channels_used * points * shards) ** (-0.5)
    pair_weight = 1.0 / (members * (members - 1))
    chunk = 8

    def crps(c, loss):
        at = pl.ds(pl.multiple_of(c * chunk, chunk), chunk)
        low_at = pl.ds(pl.multiple_of(c * chunk + channels, chunk), chunk)
        fields = [
            packed_ref[m, at].astype(F32) + packed_ref[m, low_at].astype(F32)
            for m in range(members)
        ]
        truth = truth_ref[at]
        skill = jnp.zeros_like(truth)
        slopes = []
        for m in range(members):
            apart = fields[m] - truth
            square = apart * apart + SMOOTH
            root = lax.rsqrt(square)
            skill = skill + square * root
            slopes.append(apart * root * (weight / members))
        spread = jnp.zeros_like(truth)
        for m in range(members):
            for k in range(m):
                apart = fields[m] - fields[k]
                square = apart * apart + SMOOTH
                root = lax.rsqrt(square)
                spread = spread + square * root
                ratio = apart * root * (weight * pair_weight)
                slopes[m] = slopes[m] - ratio
                slopes[k] = slopes[k] + ratio
        for m in range(members):
            slope_ref[m, at] = slopes[m].astype(BF16)
        channel = c * chunk + lax.broadcasted_iota(jnp.int32, truth.shape, 0)
        term = skill * (1.0 / members) - spread * pair_weight
        return loss + jnp.where(channel < channels_used, term, 0.0)

    loss = lax.fori_loop(0, channels // chunk, crps, jnp.zeros((chunk, points), F32))
    loss = weight * jnp.sum(jnp.sum(loss, axis=0, keepdims=True), axis=1, keepdims=True)

    first = loss.astype(BF16).astype(F32)
    second = (loss - first).astype(BF16).astype(F32)
    for i, value in enumerate((first, second, loss - first - second)):
        small_ref[i : i + 1] = jnp.broadcast_to(value, (1, width))
    small_ref[3:] = jnp.zeros((small_ref.shape[0] - 3, width), F32)
    index = index_ref[...]
    line = 3
    for tag in (index // nodes, index % nodes):
        step = min(points, width)
        for c in range(0, points, step):
            small_ref[line : line + 1, :step] = tag[:, c : c + step].astype(F32)
            line = line + 1
    small = small_ref[...].astype(BF16)
    for b in range(blocks):
        out_ref[b, 4 * points :] = small

    def put(kind, column, value):
        step = min(width, value.shape[1])
        for c in range(0, value.shape[1], step):
            block, lane = divmod(column + c, width)
            out_ref[block, kind * points : (kind + 1) * points, lane : lane + step] = value[
                :, c : c + step
            ]

    own = slope_ref[place_ref[1]]
    copies[0].wait()
    normed = normed_ref[...]
    outer = dot32(own, normed.astype(BF16))
    columns = features // shards
    parts = [outer[:, s * columns : (s + 1) * columns] for s in range(shards)]
    for k in range(shards):
        part = parts[0]
        for s in range(1, shards):
            part = jnp.where((place_ref[0] ^ k) == s, parts[s], part)
        outer_refs[k][...] = part.astype(BF16)
    d_normed = dot32(own, weight_ref[...], (0, 0))
    mean = jnp.mean(d_normed * normed, axis=-1, keepdims=True)
    d_hidden = (inverse_ref[...] * (d_normed - normed * mean)).astype(BF16)
    put(3, 0, d_hidden)
    copies[1].wait()
    d_attended_ref[...] = dot32(d_hidden, w_ref[...], (1, 1)).astype(BF16)
    factor = (features // HEADS) ** (-0.5)
    for copy in copies[2:]:
        copy.wait()
    for pair in range(features // LANES):
        at = slice(pair * LANES, (pair + 1) * LANES)
        soft = soft_ref[pair]
        d_out = d_attended_ref[:, at]
        d_probs = dot32(d_out, halves(value_ref[:, at]), (1, 1))
        put(2, pair * LANES, joined(dot32(soft.astype(BF16), d_out, (0, 0))).astype(BF16))
        product = d_probs * soft
        d_scores = []
        for head in range(2):
            block = slice(head * LANES, (head + 1) * LANES)
            summed = jnp.sum(product[:, block], axis=-1, keepdims=True)
            d_scores.append(soft[:, block] * (d_probs[:, block] - summed) * factor)
        d_scores = jnp.concatenate(d_scores, axis=1).astype(BF16)
        put(0, pair * LANES, dot32(d_scores, halves(key_ref[:, at])).astype(BF16))
        put(1, pair * LANES, joined(dot32(d_scores, query_ref[:, at], (0, 0))).astype(BF16))


def backward(place, packed, target, index, saved, readout, w_mix, shards, blocks, nodes):
    members = packed.shape[0]
    features = w_mix.shape[0]
    points = saved[0].shape[0]
    channels = padded(readout.shape[0])
    width = features // blocks
    small = 16
    return pl.pallas_call(
        functools.partial(backward_kernel, shards, blocks, nodes),
        out_shape=(
            jax.ShapeDtypeStruct((blocks, 4 * points + small, width), BF16),
        )
        + (jax.ShapeDtypeStruct((channels, features // shards), BF16),) * shards,
        in_specs=[SMEM] + [VMEM] * 3 + [HBM] * 5 + [VMEM] * 2 + [HBM],
        out_specs=(VMEM,) * (1 + shards),
        scratch_shapes=[
            pltpu.VMEM((members, channels, points), BF16),
            pltpu.VMEM((points, features), BF16),
            pltpu.VMEM((small, width), F32),
            pltpu.VMEM((channels, points), F32),
            pltpu.VMEM((channels, features), BF16),
            pltpu.VMEM((points, features), F32),
            pltpu.VMEM((features, features), BF16),
            pltpu.VMEM((points, features), BF16),
            pltpu.VMEM((features // LANES, points, 2 * LANES), F32),
            pltpu.VMEM((points, features), BF16),
            pltpu.VMEM((points, features), BF16),
            pltpu.SemaphoreType.DMA((6,)),
        ],
        cost_estimate=pl.CostEstimate(
            flops=4 * points * features * features,
            bytes_accessed=4 * features * features,
            transcendentals=0,
        ),
        name="bwd",
    )(place, packed, target, index, *saved, readout, w_mix)


def fetch(parts, full_ref, sems):
    step = full_ref.shape[0] // len(parts)
    copies = [
        pltpu.make_async_copy(part, full_ref.at[pl.ds(k * step, step)], sems.at[k])
        for k, part in enumerate(parts)
    ]
    for copy in copies:
        copy.start()
    return copies


def in_slots(blocks_ref, place_ref, pair, kind, points):
    at = slice(kind * points, (kind + 1) * points)
    return [
        blocks_ref[(place_ref[0] ^ k) * pair + (place_ref[1] ^ t), at]
        for t in range(pair)
        for k in range(blocks_ref.shape[0] // pair)
    ]


def chosen_nodes(tags_ref, place_ref, pair, start, nodes, points):
    shards = tags_ref.shape[0] // pair
    lines = max(points // tags_ref.shape[2], 1)
    chosen = []
    for k in range(shards):
        at = slice(start, start + MISC)
        index = tags_ref[(place_ref[0] ^ k) * pair, at].astype(jnp.int32)
        owner, offset = (
            jnp.concatenate([index[3 + b + i : 4 + b + i] for i in range(lines)], axis=1)
            for b in (0, lines)
        )
        position = (owner ^ place_ref[0]) * nodes + offset
        node = lax.broadcasted_iota(jnp.int32, (nodes * shards, points), 0)
        chosen.append(jnp.where(node == position, 1.0, 0.0).astype(BF16))
    return jnp.concatenate(chosen, axis=1)


def node_sums(lefts, chosen, shards):
    sums = [
        dot32(chosen, jnp.concatenate(lefts[t : t + shards], axis=0)).astype(BF16)
        for t in range(0, len(lefts), shards)
    ]
    return jnp.concatenate(sums, axis=0)


def put_members(out_ref, kind, total):
    width, depth = total.shape[0], out_ref.shape[2]
    total = total.astype(BF16)
    for m in range(out_ref.shape[0]):
        out_ref[m, kind * width : (kind + 1) * width] = total[:, m * depth : (m + 1) * depth]


def first_kernel(shards, pair, nodes, points, place_ref, blocks_hbm, *refs):
    latent_refs, early_refs, late_refs, other_refs = (
        refs[i * shards : (i + 1) * shards] for i in range(4)
    )
    out_ref, loss_ref, blocks_ref, late_ref, node_ref, sems = refs[4 * shards :]
    head = 2 * points
    used = pl.ds(head, blocks_hbm.shape[1] - head)
    first = pltpu.make_async_copy(blocks_hbm.at[:, used], blocks_ref, sems.at[0, 0])
    first.start()
    late_parts, node_parts = late_refs, latent_refs
    if pair > 1:
        late_parts = late_refs + other_refs
        node_parts = latent_refs + tuple(ref.at[:nodes] for ref in early_refs)
    late_copies = fetch(late_parts, late_ref, sems.at[1])
    node_copies = fetch(node_parts, node_ref, sems.at[2])
    first.wait()
    total = blocks_ref[0, head:].astype(F32)
    for s in range(1, shards):
        total = total + blocks_ref[s * pair, head:].astype(F32)
    loss_ref[...] = jnp.sum(total[:3, :1], axis=0, keepdims=True)
    left = jnp.concatenate(in_slots(blocks_ref, place_ref, pair, 1, points), axis=0)
    for copy in late_copies:
        copy.wait()
    put_members(out_ref, 0, dot32(left, late_ref[...], (0, 0)))
    chosen = chosen_nodes(blocks_ref, place_ref, pair, head, nodes, points)
    left = node_sums(in_slots(blocks_ref, place_ref, pair, 0, points), chosen, shards)
    for copy in node_copies:
        copy.wait()
    put_members(out_ref, 1, dot32(left, node_ref[...], (0, 0)))


def first_gradients(place, blocks, latents, early, late, other, members, pair):
    count, rows, width = blocks.shape
    shards = count // pair
    points, features = late[0].shape
    nodes = latents[0].shape[0]
    return pl.pallas_call(
        functools.partial(first_kernel, shards, pair, nodes, points),
        out_shape=(
            jax.ShapeDtypeStruct((members, 2 * width, features // members), BF16),
            jax.ShapeDtypeStruct((1, 1), F32),
        ),
        in_specs=[SMEM] + [HBM] * (1 + 4 * shards),
        out_specs=(VMEM, VMEM),
        scratch_shapes=[
            pltpu.VMEM((count, rows - 2 * points, width), BF16),
            pltpu.VMEM((count * points, features), BF16),
            pltpu.VMEM((count * nodes, features), BF16),
            pltpu.SemaphoreType.DMA((3, count)),
        ],
        cost_estimate=pl.CostEstimate(
            flops=4 * points * count * features * width,
            bytes_accessed=4 * points * count * features,
            transcendentals=0,
        ),
        name="wga",
    )(place, blocks, *latents, *early, *late, *other)


def last_kernel(shards, pair, nodes, points, place_ref, blocks_hbm, *refs):
    latent_refs, early_refs, grid_refs = (refs[i * shards : (i + 1) * shards] for i in range(3))
    *out_refs, total_ref, blocks_ref, tags_ref, node_ref, grid_ref, sems = refs[3 * shards :]
    start = 4 * points
    copies = [
        pltpu.make_async_copy(blocks_hbm.at[:, pl.ds(at, rows)], full, sems.at[0, i])
        for i, (full, at, rows) in enumerate(
            ((blocks_ref, 0, 2 * points), (tags_ref, start, tags_ref.shape[1]))
        )
    ]
    for copy in copies:
        copy.start()
    node_parts, grid_parts = latent_refs, grid_refs
    if pair > 1:
        node_parts = latent_refs + tuple(ref.at[:nodes] for ref in early_refs)
        grid_parts = grid_refs + tuple(ref.at[nodes:] for ref in early_refs)
    grid_copies = fetch(grid_parts, grid_ref, sems.at[1])
    node_copies = fetch(node_parts, node_ref, sems.at[2])
    for copy in copies:
        copy.wait()
    left = jnp.concatenate(in_slots(blocks_ref, place_ref, pair, 0, points), axis=0)
    for copy in grid_copies:
        copy.wait()
    put_members(total_ref, 0, dot32(left, grid_ref[...], (0, 0)))
    chosen = chosen_nodes(tags_ref, place_ref, pair, 0, nodes, points)
    left = node_sums(in_slots(blocks_ref, place_ref, pair, 1, points), chosen, shards)
    for copy in node_copies:
        copy.wait()
    put_members(total_ref, 1, dot32(left, node_ref[...], (0, 0)))
    for k, ref in enumerate(out_refs):
        ref[...] = total_ref[place_ref[2] ^ k]


def last_gradients(place, blocks, latents, early, grids, members, pair):
    count, rows, width = blocks.shape
    shards = count // pair
    points, features = grids[0].shape
    nodes = latents[0].shape[0]
    block = (2 * width, features // members)
    return pl.pallas_call(
        functools.partial(last_kernel, shards, pair, nodes, points),
        out_shape=(jax.ShapeDtypeStruct(block, BF16),) * members,
        in_specs=[SMEM] + [HBM] * (1 + 3 * shards),
        out_specs=(VMEM,) * members,
        scratch_shapes=[
            pltpu.VMEM((members,) + block, BF16),
            pltpu.VMEM((count, 2 * points, width), BF16),
            pltpu.VMEM((count, rows - 4 * points, width), BF16),
            pltpu.VMEM((count * nodes, features), BF16),
            pltpu.VMEM((count * points, features), BF16),
            pltpu.SemaphoreType.DMA((3, count)),
        ],
        cost_estimate=pl.CostEstimate(
            flops=4 * points * count * features * width,
            bytes_accessed=4 * points * count * features,
            transcendentals=0,
        ),
        name="wgb",
    )(place, blocks, *latents, *early, *grids)


def sum_kernel(pair, blocks_hbm, *refs):
    *refs, blocks_ref, sem = refs
    members, rows, _ = blocks_ref.shape
    width = rows // len(refs)
    copies = [
        pltpu.make_async_copy(blocks_hbm.at[:, pl.ds(i * width, width)], blocks_ref.at[:, pl.ds(i * width, width)], sem.at[i])
        for i in range(len(refs))
    ]
    for copy in copies:
        copy.start()
    for i, ref in enumerate(refs):
        copies[i].wait()
        at = slice(i * width, (i + 1) * width)
        for y in range(pair):
            total = blocks_ref[y, at].astype(F32)
            for m in range(y + pair, members, pair):
                total = total + blocks_ref[m, at].astype(F32)
            ref[:, y * width : (y + 1) * width] = total.T


def sum_groups(blocks, pair):
    _, rows, depth = blocks.shape
    return pl.pallas_call(
        functools.partial(sum_kernel, pair),
        out_shape=(jax.ShapeDtypeStruct((depth, pair * rows // 2), F32),) * 2,
        in_specs=[ANY],
        out_specs=(VMEM,) * 2,
        scratch_shapes=[pltpu.VMEM(blocks.shape, BF16), pltpu.SemaphoreType.DMA((2,))],
        compiler_params=pltpu.CompilerParams(vmem_limit_bytes=8 << 20),
        name="sums",
    )(blocks)


def sum_slots_kernel(pair, place_ref, *refs):
    slot_refs, out_refs = refs[:-2], refs[-2:]
    width = slot_refs[0].shape[0] // 2
    for i, ref in enumerate(out_refs):
        at = slice(i * width, (i + 1) * width)
        totals = []
        for y in range(pair):
            total = slot_refs[y][at].astype(F32)
            for k in range(y + pair, len(slot_refs), pair):
                total = total + slot_refs[k][at].astype(F32)
            totals.append(total.T)
        for y in range(pair):
            value = totals[y]
            if pair > 1:
                value = jnp.where(place_ref[1] == y, totals[0], totals[1])
            ref[:, y * width : (y + 1) * width] = value


def sum_slots(place, parts, pair):
    rows, depth = parts[0].shape
    return pl.pallas_call(
        functools.partial(sum_slots_kernel, pair),
        out_shape=(jax.ShapeDtypeStruct((depth, pair * rows // 2), F32),) * 2,
        in_specs=[SMEM] + [VMEM] * len(parts),
        out_specs=(VMEM,) * 2,
        compiler_params=pltpu.CompilerParams(vmem_limit_bytes=8 << 20),
        name="sumb",
    )(place, *parts)


def join_kernel(shard_ref, *refs):
    *slot_refs, out_ref = refs
    used, columns = out_ref.shape[0], slot_refs[0].shape[1]
    values = [ref[...].astype(F32) for ref in slot_refs]
    for s in range(len(values)):
        value = values[0]
        for k in range(1, len(values)):
            value = jnp.where((shard_ref[0] ^ k) == s, values[k], value)
        out_ref[:, s * columns : (s + 1) * columns] = value[:used]


def join_columns(shard, parts, channels_used):
    columns = parts[0].shape[1] * len(parts)
    return pl.pallas_call(
        join_kernel,
        out_shape=jax.ShapeDtypeStruct((channels_used, columns), F32),
        in_specs=[SMEM] + [VMEM] * len(parts),
        out_specs=VMEM,
        compiler_params=pltpu.CompilerParams(vmem_limit_bytes=6 << 20),
        name="join",
    )(shard, *parts)


def sum_outer(parts):
    total = parts[0].astype(F32)
    received = []
    for k in range(1, len(parts)):
        received.append(swap(parts[k], "space", k))
    for value in received:
        total = total + value.astype(F32)
    total = total.astype(BF16)
    size = lax.axis_size("ens")
    for bit in [1 << i for i in range(1, size.bit_length() - 1)] + [1]:
        other = swap(total, "ens", bit)
        total = (total.astype(F32) + other.astype(F32)).astype(BF16)
    return gather_slots(total, "space")


def body(
    grid_hidden, latent, tile_neighbor_index, target, w_query, w_key, w_value, w_mix, readout_weight
):
    nodes, _ = latent.shape[1:]
    channels_used = target.shape[0]
    shards, members = lax.axis_size("space"), lax.axis_size("ens")
    shard, member = lax.axis_index("space"), lax.axis_index("ens")
    pair = 2 if members % 2 == 0 and shards <= 8 else 1
    half = member % pair
    count = shards * pair
    groups = [
        [(g + y) * shards + s for s in range(shards) for y in range(pair)]
        for g in range(0, members, pair)
    ]

    own_latent, grid_rows = latent[0], grid_hidden[0]
    latents = gather_slots(own_latent, "space")
    grids = gather_slots(grid_rows, "space")
    queries, both = project_queries(own_latent, grid_rows, w_query)
    early = latents
    if pair > 1:
        early = swap(both, "ens", 1)
        early = gather_slots(early, "space")
    *saved, packed = forward(
        shard[None],
        tile_neighbor_index,
        grid_rows,
        queries,
        readout_weight,
        latents,
        (w_key, w_value, w_mix),
        members,
    )
    keyset, valueset, soft, attended, normed, inverse = saved
    packed = lax.all_to_all(packed, "ens", split_axis=0, concat_axis=0, tiled=True)
    late = gather_slots(attended, "space")
    other = late
    if pair > 1:
        other = []
        for k, part in enumerate(late):
            other.append(swap(other[k - 1], "space", 1) if k % 2 else swap(part, "ens", 1))
    saved = (queries, keyset, valueset, soft, normed, inverse)
    blocks, *outer = backward(
        jnp.stack([shard, member]),
        packed,
        target,
        tile_neighbor_index,
        saved,
        readout_weight,
        w_mix,
        shards,
        count,
        nodes,
    )
    blocks = lax.all_to_all(
        blocks,
        ("ens", "space"),
        split_axis=0,
        concat_axis=0,
        axis_index_groups=groups,
        tiled=True,
    )
    place = jnp.stack([shard, half, member])
    outer = sum_outer(outer)
    first, loss = first_gradients(place, blocks, latents, early, late, other, members, pair)
    first = lax.all_to_all(first, "ens", split_axis=0, concat_axis=0, tiled=True)
    parts = last_gradients(place, blocks, latents, early, grids, members, pair)
    last = [parts[0]]
    for k in range(1, members):
        last.append(swap(parts[k], "ens", k))
    grad_out = join_columns(shard[None], outer, channels_used)
    grad_mix, grad_value = sum_groups(first, pair)
    grad_query, grad_key = sum_slots(place, last, pair)
    return (loss.reshape(()), grad_out, grad_query, grad_key, grad_value, grad_mix)


def solution(mesh):
    in_specs = (
        P("ens", "space", None),
        P("ens", "space", None),
        P("space", None),
        P(None, "space"),
        P(),
        P(),
        P(),
        P(),
        P(),
    )
    out_specs = (
        P(),
        P(),
        P("ens", "space"),
        P("ens", "space"),
        P("ens", "space"),
        P("ens", "space"),
    )

    return jax.shard_map(body, mesh=mesh, in_specs=in_specs, out_specs=out_specs, check_vma=False)
```

```python
import functools

import jax
import jax.numpy as jnp
from jax import lax
from jax.experimental import pallas as pl
from jax.experimental.pallas import tpu as pltpu
from jax.sharding import PartitionSpec as P


HEADS = 16
EPS = 1e-06
SMOOTH = 0.01
LANES = 128
MISC = 8
BF16, F32 = jnp.bfloat16, jnp.float32
VMEM = pl.BlockSpec(memory_space=pltpu.VMEM)
SMEM = pl.BlockSpec(memory_space=pltpu.SMEM)
ANY = pl.BlockSpec(memory_space=pl.ANY)
HBM = pl.BlockSpec(memory_space=pltpu.HBM)


def dot32(left, right, contract=(1, 0)):
    dims = (((contract[0],), (contract[1],)), ((), ()))
    return lax.dot_general(left, right, dims, preferred_element_type=F32)


def swap(value, axis, bits):
    size = lax.axis_size(axis)
    return lax.ppermute(value, axis, [(i, i ^ bits) for i in range(size)])


def gather_slots(value, axis):
    parts = [value]
    for k in range(1, lax.axis_size(axis)):
        parts.append(swap(parts[k - 1], axis, 1) if k % 2 else swap(value, axis, k))
    return parts


def halves(pair):
    lane = lax.broadcasted_iota(jnp.int32, pair.shape, 1)
    zero = jnp.zeros_like(pair)
    first = lane < pair.shape[1] // 2
    return jnp.concatenate([jnp.where(first, pair, zero), jnp.where(first, zero, pair)], axis=0)


def joined(blocks):
    rows = blocks.shape[0] // 2
    lane = lax.broadcasted_iota(jnp.int32, (rows, blocks.shape[1]), 1)
    return jnp.where(lane < blocks.shape[1] // 2, blocks[:rows], blocks[rows:])


def query_kernel(latent_ref, rows_ref, w_hbm, out_ref, both_ref, w_ref, sem):
    chunks = w_ref.shape[0]
    step = w_ref.shape[2]
    copies = [
        pltpu.make_async_copy(w_hbm.at[:, pl.ds(c * step, step)], w_ref.at[c], sem.at[c])
        for c in range(chunks)
    ]
    for copy in copies:
        copy.start()
    nodes = latent_ref.shape[0]
    both_ref[:nodes] = latent_ref[...]
    both_ref[nodes:] = rows_ref[...]
    for c, copy in enumerate(copies):
        copy.wait()
        out_ref[:, c * step : (c + 1) * step] = dot32(rows_ref[...], w_ref[c]).astype(BF16)


def project_queries(latent, rows, weight):
    features = weight.shape[0]
    step = min(256, features)
    return pl.pallas_call(
        query_kernel,
        out_shape=(
            jax.ShapeDtypeStruct(rows.shape, BF16),
            jax.ShapeDtypeStruct((latent.shape[0] + rows.shape[0], features), BF16),
        ),
        in_specs=[VMEM, VMEM, ANY],
        out_specs=(VMEM, VMEM),
        scratch_shapes=[
            pltpu.VMEM((features // step, features, step), BF16),
            pltpu.SemaphoreType.DMA((features // step,)),
        ],
        cost_estimate=pl.CostEstimate(
            flops=2 * rows.size * features, bytes_accessed=2 * weight.size, transcendentals=0
        ),
        name="proj",
    )(latent, rows, weight)


def forward_kernel(shards, members, *refs):
    shard_ref, index_ref, grid_ref, query_ref, readout_ref = refs[:5]
    latent_refs = refs[5 : 5 + shards]
    weights_hbm = refs[5 + shards : 8 + shards]
    (
        key_ref,
        value_ref,
        soft_ref,
        attended_ref,
        normed_ref,
        inverse_ref,
        packed_ref,
        *w_refs,
        sem,
    ) = refs[8 + shards :]
    copies = [pltpu.make_async_copy(s, d, sem.at[i]) for i, (s, d) in enumerate(zip(weights_hbm, w_refs))]
    for copy in copies:
        copy.start()
    points, features = grid_ref.shape
    latents = jnp.concatenate([ref[...] for ref in latent_refs], axis=0)
    each = latent_refs[0].shape[0]
    index = index_ref[...]
    position = ((index // each) ^ shard_ref[0]) * each + index % each
    node = lax.broadcasted_iota(jnp.int32, (latents.shape[0], points), 0)
    chosen = jnp.where(node == position, 1.0, 0.0).astype(BF16)
    nodes = dot32(chosen, latents, (0, 0)).astype(BF16)
    copies[0].wait()
    key_ref[...] = dot32(nodes, w_refs[0][...]).astype(BF16)
    copies[1].wait()
    value_ref[...] = dot32(nodes, w_refs[1][...]).astype(BF16)
    factor = (features // HEADS) ** (-0.5)
    for pair in range(features // LANES):
        at = slice(pair * LANES, (pair + 1) * LANES)
        scores = dot32(query_ref[:, at], halves(key_ref[:, at]), (1, 1)) * factor
        soft = []
        for head in range(2):
            block = scores[:, head * LANES : (head + 1) * LANES]
            raised = jnp.exp(block - jnp.max(block, axis=-1, keepdims=True))
            soft.append(raised / jnp.sum(raised, axis=-1, keepdims=True))
        soft = jnp.concatenate(soft, axis=1)
        soft_ref[pair] = soft
        attended_ref[:, at] = dot32(soft.astype(BF16), halves(value_ref[:, at])).astype(BF16)
    copies[2].wait()
    hidden = grid_ref[...].astype(F32) + dot32(attended_ref[...], w_refs[2][...])
    inverse = lax.rsqrt(jnp.mean(hidden * hidden, axis=-1, keepdims=True) + EPS)
    normed = hidden * inverse
    normed_ref[...] = normed
    inverse_ref[...] = inverse
    normed_b = normed.astype(BF16)
    forecast = dot32(readout_ref[...], normed_b, (1, 1))
    high = forecast.astype(BF16)
    low = (forecast - high.astype(F32)).astype(BF16)
    channels = packed_ref.shape[1] // 2
    spare = jnp.zeros((channels - readout_ref.shape[0], points), BF16)
    fields = jnp.concatenate([high, spare, low, spare], axis=0)
    for m in range(members):
        packed_ref[m] = fields


def padded(channels):
    return channels + -channels % 8


def forward(shard, index, grid_rows, queries, readout, latents, weights, members):
    points, features = grid_rows.shape
    channels = padded(readout.shape[0])
    shape = jax.ShapeDtypeStruct
    return pl.pallas_call(
        functools.partial(forward_kernel, len(latents), members),
        out_shape=(
            shape((points, features), BF16),
            shape((points, features), BF16),
            shape((features // LANES, points, 2 * LANES), F32),
            shape((points, features), BF16),
            shape((points, features), F32),
            shape((points, 1), F32),
            shape((members, 2 * channels, points), BF16),
        ),
        in_specs=[SMEM] + [VMEM] * (4 + len(latents)) + [ANY] * 3,
        out_specs=(VMEM,) * 7,
        scratch_shapes=[pltpu.VMEM((features, features), BF16)] * 3
        + [pltpu.SemaphoreType.DMA((3,))],
        cost_estimate=pl.CostEstimate(
            flops=8 * points * features * features,
            bytes_accessed=6 * features * features,
            transcendentals=points * LANES * HEADS,
        ),
        name="fwd",
    )(shard, index, grid_rows, queries, readout, *latents, *weights)


def backward_kernel(
    shards,
    blocks,
    nodes,
    place_ref,
    packed_ref,
    target_ref,
    index_ref,
    query_hbm,
    key_hbm,
    value_hbm,
    soft_hbm,
    normed_hbm,
    inverse_ref,
    readout_ref,
    w_hbm,
    out_ref,
    *refs,
):
    outer_refs, refs = refs[:shards], refs[shards:]
    slope_ref, d_attended_ref, small_ref, truth_ref, weight_ref, *full_refs, sem = refs
    sources = (normed_hbm, w_hbm, value_hbm, soft_hbm, key_hbm, query_hbm)
    copies = [
        pltpu.make_async_copy(part, full, sem.at[i])
        for i, (part, full) in enumerate(zip(sources, full_refs))
    ]
    for copy in copies:
        copy.start()
    normed_ref, w_ref, value_ref, soft_ref, key_ref, query_ref = full_refs
    members = packed_ref.shape[0]
    points, features = normed_ref.shape
    channels_used = readout_ref.shape[0]
    channels = truth_ref.shape[0]
    for full, used in ((truth_ref, target_ref), (weight_ref, readout_ref)):
        full[:channels_used] = used[...]
        spare = (channels - channels_used, used.shape[1])
        full[channels_used:] = jnp.zeros(spare, used.dtype)
    width = features // blocks
    weight = (channels_used * points * shards) ** (-0.5)
    pair_weight = 1.0 / (members * (members - 1))
    chunk = 8

    def crps(c, loss):
        at = pl.ds(pl.multiple_of(c * chunk, chunk), chunk)
        low_at = pl.ds(pl.multiple_of(c * chunk + channels, chunk), chunk)
        fields = [
            packed_ref[m, at].astype(F32) + packed_ref[m, low_at].astype(F32)
            for m in range(members)
        ]
        truth = truth_ref[at]
        skill = jnp.zeros_like(truth)
        slopes = []
        for m in range(members):
            apart = fields[m] - truth
            square = apart * apart + SMOOTH
            root = lax.rsqrt(square)
            skill = skill + square * root
            slopes.append(apart * root * (weight / members))
        spread = jnp.zeros_like(truth)
        for m in range(members):
            for k in range(m):
                apart = fields[m] - fields[k]
                square = apart * apart + SMOOTH
                root = lax.rsqrt(square)
                spread = spread + square * root
                ratio = apart * root * (weight * pair_weight)
                slopes[m] = slopes[m] - ratio
                slopes[k] = slopes[k] + ratio
        for m in range(members):
            slope_ref[m, at] = slopes[m].astype(BF16)
        channel = c * chunk + lax.broadcasted_iota(jnp.int32, truth.shape, 0)
        term = skill * (1.0 / members) - spread * pair_weight
        return loss + jnp.where(channel < channels_used, term, 0.0)

    loss = lax.fori_loop(
        0, channels // chunk, crps, jnp.zeros((chunk, points), F32), unroll=members <= 8
    )
    loss = weight * jnp.sum(jnp.sum(loss, axis=0, keepdims=True), axis=1, keepdims=True)

    first = loss.astype(BF16).astype(F32)
    second = (loss - first).astype(BF16).astype(F32)
    for i, value in enumerate((first, second, loss - first - second)):
        small_ref[i : i + 1] = jnp.broadcast_to(value, (1, width))
    small_ref[3:] = jnp.zeros((small_ref.shape[0] - 3, width), F32)
    index = index_ref[...]
    line = 3
    for tag in (index // nodes, index % nodes):
        step = min(points, width)
        for c in range(0, points, step):
            small_ref[line : line + 1, :step] = tag[:, c : c + step].astype(F32)
            line = line + 1
    small = small_ref[...].astype(BF16)
    for b in range(blocks):
        out_ref[b, 4 * points :] = small

    def put(kind, column, value):
        step = min(width, value.shape[1])
        for c in range(0, value.shape[1], step):
            block, lane = divmod(column + c, width)
            out_ref[block, kind * points : (kind + 1) * points, lane : lane + step] = value[
                :, c : c + step
            ]

    own = slope_ref[place_ref[1]]
    copies[0].wait()
    normed = normed_ref[...]
    outer = dot32(own, normed.astype(BF16))
    columns = features // shards
    parts = [outer[:, s * columns : (s + 1) * columns] for s in range(shards)]
    for k in range(shards):
        part = parts[0]
        for s in range(1, shards):
            part = jnp.where((place_ref[0] ^ k) == s, parts[s], part)
        outer_refs[k][...] = part.astype(BF16)
    d_normed = dot32(own, weight_ref[...], (0, 0))
    mean = jnp.mean(d_normed * normed, axis=-1, keepdims=True)
    d_hidden = (inverse_ref[...] * (d_normed - normed * mean)).astype(BF16)
    put(3, 0, d_hidden)
    copies[1].wait()
    d_attended_ref[...] = dot32(d_hidden, w_ref[...], (1, 1)).astype(BF16)
    factor = (features // HEADS) ** (-0.5)
    for copy in copies[2:]:
        copy.wait()
    for pair in range(features // LANES):
        at = slice(pair * LANES, (pair + 1) * LANES)
        soft = soft_ref[pair]
        d_out = d_attended_ref[:, at]
        d_probs = dot32(d_out, halves(value_ref[:, at]), (1, 1))
        put(2, pair * LANES, joined(dot32(soft.astype(BF16), d_out, (0, 0))).astype(BF16))
        product = d_probs * soft
        d_scores = []
        for head in range(2):
            block = slice(head * LANES, (head + 1) * LANES)
            summed = jnp.sum(product[:, block], axis=-1, keepdims=True)
            d_scores.append(soft[:, block] * (d_probs[:, block] - summed) * factor)
        d_scores = jnp.concatenate(d_scores, axis=1).astype(BF16)
        put(0, pair * LANES, dot32(d_scores, halves(key_ref[:, at])).astype(BF16))
        put(1, pair * LANES, joined(dot32(d_scores, query_ref[:, at], (0, 0))).astype(BF16))


def backward(place, packed, target, index, saved, readout, w_mix, shards, blocks, nodes):
    members = packed.shape[0]
    features = w_mix.shape[0]
    points = saved[0].shape[0]
    channels = padded(readout.shape[0])
    width = features // blocks
    small = MISC
    return pl.pallas_call(
        functools.partial(backward_kernel, shards, blocks, nodes),
        out_shape=(
            jax.ShapeDtypeStruct((blocks, 4 * points + small, width), BF16),
        )
        + (jax.ShapeDtypeStruct((channels, features // shards), BF16),) * shards,
        in_specs=[SMEM] + [VMEM] * 3 + [HBM] * 5 + [VMEM] * 2 + [HBM],
        out_specs=(VMEM,) * (1 + shards),
        scratch_shapes=[
            pltpu.VMEM((members, channels, points), BF16),
            pltpu.VMEM((points, features), BF16),
            pltpu.VMEM((small, width), F32),
            pltpu.VMEM((channels, points), F32),
            pltpu.VMEM((channels, features), BF16),
            pltpu.VMEM((points, features), F32),
            pltpu.VMEM((features, features), BF16),
            pltpu.VMEM((points, features), BF16),
            pltpu.VMEM((features // LANES, points, 2 * LANES), F32),
            pltpu.VMEM((points, features), BF16),
            pltpu.VMEM((points, features), BF16),
            pltpu.SemaphoreType.DMA((6,)),
        ],
        cost_estimate=pl.CostEstimate(
            flops=4 * points * features * features,
            bytes_accessed=4 * features * features,
            transcendentals=0,
        ),
        name="bwd",
    )(place, packed, target, index, *saved, readout, w_mix)


def gradient_kernel(shards, pair, members, nodes, place_ref, blocks_hbm, *refs):
    latent_refs, early_refs, late_refs, other_refs, grid_refs = (
        refs[i * shards : (i + 1) * shards] for i in range(5)
    )
    out_ref, loss_ref, blocks_ref, late_ref, node_ref, grid_ref, sems = refs[5 * shards :]
    sources = [late_refs, latent_refs, grid_refs]
    if pair > 1:
        sources = [
            late_refs + other_refs,
            latent_refs + tuple(ref.at[:nodes] for ref in early_refs),
            grid_refs + tuple(ref.at[nodes:] for ref in early_refs),
        ]
    first = pltpu.make_async_copy(blocks_hbm, blocks_ref, sems.at[0, 0])
    first.start()
    copies = []
    for i, (parts, full) in enumerate(zip(sources, (late_ref, node_ref, grid_ref))):
        step = full.shape[0] // len(parts)
        copies.append(
            [
                pltpu.make_async_copy(part, full.at[pl.ds(k * step, step)], sems.at[i + 1, k])
                for k, part in enumerate(parts)
            ]
        )
        for copy in copies[-1]:
            copy.start()
    first.wait()
    width = blocks_ref.shape[2]
    features = late_ref.shape[1]
    points = grid_ref.shape[0] // (shards * pair)
    depth = features // members
    shard, half = place_ref[0], place_ref[1]
    start = 4 * points
    total = blocks_ref[0, start:].astype(F32)
    for s in range(1, shards):
        total = total + blocks_ref[s * pair, start:].astype(F32)
    loss_ref[...] = jnp.sum(total[:3, :1], axis=0, keepdims=True)

    def slots(kind, t):
        at = slice(kind * points, (kind + 1) * points)
        return [blocks_ref[(shard ^ k) * pair + (half ^ t), at] for k in range(shards)]

    def put(kind, total):
        total = total.astype(BF16)
        at = slice(kind * width, kind * width + total.shape[0])
        for m in range(members):
            out_ref[m, at] = total[:, m * depth : (m + 1) * depth]

    def product(kind, full, group):
        left = jnp.concatenate([v for t in range(pair) for v in slots(kind, t)], axis=0)
        for copy in copies[group]:
            copy.wait()
        put(kind, dot32(left, full[...], (0, 0)))

    product(3, late_ref, 0)
    chosen = []
    for k in range(shards):
        index = blocks_ref[(shard ^ k) * pair, start : start + MISC].astype(jnp.int32)
        lines = max(points // width, 1)
        owner, offset = (
            jnp.concatenate([index[3 + b + i : 4 + b + i] for i in range(lines)], axis=1)
            for b in (0, lines)
        )
        position = (owner ^ shard) * nodes + offset
        node = lax.broadcasted_iota(jnp.int32, (nodes * shards, points), 0)
        chosen.append(jnp.where(node == position, 1.0, 0.0).astype(BF16))
    chosen = jnp.concatenate(chosen, axis=1)
    sums = []
    for t in range(pair):
        both = [jnp.concatenate(slots(kind, t), axis=0) for kind in (1, 2)]
        sums.append(dot32(chosen, jnp.concatenate(both, axis=1)).astype(BF16))
    for copy in copies[1]:
        copy.wait()
    put(1, dot32(jnp.concatenate(sums, axis=0), node_ref[...], (0, 0)))
    product(0, grid_ref, 2)


def gradients(place, blocks, latents, early, late, other, grids, members, pair):
    count, _, width = blocks.shape
    shards = count // pair
    features = late[0].shape[1]
    points = late[0].shape[0]
    depth = features // members
    return pl.pallas_call(
        functools.partial(
            gradient_kernel, shards, pair, members, latents[0].shape[0]
        ),
        out_shape=(
            jax.ShapeDtypeStruct((members, 4 * width, depth), BF16),
            jax.ShapeDtypeStruct((1, 1), F32),
        ),
        in_specs=[SMEM, ANY] + [HBM] * (5 * shards),
        out_specs=(VMEM, VMEM),
        scratch_shapes=[pltpu.VMEM(blocks.shape, BF16)]
        + [
            pltpu.VMEM((count * rows, features), BF16)
            for rows in (points, latents[0].shape[0], points)
        ]
        + [pltpu.SemaphoreType.DMA((4, count))],
        cost_estimate=pl.CostEstimate(
            flops=8 * points * count * features * width,
            bytes_accessed=8 * points * count * features,
            transcendentals=0,
        ),
        compiler_params=pltpu.CompilerParams(vmem_limit_bytes=51 << 20),
        name="wgrad",
    )(place, blocks, *latents, *early, *late, *other, *grids)


def sum_kernel(pair, blocks_hbm, *refs):
    *refs, blocks_ref, sem = refs
    members, rows, _ = blocks_ref.shape
    width = rows // len(refs)
    copies = [
        pltpu.make_async_copy(blocks_hbm.at[:, pl.ds(i * width, width)], blocks_ref.at[:, pl.ds(i * width, width)], sem.at[i])
        for i in range(len(refs))
    ]
    for copy in copies:
        copy.start()
    for i, ref in enumerate(refs):
        copies[i].wait()
        at = slice(i * width, (i + 1) * width)
        for y in range(pair):
            total = blocks_ref[y, at].astype(F32)
            for m in range(y + pair, members, pair):
                total = total + blocks_ref[m, at].astype(F32)
            ref[:, y * width : (y + 1) * width] = total.T


def sum_groups(blocks, pair):
    _, rows, depth = blocks.shape
    return pl.pallas_call(
        functools.partial(sum_kernel, pair),
        out_shape=(jax.ShapeDtypeStruct((depth, pair * rows // 4), F32),) * 4,
        in_specs=[ANY],
        out_specs=(VMEM,) * 4,
        scratch_shapes=[pltpu.VMEM(blocks.shape, BF16), pltpu.SemaphoreType.DMA((4,))],
        compiler_params=pltpu.CompilerParams(vmem_limit_bytes=8 << 20),
        name="sums",
    )(blocks)


def join_kernel(shard_ref, *refs):
    *slot_refs, out_ref = refs
    used, columns = out_ref.shape[0], slot_refs[0].shape[1]
    values = [ref[...].astype(F32) for ref in slot_refs]
    for s in range(len(values)):
        value = values[0]
        for k in range(1, len(values)):
            value = jnp.where((shard_ref[0] ^ k) == s, values[k], value)
        out_ref[:, s * columns : (s + 1) * columns] = value[:used]


def join_columns(shard, parts, channels_used):
    columns = parts[0].shape[1] * len(parts)
    return pl.pallas_call(
        join_kernel,
        out_shape=jax.ShapeDtypeStruct((channels_used, columns), F32),
        in_specs=[SMEM] + [VMEM] * len(parts),
        out_specs=VMEM,
        compiler_params=pltpu.CompilerParams(vmem_limit_bytes=6 << 20),
        name="join",
    )(shard, *parts)


def sum_outer(parts):
    total = parts[0].astype(F32)
    received = []
    for k in range(1, len(parts)):
        received.append(swap(parts[k], "space", k))
    for value in received:
        total = total + value.astype(F32)
    total = total.astype(BF16)
    size = lax.axis_size("ens")
    for bit in [1 << i for i in range(1, size.bit_length() - 1)] + [1]:
        other = swap(total, "ens", bit)
        total = (total.astype(F32) + other.astype(F32)).astype(BF16)
    return gather_slots(total, "space")


def body(
    grid_hidden, latent, tile_neighbor_index, target, w_query, w_key, w_value, w_mix, readout_weight
):
    nodes, _ = latent.shape[1:]
    channels_used = target.shape[0]
    shards, members = lax.axis_size("space"), lax.axis_size("ens")
    shard, member = lax.axis_index("space"), lax.axis_index("ens")
    pair = 2 if members % 2 == 0 and shards <= 8 else 1
    half = member % pair
    count = shards * pair
    groups = [
        [(g + y) * shards + s for s in range(shards) for y in range(pair)]
        for g in range(0, members, pair)
    ]

    own_latent, grid_rows = latent[0], grid_hidden[0]
    latents = gather_slots(own_latent, "space")
    grids = gather_slots(grid_rows, "space")
    queries, both = project_queries(own_latent, grid_rows, w_query)
    early = latents
    if pair > 1:
        early = swap(both, "ens", 1)
        early = gather_slots(early, "space")
    *saved, packed = forward(
        shard[None],
        tile_neighbor_index,
        grid_rows,
        queries,
        readout_weight,
        latents,
        (w_key, w_value, w_mix),
        members,
    )
    keyset, valueset, soft, attended, normed, inverse = saved
    packed = lax.all_to_all(packed, "ens", split_axis=0, concat_axis=0, tiled=True)
    late = gather_slots(attended, "space")
    other = late
    if pair > 1:
        other = []
        for k, part in enumerate(late):
            other.append(swap(other[k - 1], "space", 1) if k % 2 else swap(part, "ens", 1))
    saved = (queries, keyset, valueset, soft, normed, inverse)
    blocks, *outer = backward(
        jnp.stack([shard, member]),
        packed,
        target,
        tile_neighbor_index,
        saved,
        readout_weight,
        w_mix,
        shards,
        count,
        nodes,
    )
    blocks = lax.all_to_all(
        blocks,
        ("ens", "space"),
        split_axis=0,
        concat_axis=0,
        axis_index_groups=groups,
        tiled=True,
    )
    place = jnp.stack([shard, half])
    outer = sum_outer(outer)
    blocks, loss = gradients(
        place, blocks, latents, early, late, other, grids, members, pair
    )
    blocks = lax.all_to_all(blocks, "ens", split_axis=0, concat_axis=0, tiled=True)
    grad_out = join_columns(shard[None], outer, channels_used)
    grads = sum_groups(blocks, pair)
    return (loss.reshape(()), grad_out, *grads)


def solution(mesh):
    in_specs = (
        P("ens", "space", None),
        P("ens", "space", None),
        P("space", None),
        P(None, "space"),
        P(),
        P(),
        P(),
        P(),
        P(),
    )
    out_specs = (
        P(),
        P(),
        P("ens", "space"),
        P("ens", "space"),
        P("ens", "space"),
        P("ens", "space"),
    )

    return jax.shard_map(body, mesh=mesh, in_specs=in_specs, out_specs=out_specs, check_vma=False)
```
